32 devices in a mesh: ctx: 32 (over z, y, x, core).
Axes of the slice: x: 2, y: 2, z: 4, core: 2. Of those that a mesh axis runs over, the one named last changes fastest.
Arguments:
- block_input: bfloat16 [64, 4, 576, 800], P('ctx'), may hold values from -6 to 6
- cotangent: bfloat16 [64, 4, 576, 800], P('ctx'), may hold values from -6 to 6
- w_in: bfloat16 [320000], P('ctx'), may hold values from -0.21875 to 0.21875
- w_conv: bfloat16 [480000], P('ctx'), may hold values from -0.1875 to 0.1875
- w_out: bfloat16 [320000], P('ctx'), may hold values from -0.4375 to 0.4375
- wide_gain: float32 [800], replicated, may hold values from 0.25 to 1.75
- wide_bias: float32 [2, 800], replicated, may hold values from -2 to 2
- narrow_gain: float32 [2, 400], replicated, may hold values from 0.25 to 1.75
- narrow_bias: float32 [4, 400], replicated, may hold values from -2 to 2
- dealing: int32 [64], replicated, may hold values from 0 to 31, as said below
Outputs:
- block_output: bfloat16 [64, 4, 576, 800], P('ctx')
- input_grad: bfloat16 [64, 4, 576, 800], P('ctx')
- grad_w_in: float32 [320000], P('ctx')
- grad_w_conv: float32 [480000], P('ctx')
- grad_w_out: float32 [320000], P('ctx')
- grad_wide_gain: float32 [800], replicated
- grad_wide_bias: float32 [2, 800], replicated
- grad_narrow_gain: float32 [2, 400], replicated
- grad_narrow_bias: float32 [4, 400], replicated
The draws below stay inside these ranges and needn't reach their ends.
Inputs may be any that keep to these rules, and one draw needn't show every extreme that they name: `dealing`: block b and block 63 - b sit on one device, the lower in its first slot. Block b + 1 lies on the device after that of block b along ctx, cyclically, for b < 31.
All inputs are finite; a program needn't handle non-finite values.
Results may differ from the reference program's by a relative error of at most 0.0065.
Values may be sent and summed in bfloat16 or wider, within the bound.
No kernel may reach another device: no remote copies, remote signals or barrier semaphores. Data moves between devices by JAX's collectives and lax.ppermute only.
A program may use at most 192 MiB of HBM per device.

```python
import jax
import jax.numpy as jnp
from jax import lax

D = 800
F = 400
SEQS = 4
BLOCK_CHARACTERS = 576
CONV_DILATION = 16
NBLK = 64


def draw_dealing(key, part):
    offset = jax.random.randint(key, (), 0, NBLK // 2)
    block_ids = jnp.arange(NBLK, dtype=jnp.int32)
    pair_index = jnp.minimum(block_ids, NBLK - 1 - block_ids)
    return ((pair_index - offset) % (NBLK // 2)).astype(jnp.int32)


def shard_levels(own_key, extent, split, smallest, top_value):
    loudness, own = 1.0, jax.random.fold_in(own_key, 6)
    for dim, parts in split:
        heights = jnp.exp(jax.random.uniform(jax.random.fold_in(own, dim), (parts,), jnp.float32, smallest / len(split), top_value / len(split)))
        loudness = loudness * jnp.repeat(heights, extent[dim] // parts).reshape([-1 if axis == dim else 1 for axis in range(len(extent))])
    return loudness


def gaussian(key, shape, scale, most, cuts=(), kind=jnp.bfloat16):
    entries = scale * jax.random.normal(key, shape, jnp.float32)
    if cuts:
        entries = entries * shard_levels(key, shape, cuts, -0.22, 0.18)
    return jnp.clip(entries, -most, most).astype(kind)


def setup_inputs(seed: int = 0) -> dict:
    keys = jax.random.split(jax.random.key(seed), 11)
    return {
        "block_input": gaussian(keys[0], (NBLK, SEQS, BLOCK_CHARACTERS, D), 1.0, 6.0, ((0, 32),)),
        "cotangent": gaussian(keys[1], (NBLK, SEQS, BLOCK_CHARACTERS, D), 1.0, 6.0, ((0, 32),)),
        "w_in": gaussian(keys[2], (D * F,), D ** -0.5, 0.21875, ((0, 32),)),
        "w_conv": gaussian(keys[3], (3 * F * F,), (3 * F) ** -0.5, 0.1875, ((0, 32),)),
        "w_out": gaussian(keys[4], (F * D,), (F // 2) ** -0.5, 0.4375, ((0, 32),)),
        "wide_gain": jnp.clip(1.0 + 0.15 * jax.random.normal(keys[5], (D,), jnp.float32), 0.25, 1.75),
        "wide_bias": gaussian(keys[6], (2, D), 0.3, 2.0, (), jnp.float32),
        "narrow_gain": jnp.clip(1.0 + 0.15 * jax.random.normal(keys[7], (2, F), jnp.float32), 0.25, 1.75),
        "narrow_bias": gaussian(keys[8], (4, F), 0.3, 2.0, (), jnp.float32),
        "dealing": draw_dealing(jax.random.fold_in(keys[10], 71), 0),
    }


epsilon = 1e-05
highest = lax.Precision.HIGHEST

@jax.custom_vjp
def low(v):
    return lax.optimization_barrier(v.astype(jnp.bfloat16)).astype(jnp.float32)

@jax.custom_vjp
def low_back(v):
    return v

def low_keep(v):
    return (low(v), None)

def low_pass(kept, grad):
    return (grad,)

def back_keep(v):
    return (v, None)

def back_low(kept, grad):
    return (low(grad),)
low.defvjp(low_keep, low_pass)
low_back.defvjp(back_keep, back_low)

def norm_silu(values, gain, shift):
    centre = lax.optimization_barrier(jnp.mean(values, axis=-1, keepdims=True))
    centred = values - centre
    spread = lax.optimization_barrier(jnp.mean(centred * centred, axis=-1, keepdims=True))
    return jax.nn.silu(centred * lax.rsqrt(spread + epsilon) * gain + shift)

def front_half(block_x, matrix_in, wide_gain, wide_bias, narrow_gain, narrow_bias):
    first_act = low(norm_silu(block_x, wide_gain, wide_bias[0]))
    in_hidden = low_back(jnp.dot(first_act, matrix_in, precision=highest) + narrow_bias[0])
    return low(norm_silu(in_hidden, narrow_gain[0], narrow_bias[1]))

def back_half(preceding_rows, convolution_input, block_x, kernel, matrix_out, wide_bias, narrow_gain, narrow_bias):
    extended = jnp.concatenate([preceding_rows, convolution_input], axis=1)
    block_rows = convolution_input.shape[1]
    conv_hidden = narrow_bias[2]
    for kernel_tap_index in range(3):
        start_position = 2 * CONV_DILATION - kernel_tap_index * CONV_DILATION
        conv_hidden = conv_hidden + jnp.dot(extended[:, start_position:start_position + block_rows], kernel[kernel_tap_index], precision=highest)
    conv_hidden = low_back(conv_hidden)
    out_act = low(norm_silu(conv_hidden, narrow_gain[1], narrow_bias[3]))
    return block_x + jnp.dot(out_act, matrix_out, precision=highest) + wide_bias[1]

def forward(blocks_x, w_in, w_conv, w_out, wide_gain, wide_bias, narrow_gain, narrow_bias):
    matrix_in = w_in.reshape(D, F)
    kernel = w_conv.reshape(3, F, F)
    matrix_out = w_out.reshape(F, D)
    front_block = jax.checkpoint(lambda block_x: front_half(block_x, matrix_in, wide_gain, wide_bias, narrow_gain, narrow_bias))
    convolution_input = lax.map(front_block, blocks_x)
    preceding_rows = jnp.concatenate([jnp.zeros_like(convolution_input[:1, :, :2 * CONV_DILATION]), convolution_input[:-1, :, BLOCK_CHARACTERS - 2 * CONV_DILATION:]], axis=0)
    back_block = jax.checkpoint(lambda packed: back_half(packed[0], packed[1], packed[2], kernel, matrix_out, wide_bias, narrow_gain, narrow_bias))
    return lax.map(back_block, (preceding_rows, convolution_input, blocks_x))

def reference(block_input, cotangent, w_in, w_conv, w_out, wide_gain, wide_bias, narrow_gain, narrow_bias, dealing):
    block_ids = jnp.arange(NBLK, dtype=jnp.int32)
    slot_index = (2 * dealing + (block_ids >= NBLK // 2).astype(jnp.int32)).astype(jnp.int32)
    blocks_x = block_input[slot_index].astype(jnp.float32)
    blocks_c = cotangent[slot_index].astype(jnp.float32)
    result, pull_back = jax.vjp(forward, blocks_x, w_in.astype(jnp.float32), w_conv.astype(jnp.float32), w_out.astype(jnp.float32), wide_gain, wide_bias, narrow_gain, narrow_bias)
    grads = pull_back(blocks_c)
    block_output = jnp.zeros(block_input.shape, jnp.bfloat16).at[slot_index].set(result.astype(jnp.bfloat16))
    input_grad = jnp.zeros(block_input.shape, jnp.bfloat16).at[slot_index].set(grads[0].astype(jnp.bfloat16))
    return (block_output, input_grad, grads[1], grads[2], grads[3], grads[4], grads[5], grads[6], grads[7])
```

```python
import functools
import math
import jax
import jax.numpy as jnp
from jax import lax
from jax.experimental import pallas as pl
from jax.experimental.pallas import tpu as pltpu
from jax.sharding import PartitionSpec as P

EPS = 1e-05
BF = jnp.bfloat16
F32 = jnp.float32
L = 128
R = 16
SHIFT = 16
UN = 25
WIDE = 256


def params(mb=52):
    return pltpu.CompilerParams(dimension_semantics=("arbitrary",), vmem_limit_bytes=mb * 1024 * 1024)


def cost(flops, nbytes, trans=0):
    return pl.CostEstimate(flops=int(flops), bytes_accessed=int(nbytes), transcendentals=int(trans))

def loop(n, body, init, unroll=None):
    return lax.fori_loop(0, n, body, init, unroll=unroll or UN)


def rows_at(i):
    return pl.ds(pl.multiple_of(i * R, R), R)


def fold(v):
    return v[:8] + v[8:]


def nt(a, b):
    return lax.dot_general(a, b, (((1,), (1,)), ((), ())), preferred_element_type=F32)


def nn(a, b):
    return jnp.dot(a, b, preferred_element_type=F32)


def col_stats(read, chans, N):
    acc = loop(chans // R, lambda i, a: a + fold(read(i)), jnp.zeros((8, N), F32))
    mean = jnp.sum(acc, axis=0, keepdims=True) * (1.0 / chans)

    def second(i, a):
        cen = read(i) - mean
        return a + fold(cen * cen)

    acc = loop(chans // R, second, jnp.zeros((8, N), F32))
    var = jnp.sum(acc, axis=0, keepdims=True) * (1.0 / chans)
    return mean, lax.rsqrt(var + EPS)


def gate(s):
    q = 0.5 * jnp.tanh(0.5 * s) + 0.5
    r = s * q
    return r, q + r * (1.0 - q)


def lane_sum(acc_ref, rows, v):
    N = v.shape[1]
    full = N // L * L
    tot = v[:, :L]
    for j in range(L, full, L):
        tot = tot + v[:, j:j + L]
    if full < N:
        tail = jnp.concatenate([v[:, full:], jnp.zeros((v.shape[0], L - (N - full)), v.dtype)], axis=1)
        tot = tot + tail
    acc_ref[rows, :] += tot


def unit_plan(n, M, C):
    size = M * C // n
    whole = math.gcd(size, C)
    q = max(d for d in range(1, WIDE + 1) if whole % d == 0)
    return q, C // q, size // q


def unit_slices(n, M, C):
    q, parts, units = unit_plan(n, M, C)
    out = []
    for p in range(n):
        for h in range(parts):
            lo = -((h - units * p) // parts)
            hi = -((h - units * (p + 1)) // parts)
            if hi > lo:
                out.append((p, h, lo, hi - lo, lo * parts + h - units * p))
    return out


def strided(start, size, step):
    return pl.ds(start, size, stride=step) if step > 1 else pl.ds(start, size)


def planes(q):
    return [(j, j * L, min(q - j * L, L)) for j in range(-(-q // L))]


def put_matrix(n, mat_ref, f32_ref, off):
    M, C = mat_ref.shape
    q, parts, _ = unit_plan(n, M, C)
    for p, h, lo, cnt, u in unit_slices(n, M, C):
        for j, at, w in planes(q):
            mat_ref[lo:lo + cnt, h * q + at:h * q + at + w] = f32_ref[p, j, strided(off + u, cnt, parts), :][:, :w]


def put_pieces(n, out_ref, mat_ref, M, C, off):
    q, parts, _ = unit_plan(n, M, C)
    for p, h, lo, cnt, u in unit_slices(n, M, C):
        for j, at, w in planes(q):
            v = mat_ref[lo:lo + cnt, h * q + at:h * q + at + w]
            if w < L:
                v = jnp.concatenate([v, jnp.zeros((cnt, L - w), v.dtype)], axis=1)
            out_ref[p, j, strided(off + u, cnt, parts), :] = v


def flipped(mat):
    C = mat.shape[1]
    eye = (lax.broadcasted_iota(jnp.int32, (C, C), 0) == lax.broadcasted_iota(jnp.int32, (C, C), 1)).astype(BF)
    return nt(eye, mat).astype(BF)


def ordered(n, slots_ref, g_ref, f32_ref):
    for p in range(n):
        f32_ref[p] = g_ref[slots_ref[p]].astype(F32)


def unpack_in_kernel(n, slots_ref, g_ref, bias_ref, w1_ref, w1t_ref, f32_ref, mat_ref):
    ordered(n, slots_ref, g_ref, f32_ref)
    put_matrix(n, mat_ref, f32_ref, 0)
    D, F = mat_ref.shape
    w1_ref[...] = mat_ref[...].astype(BF)
    w1t_ref[:, :D] = flipped(w1_ref[...])
    w1t_ref[:, D:] = bias_ref[...]


def smem():
    return pl.BlockSpec(memory_space=pltpu.SMEM)


def vmem():
    return pl.BlockSpec(memory_space=pltpu.VMEM)


def unpack_in(n, slots, g, bias, D, F):
    sd = jax.ShapeDtypeStruct
    return pl.pallas_call(
        functools.partial(unpack_in_kernel, n),
        in_specs=[smem(), vmem(), vmem()], out_specs=[vmem(), vmem()],
        out_shape=[sd((D, F), BF), sd((F, D + R), BF)],
        scratch_shapes=[pltpu.VMEM(g.shape, F32), pltpu.VMEM((D, F), F32)],
        compiler_params=pltpu.CompilerParams(vmem_limit_bytes=40 * 1024 * 1024), name="unpack_in",
    )(slots, g, bias)


def unpack_rest_kernel(n, slots_ref, g_ref, bias_ref, wide_ref, wc_ref, wct_ref, w3_ref, w3t_ref, f32_ref, matc_ref, mat3_ref):
    F, D = mat3_ref.shape
    ordered(n, slots_ref, g_ref, f32_ref)
    put_matrix(n, matc_ref, f32_ref, 0)
    put_matrix(n, mat3_ref, f32_ref, unit_plan(n, 3 * F, F)[2])
    for k in range(3):
        wc_ref[k] = matc_ref[k * F:(k + 1) * F, :].astype(BF)
        wct_ref[k, :, :F] = flipped(wc_ref[k])
        wct_ref[k, :, F:] = bias_ref[...] if k == 0 else jnp.zeros((F, R), BF)
    w3_ref[...] = mat3_ref[...].astype(BF)
    w3t_ref[:, :F] = flipped(w3_ref[...])
    w3t_ref[:, F:] = wide_ref[...]


def unpack_rest(n, slots, g, bias, wide_bias, D, F):
    sd = jax.ShapeDtypeStruct
    return pl.pallas_call(
        functools.partial(unpack_rest_kernel, n),
        in_specs=[smem()] + [vmem()] * 3, out_specs=[vmem()] * 4,
        out_shape=[sd((3, F, F), BF), sd((3, F, F + R), BF), sd((F, D), BF), sd((D, F + R), BF)],
        scratch_shapes=[pltpu.VMEM(g.shape, F32), pltpu.VMEM((3 * F, F), F32), pltpu.VMEM((F, D), F32)],
        compiler_params=pltpu.CompilerParams(vmem_limit_bytes=40 * 1024 * 1024), name="unpack_rest",
    )(slots, g, bias, wide_bias)


def lane_total(acc):
    return jnp.sum(acc.T, axis=0, keepdims=True)


def rim_store(ref, i, seqs, cols):
    w = cols.shape[1]
    for s in range(2 * seqs):
        @pl.when(i == s)
        def _(s=s):
            ref[s // seqs, :, (s % seqs) * w:(s % seqs + 1) * w] = cols


def rim_load(buf, i, seqs, w, first, second):
    for s in range(2 * seqs):
        @pl.when(i == s)
        def _(s=s):
            src = first() if s < seqs else second()
            buf[...] = src[:, (s % seqs) * w:(s % seqs + 1) * w]


def wide_fwd_kernel(x_ref, vec_ref, r1_ref, n0_ref, s0_ref, rstd_ref):
    D, N = x_ref.shape[1:]
    read = lambda i: x_ref[0, rows_at(i), :].astype(F32)
    mean, rstd = col_stats(read, D, N)
    rstd_ref[0] = rstd

    def act(i, _):
        rows = rows_at(i)
        n = (read(i) - mean) * rstd
        r, d = gate(n * vec_ref[rows, 0:1] + vec_ref[rows, 1:2])
        r1_ref[0, rows, :] = r.astype(BF)
        n0_ref[0, rows, :] = n.astype(BF)
        s0_ref[0, rows, :] = d.astype(BF)
        return 0

    loop(D // R, act, 0)
    r1_ref[0, D:, :] = jnp.ones((r1_ref.shape[1] - D, N), BF)


def seq_spec(rows, N, G=None):
    return pl.BlockSpec((1, rows, N), (lambda i: (i, 0, 0)) if G is None else (lambda i: (G - 1 - i, 0, 0)))


def fixed(shape):
    zero = (0,) * len(shape)
    return pl.BlockSpec(shape, lambda i: zero)


def wide_fwd(xT, vec):
    S, D, N = xT.shape
    sd = jax.ShapeDtypeStruct
    return pl.pallas_call(
        wide_fwd_kernel, grid=(S,),
        in_specs=[seq_spec(D, N), fixed(vec.shape)],
        out_specs=[seq_spec(D + R, N), seq_spec(D, N), seq_spec(D, N), seq_spec(1, N)],
        out_shape=[sd((S, D + R, N), BF), sd((S, D, N), BF), sd((S, D, N), BF), sd((S, 1, N), F32)],
        compiler_params=params(), name="wide_fwd",
    )(xT, vec)


def front_kernel(seqs, r1_ref, w1t_ref, vec_ref, u_ref, n_ref, s_ref, rstd_ref, tail_ref, h_ref):
    F, N = h_ref.shape
    h_ref[...] = nn(w1t_ref[...], r1_ref[0])
    read = lambda i: h_ref[rows_at(i), :]
    mean, rstd = col_stats(read, F, N)
    rstd_ref[0] = rstd

    def act(i, _):
        rows = rows_at(i)
        n = (read(i) - mean) * rstd
        r, d = gate(n * vec_ref[rows, 0:1] + vec_ref[rows, 1:2])
        u_ref[0, rows, :] = r.astype(BF)
        n_ref[0, rows, :] = n.astype(BF)
        s_ref[0, rows, :] = d.astype(BF)
        return 0

    loop(F // R, act, 0)
    rim_store(tail_ref, pl.program_id(0), seqs, u_ref[0, :, N - 2 * SHIFT:])


def front(r1, w1t, vec):
    S, DE, N = r1.shape
    F = w1t.shape[0]
    sd = jax.ShapeDtypeStruct
    return pl.pallas_call(
        functools.partial(front_kernel, S // 2), grid=(S,),
        in_specs=[seq_spec(DE, N), fixed(w1t.shape), fixed(vec.shape)],
        out_specs=[seq_spec(F, N)] * 3 + [seq_spec(1, N), fixed((2, F, S * SHIFT))],
        out_shape=[sd((S, F, N), BF)] * 3 + [sd((S, 1, N), F32), sd((2, F, S * SHIFT), BF)],
        scratch_shapes=[pltpu.VMEM((F, N), F32)],
        compiler_params=params(), name="front",
    )(r1, w1t, vec)


def pull_second(F, N, ds_ref, n_ref, vec_ref, m1, m2, rstd, e_ref, off=0):
    m1, m2 = m1 * (1.0 / F), m2 * (1.0 / F)

    def body(i, _):
        rows = rows_at(i)
        t = ds_ref[rows, :] * vec_ref[rows, 0:1]
        e = ((t - m1) - n_ref[rows, :].astype(F32) * m2) * rstd
        e_ref[rows, off:off + N] = e.astype(BF)
        return 0

    loop(F // R, body, 0)


def reduce8(a):
    return jnp.sum(a, axis=0, keepdims=True)


def middle_kernel(n, seqs, flags_ref, u_ref, below_ref, above_ref, tail_ref, c_ref, x_ref, wct_ref, w3_ref, w3t_ref, vec_ref,
                  e_ref, out_ref, pieces_ref, small_ref, head_ref,
                  ubuf, rbuf, h_ref, d_ref, n_ref, o_ref, gacc, bacc, gwo_ref, gwc_ref, hbuf, gwc_mat):
    F, N = h_ref.shape
    D = c_ref.shape[1]
    i = pl.program_id(0)

    @pl.when(i == 0)
    def _():
        ubuf[:, F:, :] = jnp.ones((3, ubuf.shape[1] - F, N), BF)
        rbuf[F:, :] = jnp.ones((rbuf.shape[0] - F, N), BF)
        gwo_ref[...] = jnp.zeros_like(gwo_ref)
        gwc_ref[...] = jnp.zeros_like(gwc_ref)
        gacc[...] = jnp.zeros_like(gacc)
        bacc[...] = jnp.zeros_like(bacc)

    rim_load(hbuf, i, seqs, 2 * SHIFT,
             lambda: jnp.where(flags_ref[0] == 1, jnp.zeros_like(below_ref[...]), below_ref[...]),
             lambda: jnp.where(flags_ref[1] == 1, tail_ref[0], above_ref[...]))
    u, halo = u_ref[0], hbuf[...]
    ubuf[0, :F, :] = u
    for k in (1, 2):
        w = k * SHIFT
        ubuf[k, :F, :] = jnp.concatenate([halo[:, 2 * SHIFT - w:], u[:, :N - w]], axis=1)
    h_ref[...] = nn(wct_ref[0], ubuf[0]) + nn(wct_ref[1], ubuf[1]) + nn(wct_ref[2], ubuf[2])
    d_ref[...] = nn(w3_ref[...], c_ref[0])
    read = lambda j: h_ref[rows_at(j), :]
    mean, rstd = col_stats(read, F, N)

    def act(j, carry):
        m1, m2 = carry
        rows = rows_at(j)
        n = (read(j) - mean) * rstd
        gain = vec_ref[rows, 0:1]
        r, d = gate(n * gain + vec_ref[rows, 1:2])
        rbuf[rows, :] = r.astype(BF)
        ds = d_ref[rows, :] * d
        dn = ds * n
        n_ref[rows, :] = n
        d_ref[rows, :] = ds
        lane_sum(bacc, rows, ds)
        lane_sum(gacc, rows, dn)
        return m1 + fold(ds * gain), m2 + fold(dn * gain)

    zero = jnp.zeros((8, N), F32)
    m1, m2 = loop(F // R, act, (zero, zero))
    pull_second(F, N, d_ref, n_ref, vec_ref, reduce8(m1), reduce8(m2), rstd, e_ref.at[0])
    o_ref[...] = nn(w3t_ref[...], rbuf[...])

    def emit(j, _):
        rows = rows_at(j)
        out_ref[0, rows, :] = (o_ref[rows, :] + x_ref[0, rows, :].astype(F32)).astype(BF)
        return 0

    loop(D // R, emit, 0)
    gwo_ref[...] += nt(rbuf[...], c_ref[0])
    for k in range(3):
        gwc_ref[k] += nt(ubuf[k], e_ref[0])
    rim_store(head_ref, i, seqs, e_ref[0, :, :2 * SHIFT])

    @pl.when(i == pl.num_programs(0) - 1)
    def _():
        small_ref[...] = jnp.zeros_like(small_ref)
        small_ref[0:1, :F] = lane_total(gacc[...])
        small_ref[0:1, F:] = lane_total(bacc[...])
        small_ref[1:2, :F] = gwc_ref[0, F:F + 1, :]
        small_ref[2:3, :] = gwo_ref[F:F + 1, :]
        for k in range(3):
            gwc_mat[k * F:(k + 1) * F, :] = gwc_ref[k, :F, :]
        put_pieces(n, pieces_ref, gwc_mat, 3 * F, F, 0)
        put_pieces(n, pieces_ref, gwo_ref, F, D, unit_plan(n, 3 * F, F)[2])


def middle(n, flags, uT, below, above, tails, cT, xT, wct, w3, w3t, vec, rows):
    S, F, N = uT.shape
    D = cT.shape[1]
    FE = F + R
    sd = jax.ShapeDtypeStruct
    return pl.pallas_call(
        functools.partial(middle_kernel, n, S // 2), grid=(S,),
        in_specs=[smem(), seq_spec(F, N), fixed(below.shape), fixed(above.shape), fixed(tails.shape), seq_spec(D, N), seq_spec(D, N),
                  fixed(wct.shape), fixed(w3.shape), fixed(w3t.shape), fixed(vec.shape)],
        out_specs=[seq_spec(F, N), seq_spec(D, N), fixed((n, WIDE // L, rows, L)), fixed((8, D)), fixed(tails.shape)],
        out_shape=[sd((S, F, N), BF), sd((S, D, N), BF), sd((n, WIDE // L, rows, L), F32), sd((8, D), F32), sd(tails.shape, BF)],
        scratch_shapes=[pltpu.VMEM((3, FE, N), BF), pltpu.VMEM((FE, N), BF), pltpu.VMEM((F, N), F32),
                        pltpu.VMEM((F, N), F32), pltpu.VMEM((F, N), F32), pltpu.VMEM((D, N), F32),
                        pltpu.VMEM((F, L), F32), pltpu.VMEM((F, L), F32), pltpu.VMEM((FE, D), F32),
                        pltpu.VMEM((3, FE, F), F32), pltpu.VMEM((F, 2 * SHIFT), BF), pltpu.VMEM((3 * F, F), F32)],
        compiler_params=params(), name="middle",
    )(flags, uT, below, above, tails, cT, xT, wct, w3, w3t, vec)


def back_kernel(n, seqs, flags_ref, e_ref, below_ref, above_ref, head_ref, n_ref, s_ref, rstd_ref, r1_ref, wc_ref, vec_ref,
                small_in, e1_ref, pieces_ref, small_ref, ebuf, d_ref, gacc, bacc, gwi_ref, hbuf):
    F, N = d_ref.shape
    D = gwi_ref.shape[0] - R
    i = pl.program_id(0)

    @pl.when(i == 0)
    def _():
        gwi_ref[...] = jnp.zeros_like(gwi_ref)
        gacc[...] = jnp.zeros_like(gacc)
        bacc[...] = jnp.zeros_like(bacc)

    rim_load(hbuf, i, seqs, 2 * SHIFT,
             lambda: jnp.where(flags_ref[1] == 1, head_ref[1], above_ref[...]),
             lambda: jnp.where(flags_ref[0] == 1, jnp.zeros_like(below_ref[...]), below_ref[...]))
    e, halo = e_ref[0], hbuf[...]
    for k in (1, 2):
        w = k * SHIFT
        ebuf[k - 1] = jnp.concatenate([e[:, w:], halo[:, :w]], axis=1)
    d_ref[...] = nn(wc_ref[0], e) + nn(wc_ref[1], ebuf[0]) + nn(wc_ref[2], ebuf[1])

    def first(j, carry):
        m1, m2 = carry
        rows = rows_at(j)
        ds = d_ref[rows, :] * s_ref[0, rows, :].astype(F32)
        dn = ds * n_ref[0, rows, :].astype(F32)
        d_ref[rows, :] = ds
        gain = vec_ref[rows, 0:1]
        lane_sum(bacc, rows, ds)
        lane_sum(gacc, rows, dn)
        return m1 + fold(ds * gain), m2 + fold(dn * gain)

    zero = jnp.zeros((8, N), F32)
    m1, m2 = loop(F // R, first, (zero, zero))
    pull_second(F, N, d_ref, n_ref.at[0], vec_ref, reduce8(m1), reduce8(m2), rstd_ref[0], e1_ref.at[0])
    gwi_ref[...] += nt(r1_ref[0], e1_ref[0])

    @pl.when(i == pl.num_programs(0) - 1)
    def _():
        small_ref[...] = small_in[...]
        small_ref[1:2, F:] = gwi_ref[D:D + 1, :]
        small_ref[3:4, :F] = lane_total(gacc[...])
        small_ref[3:4, F:] = lane_total(bacc[...])
        put_pieces(n, pieces_ref, gwi_ref, D, F, 0)


def back(n, flags, eT, below, above, heads, n1, s1, rstd1, r1, wc, vec, small, rows):
    S, F, N = eT.shape
    DE = r1.shape[1]
    sd = jax.ShapeDtypeStruct
    return pl.pallas_call(
        functools.partial(back_kernel, n, S // 2), grid=(S,),
        in_specs=[smem(), seq_spec(F, N), fixed(below.shape), fixed(above.shape), fixed(heads.shape), seq_spec(F, N), seq_spec(F, N),
                  seq_spec(1, N), seq_spec(DE, N), fixed(wc.shape), fixed(vec.shape), fixed(small.shape)],
        out_specs=[seq_spec(F, N), fixed((n, WIDE // L, rows, L)), fixed(small.shape)],
        out_shape=[sd((S, F, N), BF), sd((n, WIDE // L, rows, L), F32), sd(small.shape, F32)],
        scratch_shapes=[pltpu.VMEM((2, F, N), BF), pltpu.VMEM((F, N), F32), pltpu.VMEM((F, L), F32), pltpu.VMEM((F, L), F32),
                        pltpu.VMEM((DE, F), F32), pltpu.VMEM((F, 2 * SHIFT), BF)],
        compiler_params=params(), name="back",
    )(flags, eT, below, above, heads, n1, s1, rstd1, r1, wc, vec, small)


def wide_bwd_kernel(e_ref, w1_ref, n_ref, s_ref, rstd_ref, c_ref, vec_ref, small_in, dx_ref, small_ref, d_ref, gacc, bacc):
    D, N = d_ref.shape
    i = pl.program_id(0)

    @pl.when(i == 0)
    def _():
        gacc[...] = jnp.zeros_like(gacc)
        bacc[...] = jnp.zeros_like(bacc)

    d_ref[...] = nn(w1_ref[...], e_ref[0])

    def first(j, carry):
        m1, m2 = carry
        rows = rows_at(j)
        ds = d_ref[rows, :] * s_ref[0, rows, :].astype(F32)
        dn = ds * n_ref[0, rows, :].astype(F32)
        d_ref[rows, :] = ds
        gain = vec_ref[rows, 0:1]
        lane_sum(bacc, rows, ds)
        lane_sum(gacc, rows, dn)
        return m1 + fold(ds * gain), m2 + fold(dn * gain)

    zero = jnp.zeros((8, N), F32)
    m1, m2 = loop(D // R, first, (zero, zero))
    m1, m2 = reduce8(m1) * (1.0 / D), reduce8(m2) * (1.0 / D)
    rstd = rstd_ref[0]

    def second(j, _):
        rows = rows_at(j)
        t = d_ref[rows, :] * vec_ref[rows, 0:1]
        g = ((t - m1) - n_ref[0, rows, :].astype(F32) * m2) * rstd
        dx_ref[0, rows, :] = (g + c_ref[0, rows, :].astype(F32)).astype(BF)
        return 0

    loop(D // R, second, 0)

    @pl.when(i == pl.num_programs(0) - 1)
    def _():
        small_ref[...] = small_in[...]
        small_ref[4:5, :] = lane_total(gacc[...])
        small_ref[5:6, :] = lane_total(bacc[...])


def wide_bwd(e1, w1, n0, s0, rstd0, cT, vec, small):
    S, F, N = e1.shape
    D = cT.shape[1]
    sd = jax.ShapeDtypeStruct
    return pl.pallas_call(
        wide_bwd_kernel, grid=(S,),
        in_specs=[seq_spec(F, N), fixed(w1.shape), seq_spec(D, N), seq_spec(D, N), seq_spec(1, N), seq_spec(D, N), fixed(vec.shape),
                  fixed(small.shape)],
        out_specs=[seq_spec(D, N), fixed(small.shape)],
        out_shape=[sd((S, D, N), BF), sd(small.shape, F32)],
        scratch_shapes=[pltpu.VMEM((D, N), F32), pltpu.VMEM((D, L), F32), pltpu.VMEM((D, L), F32)],
        compiler_params=params(), name="wide_bwd",
    )(e1, w1, n0, s0, rstd0, cT, vec, small)


def bias_columns(v):
    cols, rest = [], v
    for _ in range(3):
        part = lax.reduce_precision(rest, 8, 7)
        cols.append(part)
        rest = rest - part
    return jnp.stack(cols + [jnp.zeros_like(v)] * (R - 3), axis=1).astype(BF)


def swap(v, bit, n):
    return lax.ppermute(v, "ctx", [(i, i ^ bit) for i in range(n)])


def bits_of(n):
    out, b = [], 1
    while b < n:
        out.append(b)
        b *= 2
    return out


def gather_all(piece, n):
    buf = piece[None]
    for bit in reversed(bits_of(n)):
        buf = jnp.concatenate([buf, swap(buf, bit, n)], axis=0)
    return buf


def slot_table(n, me):
    diff = jnp.arange(n, dtype=jnp.int32) ^ me
    return sum((jnp.where((diff & bit) != 0, n // 2 // bit, 0) for bit in bits_of(n)), jnp.zeros_like(diff))


def scatter_sum(full, n, me):
    rest = full
    for bit in bits_of(n):
        pairs = rest.reshape((-1, 2) + rest.shape[1:])
        mine = jnp.where((me & bit) == 0, 0, 1)
        keep = lax.dynamic_index_in_dim(pairs, mine, 1, keepdims=False)
        send = lax.dynamic_index_in_dim(pairs, 1 - mine, 1, keepdims=False).astype(BF)
        rest = keep + swap(send, bit, n).astype(F32)
    return rest[0]


def sum_all(v, n):
    for bit in bits_of(n):
        v = v + swap(v, bit, n)
    return v


def to_units(flat, n, M, C, rows=None):
    q, parts, units = unit_plan(n, M, C)
    return jnp.pad(flat.reshape(units, q), ((0, 0), (0, WIDE - q))).reshape(units, WIDE // L, L).transpose(1, 0, 2)


def round_up(v, m=8):
    return -(-v // m) * m


def on_device(block_input, cotangent, w_in, w_conv, w_out, wide_gain, wide_bias, narrow_gain, narrow_bias, dealing):
    slots, seqs, T, D = block_input.shape
    F = narrow_gain.shape[1]
    n = lax.axis_size("ctx")
    half = dealing.shape[0] // 2
    me = lax.axis_index("ctx")
    pair = jnp.sum(jnp.where(dealing[:half] == me, jnp.arange(half, dtype=jnp.int32), 0))
    flags = jnp.stack([pair == 0, pair == half - 1]).astype(jnp.int32)
    up = [(i, (i + 1) % n) for i in range(n)]
    down = [((i + 1) % n, i) for i in range(n)]
    table = slot_table(n, me)
    units_in, units_conv, units_out = (unit_plan(n, m, c)[2] for m, c in ((D, F), (3 * F, F), (F, D)))
    rows_in, rows_rest = round_up(units_in), round_up(units_conv + units_out)

    xT = block_input.transpose(0, 1, 3, 2).reshape(slots * seqs, D, T)
    cT = cotangent.transpose(0, 1, 3, 2).reshape(slots * seqs, D, T)

    piece_in = jnp.pad(to_units(w_in, n, D, F), ((0, 0), (0, rows_in - units_in), (0, 0)))
    piece_rest = jnp.concatenate([to_units(w_conv, n, 3 * F, F), to_units(w_out, n, F, D)], axis=1)
    piece_rest = jnp.pad(piece_rest, ((0, 0), (0, rows_rest - piece_rest.shape[1]), (0, 0)))
    w1, w1t = unpack_in(n, table, gather_all(piece_in, n), bias_columns(narrow_bias[0]), D, F)

    r1, n0, s0, rstd0 = wide_fwd(xT, jnp.stack([wide_gain, wide_bias[0]], axis=1))
    uT, n1, s1, rstd1, tails = front(r1, w1t, jnp.stack([narrow_gain[0], narrow_bias[1]], axis=1))

    below = lax.ppermute(tails[0], "ctx", up)
    above = lax.ppermute(tails[1], "ctx", down)
    wc, wct, w3, w3t = unpack_rest(n, table, gather_all(piece_rest, n), bias_columns(narrow_bias[2]), bias_columns(wide_bias[1]), D, F)
    eT, outT, part_rest, small, heads = middle(n, flags, uT, below, above, tails, cT, xT, wct, w3, w3t,
                                               jnp.stack([narrow_gain[1], narrow_bias[3]], axis=1), rows_rest)

    above = lax.ppermute(heads[0], "ctx", down)
    below = lax.ppermute(heads[1], "ctx", up)
    e1, part_in, small = back(n, flags, eT, below, above, heads, n1, s1, rstd1, r1, wc, narrow_gain[0][:, None], small, rows_in)
    own_rest = scatter_sum(part_rest, n, me)
    dxT, small = wide_bwd(e1, w1, n0, s0, rstd0, cT, wide_gain[:, None], small)
    own_in = scatter_sum(part_in, n, me)

    def owned(own, at, M, C):
        q, parts, units = unit_plan(n, M, C)
        return own[:, at:at + units].transpose(1, 0, 2).reshape(units, WIDE)[:, :q].reshape(-1)

    small = sum_all(small, n)
    back4 = lambda v: v.reshape(slots, seqs, D, T).transpose(0, 1, 3, 2)
    return (back4(outT), back4(dxT), owned(own_in, 0, D, F), owned(own_rest, 0, 3 * F, F), owned(own_rest, units_conv, F, D),
            small[4], jnp.stack([small[5], small[2]]), jnp.stack([small[3, :F], small[0, :F]]),
            jnp.stack([small[1, F:], small[3, F:], small[1, :F], small[0, F:]]))


def solution(mesh):
    whole, flat, copied = P("ctx", None, None, None), P("ctx"), P()
    return jax.shard_map(
        on_device, mesh=mesh,
        in_specs=(whole, whole, flat, flat, flat, copied, copied, copied, copied, copied),
        out_specs=(whole, whole, flat, flat, flat, copied, copied, copied, copied),
        check_vma=False,
    )
```

```python
import functools
import math
import jax
import jax.numpy as jnp
from jax import lax
from jax.experimental import pallas as pl
from jax.experimental.pallas import tpu as pltpu
from jax.sharding import PartitionSpec as P

EPS = 1e-05
BF = jnp.bfloat16
F32 = jnp.float32
L = 128
R = 16
SHIFT = 16
WIDE = 256


def params(mb=52):
    return pltpu.CompilerParams(dimension_semantics=("arbitrary",), vmem_limit_bytes=mb * 1024 * 1024)


def cost(flops, nbytes, trans=0):
    return pl.CostEstimate(flops=int(flops), bytes_accessed=int(nbytes), transcendentals=int(trans))


def rows_at(i):
    return pl.ds(pl.multiple_of(i * R, R), R)


def loop(n, body, init, unroll=25):
    return lax.fori_loop(0, n, body, init, unroll=min(n, unroll))


def fold(v):
    return v[:8] + v[8:]


def total8(v):
    return jnp.sum(v, axis=0, keepdims=True)


def nt(a, b):
    return lax.dot_general(a, b, (((1,), (1,)), ((), ())), preferred_element_type=F32)


def nn(a, b):
    return jnp.dot(a, b, preferred_element_type=F32)


def chunks(N, width):
    return [slice(l, min(N, l + width)) for l in range(0, N, width)]


def spread(table, rows, w):
    return jnp.concatenate([table[rows, :]] * (-(-w // L)), axis=1)[:, :w]


def fill_table(table, row):
    table[...] = jnp.broadcast_to(row, (L, row.shape[1])).T


def col_stats(read, chans, N):
    acc = loop(chans // R, lambda i, a: a + fold(read(i)), jnp.zeros((8, N), F32))
    mean = total8(acc) * (1.0 / chans)

    def second(i, a):
        cen = read(i) - mean
        return a + fold(cen * cen)

    acc = loop(chans // R, second, jnp.zeros((8, N), F32))
    return mean, lax.rsqrt(total8(acc) * (1.0 / chans) + EPS)


def gate(h):
    t = jnp.tanh(h)
    r = h + h * t
    return r, (1.0 + t) + (r - r * t)


def lane_sum(acc_ref, rows, v):
    N = v.shape[1]
    full = N // L * L
    tot = v[:, :L]
    for j in range(L, full, L):
        tot = tot + v[:, j:j + L]
    if full < N:
        tot = tot + jnp.concatenate([v[:, full:], jnp.zeros((v.shape[0], L - (N - full)), v.dtype)], axis=1)
    acc_ref[rows, :] += tot


def seq_spec(B, rows, N):
    return pl.BlockSpec((B, rows, N), lambda i: (i, 0, 0))


def fixed(shape):
    zero = (0,) * len(shape)
    return pl.BlockSpec(shape, lambda i: zero)


def smem():
    return pl.BlockSpec(memory_space=pltpu.SMEM)


def vmem():
    return pl.BlockSpec(memory_space=pltpu.VMEM)


def lane_total(acc):
    return jnp.sum(acc.T, axis=0, keepdims=True)


def unit_plan(n, M, C):
    size = M * C // n
    whole = math.gcd(size, C)
    q = max(d for d in range(1, WIDE + 1) if whole % d == 0)
    return q, C // q, size // q


def unit_slices(n, M, C):
    q, parts, units = unit_plan(n, M, C)
    out = []
    for p in range(n):
        for h in range(parts):
            lo = -((h - units * p) // parts)
            hi = -((h - units * (p + 1)) // parts)
            if hi > lo:
                out.append((p, h, lo, hi - lo, lo * parts + h - units * p))
    return out


def strided(start, size, step):
    return pl.ds(start, size, stride=step) if step > 1 else pl.ds(start, size)


def planes(q):
    return [(j, j * L, min(q - j * L, L)) for j in range(-(-q // L))]


def put_matrix(n, mat_ref, f32_ref, off):
    M, C = mat_ref.shape
    q, parts, _ = unit_plan(n, M, C)
    for p, h, lo, cnt, u in unit_slices(n, M, C):
        for j, at, w in planes(q):
            mat_ref[lo:lo + cnt, h * q + at:h * q + at + w] = f32_ref[p, j, strided(off + u, cnt, parts), :][:, :w]


def put_pieces(n, out_ref, mat_ref, M, C, off):
    q, parts, _ = unit_plan(n, M, C)
    for p, h, lo, cnt, u in unit_slices(n, M, C):
        for j, at, w in planes(q):
            v = mat_ref[lo:lo + cnt, h * q + at:h * q + at + w]
            if w < L:
                v = jnp.concatenate([v, jnp.zeros((cnt, L - w), v.dtype)], axis=1)
            out_ref[p, j, strided(off + u, cnt, parts), :] = v


def flipped(mat):
    C = mat.shape[1]
    eye = (lax.broadcasted_iota(jnp.int32, (C, C), 0) == lax.broadcasted_iota(jnp.int32, (C, C), 1)).astype(BF)
    return nt(eye, mat).astype(BF)


def ordered(n, slots_ref, g_ref, f32_ref):
    for p in range(n):
        f32_ref[p] = g_ref[slots_ref[p]].astype(F32)


def bias_block(row):
    v = jnp.broadcast_to(row, (L, row.shape[1])).T[:, :R]
    hi = v.astype(BF)
    rest = v - hi.astype(F32)
    mid = rest.astype(BF)
    low = (rest - mid.astype(F32)).astype(BF)
    col = lax.broadcasted_iota(jnp.int32, v.shape, 1)
    zero = jnp.zeros_like(v)
    return jnp.where(col == 0, hi.astype(F32), jnp.where(col == 1, mid.astype(F32), jnp.where(col == 2, low.astype(F32), zero))).astype(BF)


def unpack_in_kernel(n, slots_ref, g_ref, bias_ref, w1_ref, w1t_ref, f32_ref, mat_ref):
    ordered(n, slots_ref, g_ref, f32_ref)
    put_matrix(n, mat_ref, f32_ref, 0)
    D, F = mat_ref.shape
    w1_ref[...] = mat_ref[...].astype(BF)
    w1t_ref[:, :D] = flipped(w1_ref[...])
    w1t_ref[:, D:] = bias_block(bias_ref[0:1, :])


def unpack_in(n, slots, g, bias, D, F):
    sd = jax.ShapeDtypeStruct
    return pl.pallas_call(
        functools.partial(unpack_in_kernel, n),
        in_specs=[smem(), vmem(), vmem()], out_specs=[vmem(), vmem()],
        out_shape=[sd((D, F), BF), sd((F, D + R), BF)],
        scratch_shapes=[pltpu.VMEM(g.shape, F32), pltpu.VMEM((D, F), F32)],
        compiler_params=pltpu.CompilerParams(vmem_limit_bytes=40 * 1024 * 1024), name="unpack_in",
        cost_estimate=cost(1e9, 6e6),
    )(slots, g, bias)


def unpack_rest_kernel(n, slots_ref, g_ref, bias_ref, wide_ref, wc_ref, wct_ref, w3_ref, w3t_ref, f32_ref, matc_ref, mat3_ref):
    F, D = mat3_ref.shape
    ordered(n, slots_ref, g_ref, f32_ref)
    put_matrix(n, matc_ref, f32_ref, 0)
    put_matrix(n, mat3_ref, f32_ref, unit_plan(n, 3 * F, F)[2])
    for k in range(3):
        tap = matc_ref[k * F:(k + 1) * F, :].astype(BF)
        wc_ref[:, k * F:(k + 1) * F] = tap
        wct_ref[:, k * F:(k + 1) * F] = flipped(tap)
    wct_ref[:, 3 * F:] = bias_block(bias_ref[2:3, :])
    w3_ref[...] = mat3_ref[...].astype(BF)
    w3t_ref[:, :F] = flipped(w3_ref[...])
    w3t_ref[:, F:] = bias_block(wide_ref[1:2, :])


def unpack_rest(n, slots, g, bias, wide_bias, D, F):
    sd = jax.ShapeDtypeStruct
    return pl.pallas_call(
        functools.partial(unpack_rest_kernel, n),
        in_specs=[smem()] + [vmem()] * 3, out_specs=[vmem()] * 4,
        out_shape=[sd((F, 3 * F), BF), sd((F, 3 * F + R), BF), sd((F, D), BF), sd((D, F + R), BF)],
        scratch_shapes=[pltpu.VMEM(g.shape, F32), pltpu.VMEM((3 * F, F), F32), pltpu.VMEM((F, D), F32)],
        compiler_params=pltpu.CompilerParams(vmem_limit_bytes=40 * 1024 * 1024), name="unpack_rest",
        cost_estimate=cost(2e9, 14e6),
    )(slots, g, bias, wide_bias)


def rim_store(ref, i, steps, cols):
    for s in range(2 * steps):
        @pl.when(i == s)
        def _(s=s):
            w = cols[0].shape[1]
            for q, v in enumerate(cols):
                at = (s % steps * len(cols) + q) * w
                ref[s // steps, :, at:at + w] = v


def rim_load(buf, i, steps, first, second):
    w = buf.shape[1]
    for s in range(2 * steps):
        @pl.when(i == s)
        def _(s=s):
            src = first() if s < steps else second()
            buf[...] = src[:, s % steps * w:(s % steps + 1) * w]


def wide_fwd_kernel(Q, x_ref, gain_ref, bias_ref, *refs):
    r1_ref, n0_ref, s0_ref, rstd_ref, gtab, btab = refs[-6:]
    D, N = x_ref.shape[1:]
    fill_table(gtab, gain_ref[...] * 0.5)
    fill_table(btab, bias_ref[0:1, :] * 0.5)
    for q in range(Q):
        read = lambda i: x_ref[q, rows_at(i), :].astype(F32)
        mean, rstd = col_stats(read, D, N)
        rstd_ref[q] = rstd

        def act(i, _):
            rows = rows_at(i)
            n = (read(i) - mean) * rstd
            r, d = gate(n * spread(gtab, rows, N) + spread(btab, rows, N))
            r1_ref[0, rows, q * N:(q + 1) * N] = r.astype(BF)
            n0_ref[q, rows, :] = n.astype(BF)
            s0_ref[q, rows, :] = d.astype(BF)
            return 0

        loop(D // R, act, 0)
    r1_ref[0, D:, :] = jnp.ones((r1_ref.shape[1] - D, Q * N), BF)


def wide_fwd(xT, gain, bias, Q, start=0, steps=None, into=None):
    S, D, N = xT.shape
    steps = S // Q if steps is None else steps
    sd = jax.ShapeDtypeStruct
    at = lambda i: (start + i, 0, 0)
    into = () if into is None else into
    return pl.pallas_call(
        functools.partial(wide_fwd_kernel, Q), grid=(steps,),
        in_specs=[pl.BlockSpec((Q, D, N), at), fixed((1, D)), fixed((2, D))] + [pl.BlockSpec(memory_space=pl.ANY)] * len(into),
        out_specs=[pl.BlockSpec((1, D + R, Q * N), at), pl.BlockSpec((Q, D, N), at), pl.BlockSpec((Q, D, N), at), pl.BlockSpec((Q, 1, N), at)],
        out_shape=[sd((S // Q, D + R, Q * N), BF), sd((S, D, N), BF), sd((S, D, N), BF), sd((S, 1, N), F32)],
        scratch_shapes=[pltpu.VMEM((D, L), F32)] * 2,
        input_output_aliases={3 + j: j for j in range(len(into))},
        compiler_params=params(), name="wide_fwd", cost_estimate=cost(2e9 * steps, 11e6 * steps),
    )(xT, gain, bias, *into)


CH = 384


def front_kernel(Q, steps, r1_ref, w1t_ref, gain_ref, bias_ref, u_ref, n_ref, s_ref, rstd_ref, tail_ref, h_ref, gtab, btab):
    F, N = h_ref.shape
    T = N // Q
    i = pl.program_id(0)

    @pl.when(i == 0)
    def _():
        fill_table(gtab, gain_ref[0:1, :] * 0.5)
        fill_table(btab, bias_ref[1:2, :] * 0.5)

    h_ref[...] = nn(w1t_ref[...], r1_ref[0])
    for ls in chunks(N, CH):
        W = ls.stop - ls.start
        read = lambda j: h_ref[rows_at(j), ls]
        mean, rstd = col_stats(read, F, W)
        rstd_ref[0, :, ls] = rstd

        def act(j, _):
            rows = rows_at(j)
            n = (read(j) - mean) * rstd
            r, d = gate(n * spread(gtab, rows, W) + spread(btab, rows, W))
            u_ref[0, rows, ls] = r.astype(BF)
            n_ref[0, rows, ls] = n.astype(BF)
            s_ref[0, rows, ls] = d.astype(BF)
            return 0

        loop(F // R, act, 0)
    rim_store(tail_ref, i, steps, [u_ref[0, :, (q + 1) * T - 2 * SHIFT:(q + 1) * T] for q in range(Q)])


def front(r1, w1t, gain, bias, Q):
    G, DE, N = r1.shape
    F = w1t.shape[0]
    sd = jax.ShapeDtypeStruct
    rim = (2, F, G // 2 * Q * 2 * SHIFT)
    return pl.pallas_call(
        functools.partial(front_kernel, Q, G // 2), grid=(G,),
        in_specs=[seq_spec(1, DE, N), fixed(w1t.shape), fixed(gain.shape), fixed(bias.shape)],
        out_specs=[seq_spec(1, F, N)] * 3 + [seq_spec(1, 1, N), fixed(rim)],
        out_shape=[sd((G, F, N), BF)] * 3 + [sd((G, 1, N), F32), sd(rim, BF)],
        scratch_shapes=[pltpu.VMEM((F, N), F32)] + [pltpu.VMEM((F, L), F32)] * 2,
        compiler_params=params(), name="front", cost_estimate=cost(4e9, 19e6),
    )(r1, w1t, gain, bias)


def pull(F, W, ls, d_ref, n_at, s_at, rstd, gtab, gacc, bacc, e_ref):
    def first(j, carry):
        m1, m2 = carry
        rows = rows_at(j)
        ds = d_ref[rows, ls] * s_at(rows).astype(F32)
        dn = ds * n_at(rows).astype(F32)
        d_ref[rows, ls] = ds
        gain = spread(gtab, rows, W)
        lane_sum(bacc, rows, ds)
        lane_sum(gacc, rows, dn)
        return m1 + fold(ds * gain), m2 + fold(dn * gain)

    zero = jnp.zeros((8, W), F32)
    m1, m2 = loop(F // R, first, (zero, zero))
    m1, m2 = total8(m1) * (1.0 / F) * rstd, total8(m2) * (1.0 / F) * rstd

    def second(j, _):
        rows = rows_at(j)
        t = d_ref[rows, ls] * spread(gtab, rows, W) * rstd
        e_ref[0, rows, ls] = ((t - m1) - n_at(rows).astype(F32) * m2).astype(BF)
        return 0

    loop(F // R, second, 0)


def middle_kernel(n, Q, steps, flags_ref, u_ref, below_ref, above_ref, tail_ref, c_ref, x_ref, wct_ref, w3_ref, w3t_ref,
                  gain_ref, bias_ref, e_ref, out_ref, pieces_ref, small_ref, head_ref,
                  ubuf, cbuf, rbuf, h_ref, d_ref, n_ref, s_ref, o_ref, gacc, bacc, gwo_ref, gwc_ref, hbuf, gtab, btab):
    F, N = h_ref.shape
    T = N // Q
    D = c_ref.shape[1]
    i = pl.program_id(0)

    @pl.when(i == 0)
    def _():
        fill_table(gtab, gain_ref[1:2, :] * 0.5)
        fill_table(btab, bias_ref[3:4, :] * 0.5)
        ubuf[3 * F:, :] = jnp.ones((R, N), BF)
        rbuf[F:, :] = jnp.ones((R, N), BF)
        gwo_ref[...] = jnp.zeros_like(gwo_ref)
        gwc_ref[...] = jnp.zeros_like(gwc_ref)
        gacc[...] = jnp.zeros_like(gacc)
        bacc[...] = jnp.zeros_like(bacc)

    rim_load(hbuf, i, steps,
             lambda: jnp.where(flags_ref[0] == 1, jnp.zeros_like(below_ref[...]), below_ref[...]),
             lambda: jnp.where(flags_ref[1] == 1, tail_ref[0], above_ref[...]))
    ubuf[:F, :] = u_ref[0]
    for k in (1, 2):
        w = k * SHIFT
        parts = []
        for q in range(Q):
            parts += [hbuf[:, (q + 1) * 2 * SHIFT - w:(q + 1) * 2 * SHIFT], u_ref[0, :, q * T:(q + 1) * T - w]]
        ubuf[k * F:(k + 1) * F, :] = jnp.concatenate(parts, axis=1)
    for q in range(Q):
        cbuf[:, q * T:(q + 1) * T] = c_ref[q]
    h_ref[...] = nn(wct_ref[...], ubuf[...])
    d_ref[...] = nn(w3_ref[...], cbuf[...])
    rstds = []
    for ls in chunks(N, CH):
        W = ls.stop - ls.start
        read = lambda j: h_ref[rows_at(j), ls]
        mean, rstd = col_stats(read, F, W)
        rstds.append(rstd)

        def act(j, _):
            rows = rows_at(j)
            v = (read(j) - mean) * rstd
            r, d = gate(v * spread(gtab, rows, W) + spread(btab, rows, W))
            rbuf[rows, ls] = r.astype(BF)
            n_ref[rows, ls] = v.astype(BF)
            s_ref[rows, ls] = d.astype(BF)
            return 0

        loop(F // R, act, 0)
    o_ref[...] = nn(w3t_ref[...], rbuf[...])
    gwo_ref[...] += nt(rbuf[...], cbuf[...])
    for ls, rstd in zip(chunks(N, CH), rstds):
        pull(F, ls.stop - ls.start, ls, d_ref, lambda rows: n_ref[rows, ls], lambda rows: s_ref[rows, ls], rstd, gtab, gacc, bacc, e_ref)
    gwc_ref[...] += nt(ubuf[...], e_ref[0])
    for q in range(Q):
        def emit(j, _):
            rows = rows_at(j)
            out_ref[q, rows, :] = (o_ref[rows, q * T:(q + 1) * T] + x_ref[q, rows, :].astype(F32)).astype(BF)
            return 0

        loop(D // R, emit, 0, 50)
    rim_store(head_ref, i, steps, [e_ref[0, :, q * T:q * T + 2 * SHIFT] for q in range(Q)])

    @pl.when(i == pl.num_programs(0) - 1)
    def _():
        small_ref[...] = jnp.zeros_like(small_ref)
        small_ref[0:1, :F] = lane_total(gacc[...]) * 0.5
        small_ref[0:1, F:] = lane_total(bacc[...]) * 0.5
        small_ref[1:2, :F] = gwc_ref[3 * F:3 * F + 1, :]
        small_ref[2:3, :] = gwo_ref[F:F + 1, :]
        put_pieces(n, pieces_ref, gwc_ref, 3 * F, F, 0)
        put_pieces(n, pieces_ref, gwo_ref, F, D, unit_plan(n, 3 * F, F)[2])


def middle(n, Q, flags, uT, below, above, tails, cT, xT, wct, w3, w3t, gain, bias, rows):
    G, F, N = uT.shape
    S, D, T = cT.shape
    sd = jax.ShapeDtypeStruct
    return pl.pallas_call(
        functools.partial(middle_kernel, n, Q, G // 2), grid=(G,),
        in_specs=[smem(), seq_spec(1, F, N), fixed(below.shape), fixed(above.shape), fixed(tails.shape), seq_spec(Q, D, T), seq_spec(Q, D, T),
                  fixed(wct.shape), fixed(w3.shape), fixed(w3t.shape), fixed(gain.shape), fixed(bias.shape)],
        out_specs=[seq_spec(1, F, N), seq_spec(Q, D, T), fixed((n, WIDE // L, rows, L)), fixed((8, D)), fixed(tails.shape)],
        out_shape=[sd((G, F, N), BF), sd((S, D, T), BF), sd((n, WIDE // L, rows, L), F32), sd((8, D), F32), sd(tails.shape, BF)],
        scratch_shapes=[pltpu.VMEM((3 * F + R, N), BF), pltpu.VMEM((D, N), BF), pltpu.VMEM((F + R, N), BF), pltpu.VMEM((F, N), F32),
                        pltpu.VMEM((F, N), F32), pltpu.VMEM((F, N), BF), pltpu.VMEM((F, N), BF), pltpu.VMEM((D, N), F32),
                        pltpu.VMEM((F, L), F32), pltpu.VMEM((F, L), F32), pltpu.VMEM((F + R, D), F32),
                        pltpu.VMEM((3 * F + R, F), F32), pltpu.VMEM((F, Q * 2 * SHIFT), BF), pltpu.VMEM((F, L), F32), pltpu.VMEM((F, L), F32)],
        compiler_params=params(), name="middle", cost_estimate=cost(18e9, 36e6),
    )(flags, uT, below, above, tails, cT, xT, wct, w3, w3t, gain, bias)


def back_kernel(n, Q, steps, flags_ref, e_ref, below_ref, above_ref, head_ref, n_ref, s_ref, rstd_ref, r1_ref, wc_ref, gain_ref,
                small_in, e1_ref, pieces_ref, small_ref, ebuf, d_ref, gacc, bacc, gwi_ref, hbuf, gtab):
    F, N = d_ref.shape
    T = N // Q
    D = gwi_ref.shape[0] - R
    i = pl.program_id(0)

    @pl.when(i == 0)
    def _():
        fill_table(gtab, gain_ref[0:1, :] * 0.5)
        gwi_ref[...] = jnp.zeros_like(gwi_ref)
        gacc[...] = jnp.zeros_like(gacc)
        bacc[...] = jnp.zeros_like(bacc)

    rim_load(hbuf, i, steps,
             lambda: jnp.where(flags_ref[1] == 1, head_ref[1], above_ref[...]),
             lambda: jnp.where(flags_ref[0] == 1, jnp.zeros_like(below_ref[...]), below_ref[...]))
    ebuf[:F, :] = e_ref[0]
    for k in (1, 2):
        w = k * SHIFT
        parts = []
        for q in range(Q):
            parts += [e_ref[0, :, q * T + w:(q + 1) * T], hbuf[:, q * 2 * SHIFT:q * 2 * SHIFT + w]]
        ebuf[k * F:(k + 1) * F, :] = jnp.concatenate(parts, axis=1)
    d_ref[...] = nn(wc_ref[...], ebuf[...])
    for ls in chunks(N, CH):
        pull(F, ls.stop - ls.start, ls, d_ref, lambda rows: n_ref[0, rows, ls], lambda rows: s_ref[0, rows, ls], rstd_ref[0, :, ls],
             gtab, gacc, bacc, e1_ref)
    gwi_ref[...] += nt(r1_ref[0], e1_ref[0])

    @pl.when(i == pl.num_programs(0) - 1)
    def _():
        small_ref[...] = small_in[...]
        small_ref[1:2, F:] = gwi_ref[D:D + 1, :]
        small_ref[3:4, :F] = lane_total(gacc[...]) * 0.5
        small_ref[3:4, F:] = lane_total(bacc[...]) * 0.5
        put_pieces(n, pieces_ref, gwi_ref, D, F, 0)


def back(n, Q, flags, eT, below, above, heads, n1, s1, rstd1, r1, wc, gain, small, rows):
    G, F, N = eT.shape
    DE = r1.shape[1]
    sd = jax.ShapeDtypeStruct
    return pl.pallas_call(
        functools.partial(back_kernel, n, Q, G // 2), grid=(G,),
        in_specs=[smem(), seq_spec(1, F, N), fixed(below.shape), fixed(above.shape), fixed(heads.shape), seq_spec(1, F, N), seq_spec(1, F, N),
                  seq_spec(1, 1, N), seq_spec(1, DE, N), fixed(wc.shape), fixed(gain.shape), fixed(small.shape)],
        out_specs=[seq_spec(1, F, N), fixed((n, WIDE // L, rows, L)), fixed(small.shape)],
        out_shape=[sd((G, F, N), BF), sd((n, WIDE // L, rows, L), F32), sd(small.shape, F32)],
        scratch_shapes=[pltpu.VMEM((3 * F, N), BF), pltpu.VMEM((F, N), F32), pltpu.VMEM((F, L), F32), pltpu.VMEM((F, L), F32),
                        pltpu.VMEM((DE, F), F32), pltpu.VMEM((F, Q * 2 * SHIFT), BF), pltpu.VMEM((F, L), F32)],
        compiler_params=params(), name="back", cost_estimate=cost(8e9, 25e6),
    )(flags, eT, below, above, heads, n1, s1, rstd1, r1, wc, gain, small)


def wide_bwd_kernel(Q, e_ref, w1_ref, n_ref, s_ref, rstd_ref, c_ref, gain_ref, small_in, dx_ref, small_ref, gtab, gacc, bacc, *d_refs):
    D, N = d_refs[0].shape
    i = pl.program_id(0)

    @pl.when(i == 0)
    def _():
        fill_table(gtab, gain_ref[...] * 0.5)
        gacc[...] = jnp.zeros_like(gacc)
        bacc[...] = jnp.zeros_like(bacc)

    for q in range(Q):
        d_refs[q][...] = nn(w1_ref[...], e_ref[0, :, q * N:(q + 1) * N])
    for q in range(Q):
        d_ref = d_refs[q]

        def first(j, carry):
            m1, m2 = carry
            rows = rows_at(j)
            ds = d_ref[rows, :] * s_ref[q, rows, :].astype(F32)
            dn = ds * n_ref[q, rows, :].astype(F32)
            d_ref[rows, :] = ds
            gain = spread(gtab, rows, N)
            lane_sum(bacc, rows, ds)
            lane_sum(gacc, rows, dn)
            return m1 + fold(ds * gain), m2 + fold(dn * gain)

        zero = jnp.zeros((8, N), F32)
        m1, m2 = loop(D // R, first, (zero, zero))
        rstd = rstd_ref[q]
        m1, m2 = total8(m1) * (1.0 / D) * rstd, total8(m2) * (1.0 / D) * rstd

        def second(j, _):
            rows = rows_at(j)
            t = d_ref[rows, :] * spread(gtab, rows, N) * rstd
            g = (t - m1) - n_ref[q, rows, :].astype(F32) * m2
            dx_ref[q, rows, :] = (g + c_ref[q, rows, :].astype(F32)).astype(BF)
            return 0

        loop(D // R, second, 0)

    @pl.when(i == pl.num_programs(0) - 1)
    def _():
        small_ref[...] = small_in[...]
        small_ref[4:5, :] = lane_total(gacc[...]) * 0.5
        small_ref[5:6, :] = lane_total(bacc[...]) * 0.5


def wide_bwd(Q, e1, w1, n0, s0, rstd0, cT, gain, small):
    G, F, _ = e1.shape
    S, D, N = cT.shape
    sd = jax.ShapeDtypeStruct
    return pl.pallas_call(
        functools.partial(wide_bwd_kernel, Q), grid=(G,),
        in_specs=[seq_spec(1, F, Q * N), fixed(w1.shape), seq_spec(Q, D, N), seq_spec(Q, D, N), seq_spec(Q, 1, N), seq_spec(Q, D, N),
                  fixed(gain.shape), fixed(small.shape)],
        out_specs=[seq_spec(Q, D, N), fixed(small.shape)],
        out_shape=[sd((S, D, N), BF), sd(small.shape, F32)],
        scratch_shapes=[pltpu.VMEM((D, L), F32)] * 3 + [pltpu.VMEM((D, N), F32)] * Q,
        compiler_params=params(), name="wide_bwd", cost_estimate=cost(8e9, 34e6),
    )(e1, w1, n0, s0, rstd0, cT, gain, small)


def swap(v, bit, n):
    return lax.ppermute(v, "ctx", [(i, i ^ bit) for i in range(n)])


def bits_of(n):
    out, b = [], 1
    while b < n:
        out.append(b)
        b *= 2
    return out


def gather_all(piece, n):
    buf = piece[None]
    for bit in reversed(bits_of(n)):
        buf = jnp.concatenate([buf, swap(buf, bit, n)], axis=0)
    return buf


def slot_table(n, me):
    diff = jnp.arange(n, dtype=jnp.int32) ^ me
    return sum((jnp.where((diff & bit) != 0, n // 2 // bit, 0) for bit in bits_of(n)), jnp.zeros_like(diff))


def scatter_sum(full, n, me):
    rest = full
    for bit in bits_of(n):
        pairs = rest.reshape((-1, 2) + rest.shape[1:])
        mine = jnp.where((me & bit) == 0, 0, 1)
        keep = lax.dynamic_index_in_dim(pairs, mine, 1, keepdims=False)
        send = lax.dynamic_index_in_dim(pairs, 1 - mine, 1, keepdims=False).astype(BF)
        rest = keep + swap(send, bit, n).astype(F32)
    return rest[0]


def sum_all(v, n):
    for bit in bits_of(n):
        v = v + swap(v, bit, n)
    return v


def to_units(flat, n, M, C, rows=None):
    q, parts, units = unit_plan(n, M, C)
    return jnp.pad(flat.reshape(units, q), ((0, 0), (0, WIDE - q))).reshape(units, WIDE // L, L).transpose(1, 0, 2)


def round_up(v, m=8):
    return -(-v // m) * m


def on_device(block_input, cotangent, w_in, w_conv, w_out, wide_gain, wide_bias, narrow_gain, narrow_bias, dealing):
    slots, seqs, T, D = block_input.shape
    F = narrow_gain.shape[1]
    n = lax.axis_size("ctx")
    half = dealing.shape[0] // 2
    me = lax.axis_index("ctx")
    pair = jnp.sum(jnp.where(dealing[:half] == me, jnp.arange(half, dtype=jnp.int32), 0))
    flags = jnp.stack([pair == 0, pair == half - 1]).astype(jnp.int32)
    up = [(i, (i + 1) % n) for i in range(n)]
    down = [((i + 1) % n, i) for i in range(n)]
    table = slot_table(n, me)
    units_in, units_conv, units_out = (unit_plan(n, m, c)[2] for m, c in ((D, F), (3 * F, F), (F, D)))
    rows_in, rows_rest = round_up(units_in), round_up(units_conv + units_out)

    xT = block_input.transpose(0, 1, 3, 2).reshape(slots * seqs, D, T)
    cT = cotangent.transpose(0, 1, 3, 2).reshape(slots * seqs, D, T)

    piece_in = jnp.pad(to_units(w_in, n, D, F), ((0, 0), (0, rows_in - units_in), (0, 0)))
    piece_rest = jnp.concatenate([to_units(w_conv, n, 3 * F, F), to_units(w_out, n, F, D)], axis=1)
    piece_rest = jnp.pad(piece_rest, ((0, 0), (0, rows_rest - piece_rest.shape[1]), (0, 0)))
    w1, w1t = unpack_in(n, table, gather_all(piece_in, n), narrow_bias, D, F)

    gain0 = wide_gain.reshape(1, D)
    Q = 2
    r1, n0, s0, rstd0 = wide_fwd(xT, gain0, wide_bias, Q)
    uT, n1, s1, rstd1, tails = front(r1, w1t, narrow_gain, narrow_bias, Q)

    below = lax.ppermute(tails[0], "ctx", up)
    above = lax.ppermute(tails[1], "ctx", down)
    wc, wct, w3, w3t = unpack_rest(n, table, gather_all(piece_rest, n), narrow_bias, wide_bias, D, F)
    eT, outT, part_rest, small, heads = middle(n, Q, flags, uT, below, above, tails, cT, xT, wct, w3, w3t,
                                               narrow_gain, narrow_bias, rows_rest)

    above = lax.ppermute(heads[0], "ctx", down)
    below = lax.ppermute(heads[1], "ctx", up)
    e1, part_in, small = back(n, Q, flags, eT, below, above, heads, n1, s1, rstd1, r1, wc, narrow_gain, small, rows_in)
    own_rest = scatter_sum(part_rest, n, me)
    dxT, small = wide_bwd(Q, e1, w1, n0, s0, rstd0, cT, gain0, small)
    own_in = scatter_sum(part_in, n, me)

    def owned(own, at, M, C):
        q, parts, units = unit_plan(n, M, C)
        return own[:, at:at + units].transpose(1, 0, 2).reshape(units, WIDE)[:, :q].reshape(-1)

    small = sum_all(small, n)
    back4 = lambda v: v.reshape(slots, seqs, D, T).transpose(0, 1, 3, 2)
    return (back4(outT), back4(dxT), owned(own_in, 0, D, F), owned(own_rest, 0, 3 * F, F), owned(own_rest, units_conv, F, D),
            small[4], jnp.stack([small[5], small[2]]), jnp.stack([small[3, :F], small[0, :F]]),
            jnp.stack([small[1, F:], small[3, F:], small[1, :F], small[0, F:]]))


def solution(mesh):
    whole, flat, copied = P("ctx", None, None, None), P("ctx"), P()
    return jax.shard_map(
        on_device, mesh=mesh,
        in_specs=(whole, whole, flat, flat, flat, copied, copied, copied, copied, copied),
        out_specs=(whole, whole, flat, flat, flat, copied, copied, copied, copied),
        check_vma=False,
    )
```

```python
import functools
import math
import jax
import jax.numpy as jnp
from jax import lax
from jax.experimental import pallas as pl
from jax.experimental.pallas import tpu as pltpu
from jax.sharding import PartitionSpec as P

EPS = 1e-05
BF = jnp.bfloat16
F32 = jnp.float32
L = 128
R = 16
SHIFT = 16
WIDE = 256


def params(mb=52):
    return pltpu.CompilerParams(dimension_semantics=("arbitrary",), vmem_limit_bytes=mb * 1024 * 1024)


def cost(flops, nbytes, trans=0):
    return pl.CostEstimate(flops=int(flops), bytes_accessed=int(nbytes), transcendentals=int(trans))


def rows_at(i):
    return pl.ds(pl.multiple_of(i * R, R), R)


def loop(n, body, init, unroll=25):
    return lax.fori_loop(0, n, body, init, unroll=min(n, unroll))


def fold(v):
    return v[:8] + v[8:]


def total8(v):
    return jnp.sum(v, axis=0, keepdims=True)


def nt(a, b):
    return lax.dot_general(a, b, (((1,), (1,)), ((), ())), preferred_element_type=F32)


def nn(a, b):
    return jnp.dot(a, b, preferred_element_type=F32)


def chunks(N, width):
    return [slice(l, min(N, l + width)) for l in range(0, N, width)]


def spread(table, rows, w):
    return jnp.concatenate([table[rows, :]] * (-(-w // L)), axis=1)[:, :w]


def fill_table(table, row):
    table[...] = jnp.broadcast_to(row, (L, row.shape[1])).T


def col_stats(read, chans, N):
    acc = loop(chans // R, lambda i, a: a + fold(read(i)), jnp.zeros((8, N), F32))
    mean = total8(acc) * (1.0 / chans)

    def second(i, a):
        cen = read(i) - mean
        return a + fold(cen * cen)

    acc = loop(chans // R, second, jnp.zeros((8, N), F32))
    return mean, lax.rsqrt(total8(acc) * (1.0 / chans) + EPS)


def gate(h):
    t = jnp.tanh(h)
    r = h + h * t
    return r, (1.0 + t) + (r - r * t)


def lane_sum(acc_ref, rows, v):
    N = v.shape[1]
    full = N // L * L
    tot = v[:, :L]
    for j in range(L, full, L):
        tot = tot + v[:, j:j + L]
    if full < N:
        tot = tot + jnp.concatenate([v[:, full:], jnp.zeros((v.shape[0], L - (N - full)), v.dtype)], axis=1)
    acc_ref[rows, :] += tot


def seq_spec(B, rows, N):
    return pl.BlockSpec((B, rows, N), lambda i: (i, 0, 0))


def fixed(shape):
    zero = (0,) * len(shape)
    return pl.BlockSpec(shape, lambda i: zero)


def smem():
    return pl.BlockSpec(memory_space=pltpu.SMEM)


def vmem():
    return pl.BlockSpec(memory_space=pltpu.VMEM)


def lane_total(acc):
    return jnp.sum(acc.T, axis=0, keepdims=True)


def unit_plan(n, M, C):
    size = M * C // n
    whole = math.gcd(size, C)
    q = max(d for d in range(1, WIDE + 1) if whole % d == 0)
    return q, C // q, size // q


def unit_slices(n, M, C):
    q, parts, units = unit_plan(n, M, C)
    out = []
    for p in range(n):
        for h in range(parts):
            lo = -((h - units * p) // parts)
            hi = -((h - units * (p + 1)) // parts)
            if hi > lo:
                out.append((p, h, lo, hi - lo, lo * parts + h - units * p))
    return out


def strided(start, size, step):
    return pl.ds(start, size, stride=step) if step > 1 else pl.ds(start, size)


def planes(q):
    return [(j, j * L, min(q - j * L, L)) for j in range(-(-q // L))]


def put_matrix(n, mat_ref, f32_ref, off):
    M, C = mat_ref.shape
    q, parts, _ = unit_plan(n, M, C)
    for p, h, lo, cnt, u in unit_slices(n, M, C):
        for j, at, w in planes(q):
            mat_ref[lo:lo + cnt, h * q + at:h * q + at + w] = f32_ref[p, j, strided(off + u, cnt, parts), :][:, :w]


def put_pieces(n, out_ref, mat_ref, M, C, off):
    q, parts, _ = unit_plan(n, M, C)
    for p, h, lo, cnt, u in unit_slices(n, M, C):
        for j, at, w in planes(q):
            v = mat_ref[lo:lo + cnt, h * q + at:h * q + at + w]
            if w < L:
                v = jnp.concatenate([v, jnp.zeros((cnt, L - w), v.dtype)], axis=1)
            out_ref[p, j, strided(off + u, cnt, parts), :] = v


def flipped(mat):
    C = mat.shape[1]
    eye = (lax.broadcasted_iota(jnp.int32, (C, C), 0) == lax.broadcasted_iota(jnp.int32, (C, C), 1)).astype(BF)
    return nt(eye, mat).astype(BF)


def ordered(n, slots_ref, g_ref, f32_ref):
    for p in range(n):
        f32_ref[p] = g_ref[slots_ref[p]].astype(F32)


def bias_block(row):
    v = jnp.broadcast_to(row, (L, row.shape[1])).T[:, :R]
    hi = v.astype(BF)
    rest = v - hi.astype(F32)
    mid = rest.astype(BF)
    low = (rest - mid.astype(F32)).astype(BF)
    col = lax.broadcasted_iota(jnp.int32, v.shape, 1)
    zero = jnp.zeros_like(v)
    return jnp.where(col == 0, hi.astype(F32), jnp.where(col == 1, mid.astype(F32), jnp.where(col == 2, low.astype(F32), zero))).astype(BF)


def unpack_in_kernel(n, slots_ref, g_ref, bias_ref, token_ref, w1_ref, w1t_ref, f32_ref, mat_ref):
    ordered(n, slots_ref, g_ref, f32_ref)
    put_matrix(n, mat_ref, f32_ref, 0)
    D, F = mat_ref.shape
    w1_ref[...] = mat_ref[...].astype(BF)
    w1t_ref[:, :D] = flipped(w1_ref[...])
    w1t_ref[:, D:] = bias_block(bias_ref[0:1, :])


def unpack_in(n, slots, g, bias, token, D, F):
    sd = jax.ShapeDtypeStruct
    return pl.pallas_call(
        functools.partial(unpack_in_kernel, n),
        in_specs=[smem(), vmem(), vmem(), pl.BlockSpec(memory_space=pl.ANY)], out_specs=[vmem(), vmem()],
        out_shape=[sd((D, F), BF), sd((F, D + R), BF)],
        scratch_shapes=[pltpu.VMEM(g.shape, F32), pltpu.VMEM((D, F), F32)],
        compiler_params=pltpu.CompilerParams(vmem_limit_bytes=40 * 1024 * 1024), name="unpack_in",
        cost_estimate=cost(1e9, 6e6),
    )(slots, g, bias, token)


def unpack_rest_kernel(n, slots_ref, g_ref, bias_ref, wide_ref, wc_ref, wct_ref, w3_ref, w3t_ref, f32_ref, matc_ref, mat3_ref):
    F, D = mat3_ref.shape
    ordered(n, slots_ref, g_ref, f32_ref)
    put_matrix(n, matc_ref, f32_ref, 0)
    put_matrix(n, mat3_ref, f32_ref, unit_plan(n, 3 * F, F)[2])
    for k in range(3):
        tap = matc_ref[k * F:(k + 1) * F, :].astype(BF)
        wc_ref[:, k * F:(k + 1) * F] = tap
        wct_ref[:, k * F:(k + 1) * F] = flipped(tap)
    wct_ref[:, 3 * F:] = bias_block(bias_ref[2:3, :])
    w3_ref[...] = mat3_ref[...].astype(BF)
    w3t_ref[:, :F] = flipped(w3_ref[...])
    w3t_ref[:, F:] = bias_block(wide_ref[1:2, :])


def unpack_rest(n, slots, g, bias, wide_bias, D, F):
    sd = jax.ShapeDtypeStruct
    return pl.pallas_call(
        functools.partial(unpack_rest_kernel, n),
        in_specs=[smem()] + [vmem()] * 3, out_specs=[vmem()] * 4,
        out_shape=[sd((F, 3 * F), BF), sd((F, 3 * F + R), BF), sd((F, D), BF), sd((D, F + R), BF)],
        scratch_shapes=[pltpu.VMEM(g.shape, F32), pltpu.VMEM((3 * F, F), F32), pltpu.VMEM((F, D), F32)],
        compiler_params=pltpu.CompilerParams(vmem_limit_bytes=40 * 1024 * 1024), name="unpack_rest",
        cost_estimate=cost(2e9, 14e6),
    )(slots, g, bias, wide_bias)


def rim_store(ref, i, steps, cols):
    for s in range(2 * steps):
        @pl.when(i == s)
        def _(s=s):
            w = cols[0].shape[1]
            for q, v in enumerate(cols):
                at = (s % steps * len(cols) + q) * w
                ref[s // steps, :, at:at + w] = v


def rim_load(buf, i, steps, first, second):
    w = buf.shape[1]
    for s in range(2 * steps):
        @pl.when(i == s)
        def _(s=s):
            src = first() if s < steps else second()
            buf[...] = src[:, s % steps * w:(s % steps + 1) * w]


def wide_fwd_kernel(Q, x_ref, gain_ref, bias_ref, *refs):
    r1_ref, n0_ref, s0_ref, rstd_ref, token_ref, gtab, btab = refs[-7:]
    token_ref[...] = jnp.zeros_like(token_ref)
    D, N = x_ref.shape[1:]
    fill_table(gtab, gain_ref[...] * 0.5)
    fill_table(btab, bias_ref[0:1, :] * 0.5)
    for q in range(Q):
        read = lambda i: x_ref[q, rows_at(i), :].astype(F32)
        mean, rstd = col_stats(read, D, N)
        rstd_ref[q] = rstd

        def act(i, _):
            rows = rows_at(i)
            n = (read(i) - mean) * rstd
            r, d = gate(n * spread(gtab, rows, N) + spread(btab, rows, N))
            r1_ref[0, rows, q * N:(q + 1) * N] = r.astype(BF)
            n0_ref[q, rows, :] = n.astype(BF)
            s0_ref[q, rows, :] = d.astype(BF)
            return 0

        loop(D // R, act, 0)
    r1_ref[0, D:, :] = jnp.ones((r1_ref.shape[1] - D, Q * N), BF)


def wide_fwd(xT, gain, bias, Q, start=0, steps=None, into=None, token=None):
    S, D, N = xT.shape
    steps = S // Q if steps is None else steps
    sd = jax.ShapeDtypeStruct
    at = lambda i: (start + i, 0, 0)
    into = tuple(into or ())
    token = () if token is None else (token,)
    return pl.pallas_call(
        functools.partial(wide_fwd_kernel, Q), grid=(steps,),
        in_specs=[pl.BlockSpec((Q, D, N), at), fixed((1, D)), fixed((2, D))] + [pl.BlockSpec(memory_space=pl.ANY)] * len(into + token),
        out_specs=[pl.BlockSpec((1, D + R, Q * N), at), pl.BlockSpec((Q, D, N), at), pl.BlockSpec((Q, D, N), at), pl.BlockSpec((Q, 1, N), at),
                   fixed((8, L))],
        out_shape=[sd((S // Q, D + R, Q * N), BF), sd((S, D, N), BF), sd((S, D, N), BF), sd((S, 1, N), F32), sd((8, L), F32)],
        scratch_shapes=[pltpu.VMEM((D, L), F32)] * 2,
        input_output_aliases={3 + j: j for j in range(len(into))},
        compiler_params=params(), name="wide_fwd", cost_estimate=cost(2e9 * steps, 11e6 * steps),
    )(xT, gain, bias, *into, *token)


CH = 384


def front_kernel(Q, steps, r1_ref, w1t_ref, gain_ref, bias_ref, u_ref, n_ref, s_ref, rstd_ref, tail_ref, h_ref, gtab, btab):
    F, N = h_ref.shape
    T = N // Q
    i = pl.program_id(0)

    @pl.when(i == 0)
    def _():
        fill_table(gtab, gain_ref[0:1, :] * 0.5)
        fill_table(btab, bias_ref[1:2, :] * 0.5)

    h_ref[...] = nn(w1t_ref[...], r1_ref[0])
    for ls in chunks(N, CH):
        W = ls.stop - ls.start
        read = lambda j: h_ref[rows_at(j), ls]
        mean, rstd = col_stats(read, F, W)
        rstd_ref[0, :, ls] = rstd

        def act(j, _):
            rows = rows_at(j)
            n = (read(j) - mean) * rstd
            r, d = gate(n * spread(gtab, rows, W) + spread(btab, rows, W))
            u_ref[0, rows, ls] = r.astype(BF)
            n_ref[0, rows, ls] = n.astype(BF)
            s_ref[0, rows, ls] = d.astype(BF)
            return 0

        loop(F // R, act, 0)
    rim_store(tail_ref, i, steps, [u_ref[0, :, (q + 1) * T - 2 * SHIFT:(q + 1) * T] for q in range(Q)])


def front(r1, w1t, gain, bias, Q):
    G, DE, N = r1.shape
    F = w1t.shape[0]
    sd = jax.ShapeDtypeStruct
    rim = (2, F, G // 2 * Q * 2 * SHIFT)
    return pl.pallas_call(
        functools.partial(front_kernel, Q, G // 2), grid=(G,),
        in_specs=[seq_spec(1, DE, N), fixed(w1t.shape), fixed(gain.shape), fixed(bias.shape)],
        out_specs=[seq_spec(1, F, N)] * 3 + [seq_spec(1, 1, N), fixed(rim)],
        out_shape=[sd((G, F, N), BF)] * 3 + [sd((G, 1, N), F32), sd(rim, BF)],
        scratch_shapes=[pltpu.VMEM((F, N), F32)] + [pltpu.VMEM((F, L), F32)] * 2,
        compiler_params=params(), name="front", cost_estimate=cost(4e9, 19e6),
    )(r1, w1t, gain, bias)


def pull(F, W, ls, d_ref, n_at, s_at, rstd, gtab, gacc, bacc, e_ref):
    def first(j, carry):
        m1, m2 = carry
        rows = rows_at(j)
        ds = d_ref[rows, ls] * s_at(rows).astype(F32)
        dn = ds * n_at(rows).astype(F32)
        d_ref[rows, ls] = ds
        gain = spread(gtab, rows, W)
        lane_sum(bacc, rows, ds)
        lane_sum(gacc, rows, dn)
        return m1 + fold(ds * gain), m2 + fold(dn * gain)

    zero = jnp.zeros((8, W), F32)
    m1, m2 = loop(F // R, first, (zero, zero))
    m1, m2 = total8(m1) * (1.0 / F) * rstd, total8(m2) * (1.0 / F) * rstd

    def second(j, _):
        rows = rows_at(j)
        t = d_ref[rows, ls] * spread(gtab, rows, W) * rstd
        e_ref[0, rows, ls] = ((t - m1) - n_at(rows).astype(F32) * m2).astype(BF)
        return 0

    loop(F // R, second, 0)


def middle_kernel(n, Q, steps, flags_ref, u_ref, below_ref, above_ref, tail_ref, c_ref, x_ref, wct_ref, w3_ref, w3t_ref,
                  gain_ref, bias_ref, e_ref, out_ref, pieces_ref, small_ref, head_ref,
                  ubuf, cbuf, rbuf, h_ref, d_ref, n_ref, s_ref, o_ref, gacc, bacc, gwo_ref, gwc_ref, hbuf, gtab, btab):
    F, N = h_ref.shape
    T = N // Q
    D = c_ref.shape[1]
    i = pl.program_id(0)

    @pl.when(i == 0)
    def _():
        fill_table(gtab, gain_ref[1:2, :] * 0.5)
        fill_table(btab, bias_ref[3:4, :] * 0.5)
        ubuf[3 * F:, :] = jnp.ones((R, N), BF)
        rbuf[F:, :] = jnp.ones((R, N), BF)
        gwo_ref[...] = jnp.zeros_like(gwo_ref)
        gwc_ref[...] = jnp.zeros_like(gwc_ref)
        gacc[...] = jnp.zeros_like(gacc)
        bacc[...] = jnp.zeros_like(bacc)

    rim_load(hbuf, i, steps,
             lambda: jnp.where(flags_ref[0] == 1, jnp.zeros_like(below_ref[...]), below_ref[...]),
             lambda: jnp.where(flags_ref[1] == 1, tail_ref[0], above_ref[...]))
    ubuf[:F, :] = u_ref[0]
    for k in (1, 2):
        w = k * SHIFT
        parts = []
        for q in range(Q):
            parts += [hbuf[:, (q + 1) * 2 * SHIFT - w:(q + 1) * 2 * SHIFT], u_ref[0, :, q * T:(q + 1) * T - w]]
        ubuf[k * F:(k + 1) * F, :] = jnp.concatenate(parts, axis=1)
    for q in range(Q):
        cbuf[:, q * T:(q + 1) * T] = c_ref[q]
    h_ref[...] = nn(wct_ref[...], ubuf[...])
    d_ref[...] = nn(w3_ref[...], cbuf[...])
    rstds = []
    for ls in chunks(N, CH):
        W = ls.stop - ls.start
        read = lambda j: h_ref[rows_at(j), ls]
        mean, rstd = col_stats(read, F, W)
        rstds.append(rstd)

        def act(j, _):
            rows = rows_at(j)
            v = (read(j) - mean) * rstd
            r, d = gate(v * spread(gtab, rows, W) + spread(btab, rows, W))
            rbuf[rows, ls] = r.astype(BF)
            n_ref[rows, ls] = v
            s_ref[rows, ls] = d
            return 0

        loop(F // R, act, 0)
    o_ref[...] = nn(w3t_ref[...], rbuf[...])
    gwo_ref[...] += nt(rbuf[...], cbuf[...])
    for ls, rstd in zip(chunks(N, CH), rstds):
        pull(F, ls.stop - ls.start, ls, d_ref, lambda rows: n_ref[rows, ls], lambda rows: s_ref[rows, ls], rstd, gtab, gacc, bacc, e_ref)
    gwc_ref[...] += nt(ubuf[...], e_ref[0])
    for q in range(Q):
        def emit(j, _):
            rows = rows_at(j)
            out_ref[q, rows, :] = (o_ref[rows, q * T:(q + 1) * T] + x_ref[q, rows, :].astype(F32)).astype(BF)
            return 0

        loop(D // R, emit, 0, 50)
    rim_store(head_ref, i, steps, [e_ref[0, :, q * T:q * T + 2 * SHIFT] for q in range(Q)])

    @pl.when(i == pl.num_programs(0) - 1)
    def _():
        small_ref[...] = jnp.zeros_like(small_ref)
        small_ref[0:1, :F] = lane_total(gacc[...]) * 0.5
        small_ref[0:1, F:] = lane_total(bacc[...]) * 0.5
        small_ref[1:2, :F] = gwc_ref[3 * F:3 * F + 1, :]
        small_ref[2:3, :] = gwo_ref[F:F + 1, :]
        put_pieces(n, pieces_ref, gwc_ref, 3 * F, F, 0)
        put_pieces(n, pieces_ref, gwo_ref, F, D, unit_plan(n, 3 * F, F)[2])


def middle(n, Q, flags, uT, below, above, tails, cT, xT, wct, w3, w3t, gain, bias, rows):
    G, F, N = uT.shape
    S, D, T = cT.shape
    sd = jax.ShapeDtypeStruct
    return pl.pallas_call(
        functools.partial(middle_kernel, n, Q, G // 2), grid=(G,),
        in_specs=[smem(), seq_spec(1, F, N), fixed(below.shape), fixed(above.shape), fixed(tails.shape), seq_spec(Q, D, T), seq_spec(Q, D, T),
                  fixed(wct.shape), fixed(w3.shape), fixed(w3t.shape), fixed(gain.shape), fixed(bias.shape)],
        out_specs=[seq_spec(1, F, N), seq_spec(Q, D, T), fixed((n, WIDE // L, rows, L)), fixed((8, D)), fixed(tails.shape)],
        out_shape=[sd((G, F, N), BF), sd((S, D, T), BF), sd((n, WIDE // L, rows, L), F32), sd((8, D), F32), sd(tails.shape, BF)],
        scratch_shapes=[pltpu.VMEM((3 * F + R, N), BF), pltpu.VMEM((D, N), BF), pltpu.VMEM((F + R, N), BF), pltpu.VMEM((F, N), F32),
                        pltpu.VMEM((F, N), F32), pltpu.VMEM((F, N), F32), pltpu.VMEM((F, N), F32), pltpu.VMEM((D, N), F32),
                        pltpu.VMEM((F, L), F32), pltpu.VMEM((F, L), F32), pltpu.VMEM((F + R, D), F32),
                        pltpu.VMEM((3 * F + R, F), F32), pltpu.VMEM((F, Q * 2 * SHIFT), BF), pltpu.VMEM((F, L), F32), pltpu.VMEM((F, L), F32)],
        compiler_params=params(), name="middle", cost_estimate=cost(18e9, 36e6),
    )(flags, uT, below, above, tails, cT, xT, wct, w3, w3t, gain, bias)


def back_kernel(n, Q, steps, flags_ref, e_ref, below_ref, above_ref, head_ref, n_ref, s_ref, rstd_ref, r1_ref, wc_ref, gain_ref,
                small_in, e1_ref, pieces_ref, small_ref, ebuf, d_ref, gacc, bacc, gwi_ref, hbuf, gtab, e1buf):
    F, N = d_ref.shape
    T = N // Q
    D = gwi_ref.shape[0] - R
    i = pl.program_id(0)

    @pl.when(i == 0)
    def _():
        fill_table(gtab, gain_ref[0:1, :] * 0.5)
        gwi_ref[...] = jnp.zeros_like(gwi_ref)
        gacc[...] = jnp.zeros_like(gacc)
        bacc[...] = jnp.zeros_like(bacc)

    rim_load(hbuf, i, steps,
             lambda: jnp.where(flags_ref[1] == 1, head_ref[1], above_ref[...]),
             lambda: jnp.where(flags_ref[0] == 1, jnp.zeros_like(below_ref[...]), below_ref[...]))
    ebuf[:F, :] = e_ref[0]
    for k in (1, 2):
        w = k * SHIFT
        parts = []
        for q in range(Q):
            parts += [e_ref[0, :, q * T + w:(q + 1) * T], hbuf[:, q * 2 * SHIFT:q * 2 * SHIFT + w]]
        ebuf[k * F:(k + 1) * F, :] = jnp.concatenate(parts, axis=1)
    d_ref[...] = nn(wc_ref[...], ebuf[...])
    for ls in chunks(N, CH):
        pull(F, ls.stop - ls.start, ls, d_ref, lambda rows: n_ref[0, rows, ls], lambda rows: s_ref[0, rows, ls], rstd_ref[0, :, ls],
             gtab, gacc, bacc, e1buf)
    gwi_ref[...] += nt(r1_ref[0], e1buf[0])
    for q in range(Q):
        e1_ref[q] = e1buf[0, :, q * T:(q + 1) * T]

    @pl.when(i == pl.num_programs(0) - 1)
    def _():
        small_ref[...] = small_in[...]
        small_ref[1:2, F:] = gwi_ref[D:D + 1, :]
        small_ref[3:4, :F] = lane_total(gacc[...]) * 0.5
        small_ref[3:4, F:] = lane_total(bacc[...]) * 0.5
        put_pieces(n, pieces_ref, gwi_ref, D, F, 0)


def back(n, Q, flags, eT, below, above, heads, n1, s1, rstd1, r1, wc, gain, small, rows):
    G, F, N = eT.shape
    DE = r1.shape[1]
    sd = jax.ShapeDtypeStruct
    return pl.pallas_call(
        functools.partial(back_kernel, n, Q, G // 2), grid=(G,),
        in_specs=[smem(), seq_spec(1, F, N), fixed(below.shape), fixed(above.shape), fixed(heads.shape), seq_spec(1, F, N), seq_spec(1, F, N),
                  seq_spec(1, 1, N), seq_spec(1, DE, N), fixed(wc.shape), fixed(gain.shape), fixed(small.shape)],
        out_specs=[seq_spec(Q, F, N // Q), fixed((n, WIDE // L, rows, L)), fixed(small.shape)],
        out_shape=[sd((G * Q, F, N // Q), BF), sd((n, WIDE // L, rows, L), F32), sd(small.shape, F32)],
        scratch_shapes=[pltpu.VMEM((3 * F, N), BF), pltpu.VMEM((F, N), F32), pltpu.VMEM((F, L), F32), pltpu.VMEM((F, L), F32),
                        pltpu.VMEM((DE, F), F32), pltpu.VMEM((F, Q * 2 * SHIFT), BF), pltpu.VMEM((F, L), F32),
                        pltpu.VMEM((1, F, N), BF)],
        compiler_params=params(), name="back", cost_estimate=cost(8e9, 25e6),
    )(flags, eT, below, above, heads, n1, s1, rstd1, r1, wc, gain, small)


def wide_bwd_kernel(e_ref, w1_ref, n_ref, s_ref, rstd_ref, c_ref, gain_ref, small_in, *refs):
    dx_ref, small_ref, gtab, gacc, bacc, d_ref = refs[-6:]
    D, N = d_ref.shape
    i = pl.program_id(0)

    @pl.when(i == 0)
    def _():
        fill_table(gtab, gain_ref[...] * 0.5)
        gacc[...] = jnp.zeros_like(gacc)
        bacc[...] = jnp.zeros_like(bacc)

    d_ref[...] = nn(w1_ref[...], e_ref[0])

    def first(j, carry):
        m1, m2 = carry
        rows = rows_at(j)
        ds = d_ref[rows, :] * s_ref[0, rows, :].astype(F32)
        dn = ds * n_ref[0, rows, :].astype(F32)
        d_ref[rows, :] = ds
        gain = spread(gtab, rows, N)
        lane_sum(bacc, rows, ds)
        lane_sum(gacc, rows, dn)
        return m1 + fold(ds * gain), m2 + fold(dn * gain)

    zero = jnp.zeros((8, N), F32)
    m1, m2 = loop(D // R, first, (zero, zero))
    rstd = rstd_ref[0]
    m1, m2 = total8(m1) * (1.0 / D) * rstd, total8(m2) * (1.0 / D) * rstd

    def second(j, _):
        rows = rows_at(j)
        t = d_ref[rows, :] * spread(gtab, rows, N) * rstd
        g = (t - m1) - n_ref[0, rows, :].astype(F32) * m2
        dx_ref[0, rows, :] = (g + c_ref[0, rows, :].astype(F32)).astype(BF)
        return 0

    loop(D // R, second, 0)

    @pl.when(i == pl.num_programs(0) - 1)
    def _():
        small_ref[...] = small_in[...]
        small_ref[4:5, :] = small_in[4:5, :] + lane_total(gacc[...]) * 0.5
        small_ref[5:6, :] = small_in[5:6, :] + lane_total(bacc[...]) * 0.5


def wide_bwd(e1, w1, n0, s0, rstd0, cT, gain, small, start=0, steps=None, into=None):
    S, D, N = cT.shape
    F = e1.shape[1]
    steps = S if steps is None else steps
    sd = jax.ShapeDtypeStruct
    at = lambda i: (start + i, 0, 0)
    into = () if into is None else (into,)
    part = lambda rows: pl.BlockSpec((1, rows, N), at)
    return pl.pallas_call(
        wide_bwd_kernel, grid=(steps,),
        in_specs=[part(F), fixed(w1.shape), part(D), part(D), part(1), part(D),
                  fixed(gain.shape), fixed(small.shape)] + [pl.BlockSpec(memory_space=pl.ANY)] * len(into),
        out_specs=[part(D), fixed(small.shape)],
        out_shape=[sd((S, D, N), BF), sd(small.shape, F32)],
        scratch_shapes=[pltpu.VMEM((D, L), F32)] * 3 + [pltpu.VMEM((D, N), F32)],
        input_output_aliases={8: 0} if into else {},
        compiler_params=params(), name="wide_bwd", cost_estimate=cost(1e9 * steps, 4.2e6 * steps),
    )(e1, w1, n0, s0, rstd0, cT, gain, small, *into)


def swap(v, bit, n):
    return lax.ppermute(v, "ctx", [(i, i ^ bit) for i in range(n)])


def bits_of(n):
    out, b = [], 1
    while b < n:
        out.append(b)
        b *= 2
    return out


def together(*values):
    return lax.optimization_barrier(values)


def slot_table(n, me):
    diff = jnp.arange(n, dtype=jnp.int32) ^ me
    return sum((jnp.where((diff & bit) != 0, n // 2 // bit, 0) for bit in bits_of(n)), jnp.zeros_like(diff))


def split_for(full, bit, me):
    pairs = full.reshape((-1, 2) + full.shape[1:])
    mine = jnp.where((me & bit) == 0, 0, 1)
    keep = lax.dynamic_index_in_dim(pairs, mine, 1, keepdims=False)
    return keep, lax.dynamic_index_in_dim(pairs, 1 - mine, 1, keepdims=False).astype(BF)


def sum_all(v, n):
    for bit in bits_of(n):
        v = v + swap(v, bit, n)
    return v


def to_units(flat, n, M, C, rows=None):
    q, parts, units = unit_plan(n, M, C)
    return jnp.pad(flat.reshape(units, q), ((0, 0), (0, WIDE - q))).reshape(units, WIDE // L, L).transpose(1, 0, 2)


def round_up(v, m=8):
    return -(-v // m) * m


def on_device(block_input, cotangent, w_in, w_conv, w_out, wide_gain, wide_bias, narrow_gain, narrow_bias, dealing):
    slots, seqs, T, D = block_input.shape
    F = narrow_gain.shape[1]
    n = lax.axis_size("ctx")
    half = dealing.shape[0] // 2
    me = lax.axis_index("ctx")
    pair = jnp.sum(jnp.where(dealing[:half] == me, jnp.arange(half, dtype=jnp.int32), 0))
    flags = jnp.stack([pair == 0, pair == half - 1]).astype(jnp.int32)
    up = [(i, (i + 1) % n) for i in range(n)]
    down = [((i + 1) % n, i) for i in range(n)]
    table = slot_table(n, me)
    units_in, units_conv, units_out = (unit_plan(n, m, c)[2] for m, c in ((D, F), (3 * F, F), (F, D)))
    rows_in, rows_rest = round_up(units_in), round_up(units_conv + units_out)

    xT = block_input.transpose(0, 1, 3, 2).reshape(slots * seqs, D, T)
    cT = cotangent.transpose(0, 1, 3, 2).reshape(slots * seqs, D, T)

    piece_in = jnp.pad(to_units(w_in, n, D, F), ((0, 0), (0, rows_in - units_in), (0, 0)))
    piece_rest = jnp.concatenate([to_units(w_conv, n, 3 * F, F), to_units(w_out, n, F, D)], axis=1)
    piece_rest = jnp.pad(piece_rest, ((0, 0), (0, rows_rest - piece_rest.shape[1]), (0, 0)))
    gain0 = wide_gain.reshape(1, D)
    bits = bits_of(n)
    Q = 2
    steps = slots * seqs // Q

    buf_in, buf_rest = piece_in[None], piece_rest[None]
    acts, gain, done, token = (), gain0, 0, None
    far = list(reversed(bits))
    for s, bit in enumerate(far):
        got_in = swap(buf_in, bit, n)
        if s < len(far) - 2:
            got_rest = swap(buf_rest, bit, n)
        count = (steps * (s + 1)) // (len(far) - 1) - done if s < len(far) - 1 else 0
        if count:
            *acts, token = wide_fwd(xT, gain, wide_bias, Q, done, count, acts, token)
            done += count
        buf_in = jnp.concatenate([buf_in, got_in], axis=0)
        if s < len(far) - 2:
            buf_rest = jnp.concatenate([buf_rest, got_rest], axis=0)
        buf_in, buf_rest, token, gain = together(buf_in, buf_rest, token, gain)
    r1, n0, s0, rstd0 = acts
    got_rest = swap(buf_rest, far[-2], n)
    w1, w1t = unpack_in(n, table, buf_in, narrow_bias, token, D, F)
    uT, n1, s1, rstd1, tails = front(r1, w1t, narrow_gain, narrow_bias, Q)
    buf_rest, tails = together(jnp.concatenate([buf_rest, got_rest], axis=0), tails)
    below = lax.ppermute(tails[0], "ctx", up)
    above = lax.ppermute(tails[1], "ctx", down)
    buf_rest = jnp.concatenate([buf_rest, swap(buf_rest, far[-1], n)], axis=0)
    wc, wct, w3, w3t = unpack_rest(n, table, buf_rest, narrow_bias, wide_bias, D, F)
    eT, outT, rest, small, heads = middle(n, Q, flags, uT, below, above, tails, cT, xT, wct, w3, w3t,
                                          narrow_gain, narrow_bias, rows_rest)

    keep, send = split_for(rest, bits[0], me)
    got = swap(send, bits[0], n)
    above = lax.ppermute(heads[0], "ctx", down)
    below = lax.ppermute(heads[1], "ctx", up)
    rest = keep + got.astype(F32)
    keep, send = split_for(rest, bits[1], me)
    send, gain1 = together(send, narrow_gain)
    got = swap(send, bits[1], n)
    e1, into, small = back(n, Q, flags, eT, below, above, heads, n1, s1, rstd1, r1, wc, gain1, small, rows_in)
    keep, small = together(keep, small)
    rest = keep + got.astype(F32)

    rest_bits, in_bits = bits[2:], list(bits)
    dxT, total = None, slots * seqs
    parts = len(rest_bits) + 1
    done, gain = 0, gain0
    for s in range(parts):
        more = s < len(rest_bits)
        keep_i, send_i = split_for(into, in_bits[s], me)
        if more:
            keep_r, send_r = split_for(rest, rest_bits[s], me)
            send_r, send_i, gain = together(send_r, send_i, gain)
            got_r = swap(send_r, rest_bits[s], n)
        else:
            send_i, gain = together(send_i, gain)
        got_i = swap(send_i, in_bits[s], n)
        count = total * (s + 1) // parts - done
        dxT, small = wide_bwd(e1, w1, n0, s0, rstd0, cT, gain, small, done, count, dxT)
        done += count
        if more:
            keep_r, keep_i, small = together(keep_r, keep_i, small)
            rest = keep_r + got_r.astype(F32)
        else:
            keep_i, small = together(keep_i, small)
        into = keep_i + got_i.astype(F32)
    for bit in in_bits[parts:]:
        keep_i, send_i = split_for(into, bit, me)
        into = keep_i + swap(send_i, bit, n).astype(F32)
    own_rest, own_in = rest[0], into[0]

    def owned(own, at, M, C):
        q, parts, units = unit_plan(n, M, C)
        return own[:, at:at + units].transpose(1, 0, 2).reshape(units, WIDE)[:, :q].reshape(-1)

    small = sum_all(small, n)
    back4 = lambda v: v.reshape(slots, seqs, D, T).transpose(0, 1, 3, 2)
    return (back4(outT), back4(dxT), owned(own_in, 0, D, F), owned(own_rest, 0, 3 * F, F), owned(own_rest, units_conv, F, D),
            small[4], jnp.stack([small[5], small[2]]), jnp.stack([small[3, :F], small[0, :F]]),
            jnp.stack([small[1, F:], small[3, F:], small[1, :F], small[0, F:]]))


def solution(mesh):
    whole, flat, copied = P("ctx", None, None, None), P("ctx"), P()
    return jax.shard_map(
        on_device, mesh=mesh,
        in_specs=(whole, whole, flat, flat, flat, copied, copied, copied, copied, copied),
        out_specs=(whole, whole, flat, flat, flat, copied, copied, copied, copied),
        check_vma=False,
    )
```

```python
import functools
import math
import jax
import jax.numpy as jnp
from jax import lax
from jax.experimental import pallas as pl
from jax.experimental.pallas import tpu as pltpu
from jax.sharding import PartitionSpec as P

EPS = 1e-05
BF = jnp.bfloat16
F32 = jnp.float32
L = 128
R = 16
SHIFT = 16
WIDE = 256


def params(mb=52):
    return pltpu.CompilerParams(dimension_semantics=("arbitrary",), vmem_limit_bytes=mb * 1024 * 1024)


def cost(flops, nbytes, trans=0):
    return pl.CostEstimate(flops=int(flops), bytes_accessed=int(nbytes), transcendentals=int(trans))


def rows_at(i):
    return pl.ds(pl.multiple_of(i * R, R), R)


def loop(n, body, init, unroll=25):
    return lax.fori_loop(0, n, body, init, unroll=min(n, unroll))


def fold(v):
    return v[:8] + v[8:]


def total8(v):
    return jnp.sum(v, axis=0, keepdims=True)


def nt(a, b):
    return lax.dot_general(a, b, (((1,), (1,)), ((), ())), preferred_element_type=F32)


def nn(a, b):
    return jnp.dot(a, b, preferred_element_type=F32)


def chunks(N, width):
    return [slice(l, min(N, l + width)) for l in range(0, N, width)]


def spread(table, rows, w):
    return jnp.concatenate([table[rows, :]] * (-(-w // L)), axis=1)[:, :w]


def fill_table(table, row):
    table[...] = jnp.broadcast_to(row, (L, row.shape[1])).T


def col_stats(read, chans, N, unroll=25):
    acc = loop(chans // R, lambda i, a: a + fold(read(i)), jnp.zeros((8, N), F32), unroll)
    mean = total8(acc) * (1.0 / chans)

    def second(i, a):
        cen = read(i) - mean
        return a + fold(cen * cen)

    acc = loop(chans // R, second, jnp.zeros((8, N), F32), unroll)
    return mean, lax.rsqrt(total8(acc) * (1.0 / chans) + EPS)


def gate(h):
    t = jnp.tanh(h)
    r = h + h * t
    return r, (1.0 + t) + (r - r * t)


def lane_sum(acc_ref, rows, v):
    N = v.shape[1]
    full = N // L * L
    tot = v[:, :L]
    for j in range(L, full, L):
        tot = tot + v[:, j:j + L]
    if full < N:
        tot = tot + jnp.concatenate([v[:, full:], jnp.zeros((v.shape[0], L - (N - full)), v.dtype)], axis=1)
    acc_ref[rows, :] += tot


def seq_spec(B, rows, N):
    return pl.BlockSpec((B, rows, N), lambda i: (i, 0, 0))


def fixed(shape):
    zero = (0,) * len(shape)
    return pl.BlockSpec(shape, lambda i: zero)


def smem():
    return pl.BlockSpec(memory_space=pltpu.SMEM)


def vmem():
    return pl.BlockSpec(memory_space=pltpu.VMEM)


def lane_total(acc):
    return jnp.sum(acc.T, axis=0, keepdims=True)


def unit_plan(n, M, C):
    size = M * C // n
    whole = math.gcd(size, C)
    q = max(d for d in range(1, WIDE + 1) if whole % d == 0)
    return q, C // q, size // q


def unit_slices(n, M, C):
    q, parts, units = unit_plan(n, M, C)
    out = []
    for p in range(n):
        for h in range(parts):
            lo = -((h - units * p) // parts)
            hi = -((h - units * (p + 1)) // parts)
            if hi > lo:
                out.append((p, h, lo, hi - lo, lo * parts + h - units * p))
    return out


def strided(start, size, step):
    return pl.ds(start, size, stride=step) if step > 1 else pl.ds(start, size)


def planes(q):
    return [(j, j * L, min(q - j * L, L)) for j in range(-(-q // L))]


def put_matrix(n, mat_ref, f32_ref, off):
    M, C = mat_ref.shape
    q, parts, _ = unit_plan(n, M, C)
    for p, h, lo, cnt, u in unit_slices(n, M, C):
        for j, at, w in planes(q):
            mat_ref[lo:lo + cnt, h * q + at:h * q + at + w] = f32_ref[p, j, strided(off + u, cnt, parts), :][:, :w]


def put_pieces(n, out_ref, mat_ref, M, C, off):
    q, parts, _ = unit_plan(n, M, C)
    for p, h, lo, cnt, u in unit_slices(n, M, C):
        for j, at, w in planes(q):
            v = mat_ref[lo:lo + cnt, h * q + at:h * q + at + w]
            if w < L:
                v = jnp.concatenate([v, jnp.zeros((cnt, L - w), v.dtype)], axis=1)
            out_ref[p, j, strided(off + u, cnt, parts), :] = v


def flipped(mat):
    C = mat.shape[1]
    eye = (lax.broadcasted_iota(jnp.int32, (C, C), 0) == lax.broadcasted_iota(jnp.int32, (C, C), 1)).astype(BF)
    return nt(eye, mat).astype(BF)


def ordered(n, slots_ref, g_ref, f32_ref):
    for p in range(n):
        f32_ref[p] = g_ref[slots_ref[p]].astype(F32)


def bias_block(row):
    v = jnp.broadcast_to(row, (L, row.shape[1])).T[:, :R]
    hi = v.astype(BF)
    rest = v - hi.astype(F32)
    mid = rest.astype(BF)
    low = (rest - mid.astype(F32)).astype(BF)
    col = lax.broadcasted_iota(jnp.int32, v.shape, 1)
    zero = jnp.zeros_like(v)
    return jnp.where(col == 0, hi.astype(F32), jnp.where(col == 1, mid.astype(F32), jnp.where(col == 2, low.astype(F32), zero))).astype(BF)


def unpack_in_kernel(n, slots_ref, g_ref, bias_ref, token_ref, w1_ref, w1t_ref, f32_ref, mat_ref):
    ordered(n, slots_ref, g_ref, f32_ref)
    put_matrix(n, mat_ref, f32_ref, 0)
    D, F = mat_ref.shape
    w1_ref[...] = mat_ref[...].astype(BF)
    w1t_ref[:, :D] = flipped(w1_ref[...])
    w1t_ref[:, D:] = bias_block(bias_ref[0:1, :])


def unpack_in(n, slots, g, bias, token, D, F):
    sd = jax.ShapeDtypeStruct
    return pl.pallas_call(
        functools.partial(unpack_in_kernel, n),
        in_specs=[smem(), vmem(), vmem(), pl.BlockSpec(memory_space=pl.ANY)], out_specs=[vmem(), vmem()],
        out_shape=[sd((D, F), BF), sd((F, D + R), BF)],
        scratch_shapes=[pltpu.VMEM(g.shape, F32), pltpu.VMEM((D, F), F32)],
        compiler_params=pltpu.CompilerParams(vmem_limit_bytes=40 * 1024 * 1024), name="unpack_in",
        cost_estimate=cost(1e9, 6e6),
    )(slots, g, bias, token)


def unpack_rest_kernel(n, slots_ref, g_ref, bias_ref, wide_ref, wc_ref, wct_ref, w3_ref, w3t_ref, f32_ref, matc_ref, mat3_ref):
    F, D = mat3_ref.shape
    ordered(n, slots_ref, g_ref, f32_ref)
    put_matrix(n, matc_ref, f32_ref, 0)
    put_matrix(n, mat3_ref, f32_ref, unit_plan(n, 3 * F, F)[2])
    for k in range(3):
        tap = matc_ref[k * F:(k + 1) * F, :].astype(BF)
        wc_ref[:, k * F:(k + 1) * F] = tap
        wct_ref[:, k * F:(k + 1) * F] = flipped(tap)
    wct_ref[:, 3 * F:] = bias_block(bias_ref[2:3, :])
    w3_ref[...] = mat3_ref[...].astype(BF)
    w3t_ref[:, :F] = flipped(w3_ref[...])
    w3t_ref[:, F:] = bias_block(wide_ref[1:2, :])


def unpack_rest(n, slots, g, bias, wide_bias, D, F):
    sd = jax.ShapeDtypeStruct
    return pl.pallas_call(
        functools.partial(unpack_rest_kernel, n),
        in_specs=[smem()] + [vmem()] * 3, out_specs=[vmem()] * 4,
        out_shape=[sd((F, 3 * F), BF), sd((F, 3 * F + R), BF), sd((F, D), BF), sd((D, F + R), BF)],
        scratch_shapes=[pltpu.VMEM(g.shape, F32), pltpu.VMEM((3 * F, F), F32), pltpu.VMEM((F, D), F32)],
        compiler_params=pltpu.CompilerParams(vmem_limit_bytes=40 * 1024 * 1024), name="unpack_rest",
        cost_estimate=cost(2e9, 14e6),
    )(slots, g, bias, wide_bias)


def rim_store(ref, i, steps, cols):
    for s in range(2 * steps):
        @pl.when(i == s)
        def _(s=s):
            w = cols[0].shape[1]
            for q, v in enumerate(cols):
                at = (s % steps * len(cols) + q) * w
                ref[s // steps, :, at:at + w] = v


def rim_load(buf, i, steps, first, second):
    w = buf.shape[1]
    for s in range(2 * steps):
        @pl.when(i == s)
        def _(s=s):
            src = first() if s < steps else second()
            buf[...] = src[:, s % steps * w:(s % steps + 1) * w]


def wide_fwd_kernel(Q, start, x_ref, gain_ref, bias_ref, *refs):
    r1_ref, n0_ref, s0_ref, rstd_ref, token_ref, gtab, btab, rbuf = refs[-8:]
    D, N = x_ref.shape[1:]
    i = pl.program_id(0)

    @pl.when(i == 0)
    def _():
        fill_table(gtab, gain_ref[...] * 0.5)
        fill_table(btab, bias_ref[0:1, :] * 0.5)
        token_ref[...] = jnp.zeros_like(token_ref)

    read = lambda j: x_ref[0, rows_at(j), :].astype(F32)
    mean, rstd = col_stats(read, D, N, 10)
    rstd_ref[0] = rstd

    def act(j, _):
        rows = rows_at(j)
        n = (read(j) - mean) * rstd
        r, d = gate(n * spread(gtab, rows, N) + spread(btab, rows, N))
        n0_ref[0, rows, :] = n.astype(BF)
        s0_ref[0, rows, :] = d.astype(BF)
        rbuf[rows, :] = r.astype(BF)
        return 0

    loop(D // R, act, 0, 10)
    for q in range(Q):
        @pl.when(lax.rem(start + i, Q) == q)
        def _(q=q):
            r1_ref[0, :D, q * N:(q + 1) * N] = rbuf[...]
            r1_ref[0, D:, q * N:(q + 1) * N] = jnp.ones((r1_ref.shape[1] - D, N), BF)


def wide_fwd(xT, gain, bias, Q, start=0, steps=None, into=None, token=None):
    S, D, N = xT.shape
    steps = S if steps is None else steps
    sd = jax.ShapeDtypeStruct
    at = lambda i: (start + i, 0, 0)
    into = tuple(into or ())
    token = () if token is None else (token,)
    one = lambda rows: pl.BlockSpec((1, rows, N), at)
    return pl.pallas_call(
        functools.partial(wide_fwd_kernel, Q, start), grid=(steps,),
        in_specs=[one(D), fixed((1, D)), fixed((2, D))] + [pl.BlockSpec(memory_space=pl.ANY)] * len(into + token),
        out_specs=[pl.BlockSpec((1, D + R, Q * N), lambda i: ((start + i) // Q, 0, 0)), one(D), one(D), one(1), fixed((8, L))],
        out_shape=[sd((S // Q, D + R, Q * N), BF), sd((S, D, N), BF), sd((S, D, N), BF), sd((S, 1, N), F32), sd((8, L), F32)],
        scratch_shapes=[pltpu.VMEM((D, L), F32)] * 2 + [pltpu.VMEM((D, N), BF)],
        input_output_aliases={3 + j: j for j in range(len(into))},
        compiler_params=params(), name="wide_fwd", cost_estimate=cost(1e9 * steps, 5.5e6 * steps),
    )(xT, gain, bias, *into, *token)


CH = 384


def front_kernel(Q, steps, r1_ref, w1t_ref, gain_ref, bias_ref, u_ref, n_ref, s_ref, rstd_ref, tail_ref, h_ref, gtab, btab):
    F, N = h_ref.shape
    T = N // Q
    i = pl.program_id(0)

    @pl.when(i == 0)
    def _():
        fill_table(gtab, gain_ref[0:1, :] * 0.5)
        fill_table(btab, bias_ref[1:2, :] * 0.5)

    h_ref[...] = nn(w1t_ref[...], r1_ref[0])
    for ls in chunks(N, CH):
        W = ls.stop - ls.start
        read = lambda j: h_ref[rows_at(j), ls]
        mean, rstd = col_stats(read, F, W)
        rstd_ref[0, :, ls] = rstd

        def act(j, _):
            rows = rows_at(j)
            n = (read(j) - mean) * rstd
            r, d = gate(n * spread(gtab, rows, W) + spread(btab, rows, W))
            u_ref[0, rows, ls] = r.astype(BF)
            n_ref[0, rows, ls] = n.astype(BF)
            s_ref[0, rows, ls] = d.astype(BF)
            return 0

        loop(F // R, act, 0)
    rim_store(tail_ref, i, steps, [u_ref[0, :, (q + 1) * T - 2 * SHIFT:(q + 1) * T] for q in range(Q)])


def front(r1, w1t, gain, bias, Q):
    G, DE, N = r1.shape
    F = w1t.shape[0]
    sd = jax.ShapeDtypeStruct
    rim = (2, F, G // 2 * Q * 2 * SHIFT)
    return pl.pallas_call(
        functools.partial(front_kernel, Q, G // 2), grid=(G,),
        in_specs=[seq_spec(1, DE, N), fixed(w1t.shape), fixed(gain.shape), fixed(bias.shape)],
        out_specs=[seq_spec(1, F, N)] * 3 + [seq_spec(1, 1, N), fixed(rim)],
        out_shape=[sd((G, F, N), BF)] * 3 + [sd((G, 1, N), F32), sd(rim, BF)],
        scratch_shapes=[pltpu.VMEM((F, N), F32)] + [pltpu.VMEM((F, L), F32)] * 2,
        compiler_params=params(), name="front", cost_estimate=cost(4e9, 19e6),
    )(r1, w1t, gain, bias)


def pull(F, W, ls, d_ref, n_at, s_at, rstd, gtab, gacc, bacc, e_ref, unroll=25):
    def first(j, carry):
        m1, m2 = carry
        rows = rows_at(j)
        ds = d_ref[rows, ls] * s_at(rows).astype(F32)
        dn = ds * n_at(rows).astype(F32)
        gain = spread(gtab, rows, W)
        t = ds * gain
        d_ref[rows, ls] = t
        lane_sum(bacc, rows, ds)
        lane_sum(gacc, rows, dn)
        return m1 + fold(t), m2 + fold(dn * gain)

    zero = jnp.zeros((8, W), F32)
    m1, m2 = loop(F // R, first, (zero, zero), unroll)
    m1, m2 = total8(m1) * (1.0 / F) * rstd, total8(m2) * (1.0 / F) * rstd

    def second(j, _):
        rows = rows_at(j)
        e_ref[0, rows, ls] = ((d_ref[rows, ls] * rstd - m1) - n_at(rows).astype(F32) * m2).astype(BF)
        return 0

    loop(F // R, second, 0, unroll)


def middle_kernel(n, Q, steps, flags_ref, u_ref, below_ref, above_ref, tail_ref, c_ref, x_ref, wct_ref, w3_ref, w3t_ref,
                  gain_ref, bias_ref, e_ref, out_ref, pieces_ref, small_ref, head_ref,
                  ubuf, cbuf, rbuf, h_ref, d_ref, n_ref, s_ref, o_ref, gacc, bacc, gwo_ref, gwc_ref, hbuf, gtab, btab):
    F, N = h_ref.shape
    T = N // Q
    D = c_ref.shape[1]
    i = pl.program_id(0)

    @pl.when(i == 0)
    def _():
        fill_table(gtab, gain_ref[1:2, :] * 0.5)
        fill_table(btab, bias_ref[3:4, :] * 0.5)
        ubuf[3 * F:, :] = jnp.ones((R, N), BF)
        rbuf[F:, :] = jnp.ones((R, N), BF)
        gwo_ref[...] = jnp.zeros_like(gwo_ref)
        gwc_ref[...] = jnp.zeros_like(gwc_ref)
        gacc[...] = jnp.zeros_like(gacc)
        bacc[...] = jnp.zeros_like(bacc)

    rim_load(hbuf, i, steps,
             lambda: jnp.where(flags_ref[0] == 1, jnp.zeros_like(below_ref[...]), below_ref[...]),
             lambda: jnp.where(flags_ref[1] == 1, tail_ref[0], above_ref[...]))
    ubuf[:F, :] = u_ref[0]
    for k in (1, 2):
        w = k * SHIFT
        parts = []
        for q in range(Q):
            parts += [hbuf[:, (q + 1) * 2 * SHIFT - w:(q + 1) * 2 * SHIFT], u_ref[0, :, q * T:(q + 1) * T - w]]
        ubuf[k * F:(k + 1) * F, :] = jnp.concatenate(parts, axis=1)
    for q in range(Q):
        cbuf[:, q * T:(q + 1) * T] = c_ref[q]
    h_ref[...] = nn(wct_ref[...], ubuf[...])
    d_ref[...] = nn(w3_ref[...], cbuf[...])
    rstds = []
    for ls in chunks(N, CH):
        W = ls.stop - ls.start
        read = lambda j: h_ref[rows_at(j), ls]
        mean, rstd = col_stats(read, F, W)
        rstds.append(rstd)

        def act(j, _):
            rows = rows_at(j)
            v = (read(j) - mean) * rstd
            r, d = gate(v * spread(gtab, rows, W) + spread(btab, rows, W))
            rbuf[rows, ls] = r.astype(BF)
            n_ref[rows, ls] = v
            s_ref[rows, ls] = d
            return 0

        loop(F // R, act, 0)
    o_ref[...] = nn(w3t_ref[...], rbuf[...])
    gwo_ref[...] += nt(rbuf[...], cbuf[...])
    for ls, rstd in zip(chunks(N, CH), rstds):
        pull(F, ls.stop - ls.start, ls, d_ref, lambda rows: n_ref[rows, ls], lambda rows: s_ref[rows, ls], rstd, gtab, gacc, bacc, e_ref)
    gwc_ref[...] += nt(ubuf[...], e_ref[0])
    for q in range(Q):
        def emit(j, _):
            rows = rows_at(j)
            out_ref[q, rows, :] = (o_ref[rows, q * T:(q + 1) * T] + x_ref[q, rows, :].astype(F32)).astype(BF)
            return 0

        loop(D // R, emit, 0, 50)
    rim_store(head_ref, i, steps, [e_ref[0, :, q * T:q * T + 2 * SHIFT] for q in range(Q)])

    @pl.when(i == pl.num_programs(0) - 1)
    def _():
        small_ref[...] = jnp.zeros_like(small_ref)
        small_ref[0:1, :F] = lane_total(gacc[...]) * 0.5
        small_ref[0:1, F:] = lane_total(bacc[...]) * 0.5
        small_ref[1:2, :F] = gwc_ref[3 * F:3 * F + 1, :]
        small_ref[2:3, :] = gwo_ref[F:F + 1, :]
        put_pieces(n, pieces_ref, gwc_ref, 3 * F, F, 0)
        put_pieces(n, pieces_ref, gwo_ref, F, D, unit_plan(n, 3 * F, F)[2])


def middle(n, Q, flags, uT, below, above, tails, cT, xT, wct, w3, w3t, gain, bias, rows):
    G, F, N = uT.shape
    S, D, T = cT.shape
    sd = jax.ShapeDtypeStruct
    return pl.pallas_call(
        functools.partial(middle_kernel, n, Q, G // 2), grid=(G,),
        in_specs=[smem(), seq_spec(1, F, N), fixed(below.shape), fixed(above.shape), fixed(tails.shape), seq_spec(Q, D, T), seq_spec(Q, D, T),
                  fixed(wct.shape), fixed(w3.shape), fixed(w3t.shape), fixed(gain.shape), fixed(bias.shape)],
        out_specs=[seq_spec(1, F, N), seq_spec(Q, D, T), fixed((n, WIDE // L, rows, L)), fixed((8, D)), fixed(tails.shape)],
        out_shape=[sd((G, F, N), BF), sd((S, D, T), BF), sd((n, WIDE // L, rows, L), F32), sd((8, D), F32), sd(tails.shape, BF)],
        scratch_shapes=[pltpu.VMEM((3 * F + R, N), BF), pltpu.VMEM((D, N), BF), pltpu.VMEM((F + R, N), BF), pltpu.VMEM((F, N), F32),
                        pltpu.VMEM((F, N), F32), pltpu.VMEM((F, N), F32), pltpu.VMEM((F, N), F32), pltpu.VMEM((D, N), F32),
                        pltpu.VMEM((F, L), F32), pltpu.VMEM((F, L), F32), pltpu.VMEM((F + R, D), F32),
                        pltpu.VMEM((3 * F + R, F), F32), pltpu.VMEM((F, Q * 2 * SHIFT), BF), pltpu.VMEM((F, L), F32), pltpu.VMEM((F, L), F32)],
        compiler_params=params(), name="middle", cost_estimate=cost(18e9, 36e6),
    )(flags, uT, below, above, tails, cT, xT, wct, w3, w3t, gain, bias)


def tail_kernel(n, Q, steps, flags_ref, e_ref, below_ref, above_ref, head_ref, n_ref, s_ref, rstd_ref, r1_ref, wc_ref, gain_ref,
                n0_ref, s0_ref, rstd0_ref, c_ref, w1_ref, gain0_ref, small_in,
                dx_ref, pieces_ref, small_ref,
                ebuf, d_ref, gacc, bacc, gwi_ref, hbuf, gtab, e1new, e1old, gtab0, gacc0, bacc0, *d0_refs):
    F, N = d_ref.shape
    T = N // Q
    D = gwi_ref.shape[0] - R
    i = pl.program_id(0)
    last = pl.num_programs(0) - 1

    @pl.when(i == 0)
    def _():
        fill_table(gtab, gain_ref[0:1, :] * 0.5)
        fill_table(gtab0, gain0_ref[...] * 0.5)
        for ref in (gwi_ref, gacc, bacc, gacc0, bacc0):
            ref[...] = jnp.zeros_like(ref)

    def narrow_shift():
        ebuf[:F, :] = e_ref[0]
        for k in (1, 2):
            w = k * SHIFT
            parts = []
            for q in range(Q):
                parts += [e_ref[0, :, q * T + w:(q + 1) * T], hbuf[:, q * 2 * SHIFT:q * 2 * SHIFT + w]]
            ebuf[k * F:(k + 1) * F, :] = jnp.concatenate(parts, axis=1)
        d_ref[...] = nn(wc_ref[...], ebuf[...])

    def narrow_pull(unroll):
        for ls in chunks(N, CH):
            pull(F, ls.stop - ls.start, ls, d_ref, lambda rows: n_ref[0, rows, ls], lambda rows: s_ref[0, rows, ls], rstd_ref[0, :, ls],
                 gtab, gacc, bacc, e1new, unroll)

    def narrow_sum():
        gwi_ref[...] += nt(r1_ref[0], e1new[0])

    def wide_dot(q):
        d0_refs[q][...] = nn(w1_ref[...], e1old[0, :, q * T:(q + 1) * T])

    def wide_pull(q, unroll):
        d0 = d0_refs[q]

        def first(j, carry):
            m1, m2 = carry
            rows = rows_at(j)
            ds = d0[rows, :] * s0_ref[q, rows, :].astype(F32)
            dn = ds * n0_ref[q, rows, :].astype(F32)
            gain = spread(gtab0, rows, T)
            t = ds * gain
            d0[rows, :] = t
            lane_sum(bacc0, rows, ds)
            lane_sum(gacc0, rows, dn)
            return m1 + fold(t), m2 + fold(dn * gain)

        zero = jnp.zeros((8, T), F32)
        m1, m2 = loop(D // R, first, (zero, zero), unroll)
        rstd = rstd0_ref[q]
        m1, m2 = total8(m1) * (1.0 / D) * rstd, total8(m2) * (1.0 / D) * rstd

        def second(j, _):
            rows = rows_at(j)
            g = (d0[rows, :] * rstd - m1) - n0_ref[q, rows, :].astype(F32) * m2
            dx_ref[q, rows, :] = (g + c_ref[q, rows, :].astype(F32)).astype(BF)
            return 0

        loop(D // R, second, 0, unroll)

    rim_load(hbuf, jnp.minimum(i, last - 1), steps,
             lambda: jnp.where(flags_ref[1] == 1, head_ref[1], above_ref[...]),
             lambda: jnp.where(flags_ref[0] == 1, jnp.zeros_like(below_ref[...]), below_ref[...]))

    @pl.when(i == 0)
    def _():
        narrow_shift()
        narrow_pull(5)
        narrow_sum()

    @pl.when((i > 0) & (i < last))
    def _():
        wide_dot(0)
        narrow_shift()
        wide_pull(0, 50)
        wide_dot(1)
        narrow_pull(25)
        narrow_sum()
        wide_pull(1, 50)

    @pl.when(i == last)
    def _():
        for q in range(Q):
            wide_dot(q)
            wide_pull(q, 5)
        small_ref[...] = small_in[...]
        small_ref[1:2, F:] = gwi_ref[D:D + 1, :]
        small_ref[3:4, :F] = lane_total(gacc[...]) * 0.5
        small_ref[3:4, F:] = lane_total(bacc[...]) * 0.5
        small_ref[4:5, :] = lane_total(gacc0[...]) * 0.5
        small_ref[5:6, :] = lane_total(bacc0[...]) * 0.5
        put_pieces(n, pieces_ref, gwi_ref, D, F, 0)

    e1old[...] = e1new[...]


def tail(n, Q, flags, eT, below, above, heads, n1, s1, rstd1, r1, wc, gain, n0, s0, rstd0, cT, w1, gain0, small, rows):
    G, F, N = eT.shape
    DE = r1.shape[1]
    S, D, T = cT.shape
    sd = jax.ShapeDtypeStruct
    now = lambda i: (jnp.minimum(i, G - 1), 0, 0)
    then = lambda i: (jnp.maximum(i - 1, 0), 0, 0)
    narrow = lambda rows: pl.BlockSpec((1, rows, N), now)
    wide = lambda rows: pl.BlockSpec((Q, rows, T), then)
    return pl.pallas_call(
        functools.partial(tail_kernel, n, Q, G // 2), grid=(G + 1,),
        in_specs=[smem(), narrow(F), fixed(below.shape), fixed(above.shape), fixed(heads.shape), narrow(F), narrow(F),
                  narrow(1), narrow(DE), fixed(wc.shape), fixed(gain.shape), wide(D), wide(D), wide(1), wide(D),
                  fixed(w1.shape), fixed(gain0.shape), fixed(small.shape)],
        out_specs=[wide(D), fixed((n, WIDE // L, rows, L)), fixed(small.shape)],
        out_shape=[sd((S, D, T), BF), sd((n, WIDE // L, rows, L), F32), sd(small.shape, F32)],
        scratch_shapes=[pltpu.VMEM((3 * F, N), BF), pltpu.VMEM((F, N), F32), pltpu.VMEM((F, L), F32), pltpu.VMEM((F, L), F32),
                        pltpu.VMEM((DE, F), F32), pltpu.VMEM((F, Q * 2 * SHIFT), BF), pltpu.VMEM((F, L), F32),
                        pltpu.VMEM((1, F, N), BF), pltpu.VMEM((1, F, N), BF)] + [pltpu.VMEM((D, L), F32)] * 3 + [pltpu.VMEM((D, T), F32)] * Q,
        compiler_params=params(56), name="tail", cost_estimate=cost(12e9, 60e6),
    )(flags, eT, below, above, heads, n1, s1, rstd1, r1, wc, gain, n0, s0, rstd0, cT, w1, gain0, small)


def swap(v, bit, n):
    return lax.ppermute(v, "ctx", [(i, i ^ bit) for i in range(n)])


def bits_of(n):
    out, b = [], 1
    while b < n:
        out.append(b)
        b *= 2
    return out


def together(*values):
    return lax.optimization_barrier(values)


def slot_table(n, me):
    diff = jnp.arange(n, dtype=jnp.int32) ^ me
    return sum((jnp.where((diff & bit) != 0, n // 2 // bit, 0) for bit in bits_of(n)), jnp.zeros_like(diff))


def split_for(full, bit, me):
    pairs = full.reshape((-1, 2) + full.shape[1:])
    mine = jnp.where((me & bit) == 0, 0, 1)
    keep = lax.dynamic_index_in_dim(pairs, mine, 1, keepdims=False)
    return keep, lax.dynamic_index_in_dim(pairs, 1 - mine, 1, keepdims=False).astype(BF)


def sum_all(v, n):
    for bit in bits_of(n):
        v = v + swap(v, bit, n)
    return v


def to_units(flat, n, M, C, rows=None):
    q, parts, units = unit_plan(n, M, C)
    return jnp.pad(flat.reshape(units, q), ((0, 0), (0, WIDE - q))).reshape(units, WIDE // L, L).transpose(1, 0, 2)


def round_up(v, m=8):
    return -(-v // m) * m


def on_device(block_input, cotangent, w_in, w_conv, w_out, wide_gain, wide_bias, narrow_gain, narrow_bias, dealing):
    slots, seqs, T, D = block_input.shape
    F = narrow_gain.shape[1]
    n = lax.axis_size("ctx")
    half = dealing.shape[0] // 2
    me = lax.axis_index("ctx")
    pair = jnp.sum(jnp.where(dealing[:half] == me, jnp.arange(half, dtype=jnp.int32), 0))
    flags = jnp.stack([pair == 0, pair == half - 1]).astype(jnp.int32)
    up = [(i, (i + 1) % n) for i in range(n)]
    down = [((i + 1) % n, i) for i in range(n)]
    table = slot_table(n, me)
    units_in, units_conv, units_out = (unit_plan(n, m, c)[2] for m, c in ((D, F), (3 * F, F), (F, D)))
    rows_in, rows_rest = round_up(units_in), round_up(units_conv + units_out)

    xT = block_input.transpose(0, 1, 3, 2).reshape(slots * seqs, D, T)
    cT = cotangent.transpose(0, 1, 3, 2).reshape(slots * seqs, D, T)

    piece_in = jnp.pad(to_units(w_in, n, D, F), ((0, 0), (0, rows_in - units_in), (0, 0)))
    piece_rest = jnp.concatenate([to_units(w_conv, n, 3 * F, F), to_units(w_out, n, F, D)], axis=1)
    piece_rest = jnp.pad(piece_rest, ((0, 0), (0, rows_rest - piece_rest.shape[1]), (0, 0)))
    gain0 = wide_gain.reshape(1, D)
    bits = bits_of(n)
    Q = 2
    steps = slots * seqs // Q

    buf_in, buf_rest = piece_in[None], piece_rest[None]
    acts, gain, done, token = (), gain0, 0, None
    far = list(reversed(bits))
    for s, bit in enumerate(far):
        got_in = swap(buf_in, bit, n)
        if s < len(far) - 2:
            got_rest = swap(buf_rest, bit, n)
        count = (steps * (s + 1)) // (len(far) - 1) * Q - done if s < len(far) - 1 else 0
        if count:
            *acts, token = wide_fwd(xT, gain, wide_bias, Q, done, count, acts, token)
            done += count
        buf_in = jnp.concatenate([buf_in, got_in], axis=0)
        if s < len(far) - 2:
            buf_rest = jnp.concatenate([buf_rest, got_rest], axis=0)
        buf_in, buf_rest, token, gain = together(buf_in, buf_rest, token, gain)
    r1, n0, s0, rstd0 = acts
    got_rest = swap(buf_rest, far[-2], n)
    w1, w1t = unpack_in(n, table, buf_in, narrow_bias, token, D, F)
    uT, n1, s1, rstd1, tails = front(r1, w1t, narrow_gain, narrow_bias, Q)
    buf_rest, tails = together(jnp.concatenate([buf_rest, got_rest], axis=0), tails)
    below = lax.ppermute(tails[0], "ctx", up)
    above = lax.ppermute(tails[1], "ctx", down)
    buf_rest = jnp.concatenate([buf_rest, swap(buf_rest, far[-1], n)], axis=0)
    wc, wct, w3, w3t = unpack_rest(n, table, buf_rest, narrow_bias, wide_bias, D, F)
    eT, outT, rest, small, heads = middle(n, Q, flags, uT, below, above, tails, cT, xT, wct, w3, w3t,
                                          narrow_gain, narrow_bias, rows_rest)

    keep, send = split_for(rest, bits[0], me)
    got = swap(send, bits[0], n)
    above = lax.ppermute(heads[0], "ctx", down)
    below = lax.ppermute(heads[1], "ctx", up)
    rest = keep + got.astype(F32)
    keep, send = split_for(rest, bits[1], me)
    send, gain1 = together(send, narrow_gain)
    got = swap(send, bits[1], n)
    dxT, into, small = tail(n, Q, flags, eT, below, above, heads, n1, s1, rstd1, r1, wc, gain1, n0, s0, rstd0, cT, w1, gain0, small, rows_in)
    rest, small = together(keep + got.astype(F32), small)
    for j, bit in enumerate(bits):
        if j == 2:
            into = jnp.concatenate([into, rest], axis=2)
        keep, send = split_for(into, bit, me)
        send, small = together(send, small)
        small_got, got = swap(small, bit, n), swap(send, bit, n)
        small = small + small_got
        into, small = together(keep + got.astype(F32), small)
    own_in, own_rest = into[0, :, :rows_in], into[0, :, rows_in:]

    def owned(own, at, M, C):
        q, parts, units = unit_plan(n, M, C)
        return own[:, at:at + units].transpose(1, 0, 2).reshape(units, WIDE)[:, :q].reshape(-1)

    back4 = lambda v: v.reshape(slots, seqs, D, T).transpose(0, 1, 3, 2)
    return (back4(outT), back4(dxT), owned(own_in, 0, D, F), owned(own_rest, 0, 3 * F, F), owned(own_rest, units_conv, F, D),
            small[4], jnp.stack([small[5], small[2]]), jnp.stack([small[3, :F], small[0, :F]]),
            jnp.stack([small[1, F:], small[3, F:], small[1, :F], small[0, F:]]))


def solution(mesh):
    whole, flat, copied = P("ctx", None, None, None), P("ctx"), P()
    return jax.shard_map(
        on_device, mesh=mesh,
        in_specs=(whole, whole, flat, flat, flat, copied, copied, copied, copied, copied),
        out_specs=(whole, whole, flat, flat, flat, copied, copied, copied, copied),
        check_vma=False,
    )
```

```python
import functools
import math
import jax
import jax.numpy as jnp
from jax import lax
from jax.experimental import pallas as pl
from jax.experimental.pallas import tpu as pltpu
from jax.sharding import PartitionSpec as P

EPS = 1e-05
BF = jnp.bfloat16
F32 = jnp.float32
L = 128
R = 16
SHIFT = 16
WIDE = 256


def params(mb=52):
    return pltpu.CompilerParams(dimension_semantics=("arbitrary",), vmem_limit_bytes=mb * 1024 * 1024)


def cost(flops, nbytes, trans=0):
    return pl.CostEstimate(flops=int(flops), bytes_accessed=int(nbytes), transcendentals=int(trans))


def rows_at(i):
    return pl.ds(pl.multiple_of(i * R, R), R)


def loop(n, body, init, unroll=25):
    return lax.fori_loop(0, n, body, init, unroll=min(n, unroll))


def fold(v):
    return v[:8] + v[8:]


def total8(v):
    return jnp.sum(v, axis=0, keepdims=True)


def nt(a, b):
    return lax.dot_general(a, b, (((1,), (1,)), ((), ())), preferred_element_type=F32)


def nn(a, b):
    return jnp.dot(a, b, preferred_element_type=F32)


def chunks(N, width):
    return [slice(l, min(N, l + width)) for l in range(0, N, width)]


def spread(table, rows, w):
    return jnp.concatenate([table[rows, :]] * (-(-w // L)), axis=1)[:, :w]


def fill_table(table, row):
    table[...] = jnp.broadcast_to(row, (L, row.shape[1])).T


def col_stats(read, chans, N, unroll=25):
    acc = loop(chans // R, lambda i, a: a + fold(read(i)), jnp.zeros((8, N), F32), unroll)
    mean = total8(acc) * (1.0 / chans)

    def second(i, a):
        cen = read(i) - mean
        return a + fold(cen * cen)

    acc = loop(chans // R, second, jnp.zeros((8, N), F32), unroll)
    return mean, lax.rsqrt(total8(acc) * (1.0 / chans) + EPS)


def gate(h):
    t = jnp.tanh(h)
    r = h + h * t
    return r, (1.0 + t) + (r - r * t)


def lane_sum(acc_ref, rows, v):
    N = v.shape[1]
    full = N // L * L
    tot = v[:, :L]
    for j in range(L, full, L):
        tot = tot + v[:, j:j + L]
    if full < N:
        tot = tot + jnp.concatenate([v[:, full:], jnp.zeros((v.shape[0], L - (N - full)), v.dtype)], axis=1)
    acc_ref[rows, :] += tot


def seq_spec(B, rows, N):
    return pl.BlockSpec((B, rows, N), lambda i: (i, 0, 0))


def fixed(shape):
    zero = (0,) * len(shape)
    return pl.BlockSpec(shape, lambda i: zero)


def smem():
    return pl.BlockSpec(memory_space=pltpu.SMEM)


def vmem():
    return pl.BlockSpec(memory_space=pltpu.VMEM)


def lane_total(acc):
    return jnp.sum(acc.T, axis=0, keepdims=True)


def unit_plan(n, M, C):
    size = M * C // n
    whole = math.gcd(size, C)
    q = max(d for d in range(1, WIDE + 1) if whole % d == 0)
    return q, C // q, size // q


def unit_slices(n, M, C):
    q, parts, units = unit_plan(n, M, C)
    out = []
    for p in range(n):
        for h in range(parts):
            lo = -((h - units * p) // parts)
            hi = -((h - units * (p + 1)) // parts)
            if hi > lo:
                out.append((p, h, lo, hi - lo, lo * parts + h - units * p))
    return out


def strided(start, size, step):
    return pl.ds(start, size, stride=step) if step > 1 else pl.ds(start, size)


def planes(q):
    return [(j, j * L, min(q - j * L, L)) for j in range(-(-q // L))]


def put_matrix(n, mat_ref, f32_ref, off):
    M, C = mat_ref.shape
    q, parts, _ = unit_plan(n, M, C)
    for p, h, lo, cnt, u in unit_slices(n, M, C):
        for j, at, w in planes(q):
            mat_ref[lo:lo + cnt, h * q + at:h * q + at + w] = f32_ref[p, j, strided(off + u, cnt, parts), :][:, :w]


def put_pieces(n, out_ref, mat_ref, M, C, off):
    q, parts, _ = unit_plan(n, M, C)
    for p, h, lo, cnt, u in unit_slices(n, M, C):
        for j, at, w in planes(q):
            v = mat_ref[lo:lo + cnt, h * q + at:h * q + at + w]
            if w < L:
                v = jnp.concatenate([v, jnp.zeros((cnt, L - w), v.dtype)], axis=1)
            out_ref[p, j, strided(off + u, cnt, parts), :] = v


def flipped(mat):
    C = mat.shape[1]
    eye = (lax.broadcasted_iota(jnp.int32, (C, C), 0) == lax.broadcasted_iota(jnp.int32, (C, C), 1)).astype(BF)
    return nt(eye, mat).astype(BF)


def ordered(n, slots_ref, g_ref, f32_ref):
    for p in range(n):
        f32_ref[p] = g_ref[slots_ref[p]].astype(F32)


def bias_block(row):
    v = jnp.broadcast_to(row, (L, row.shape[1])).T[:, :R]
    hi = v.astype(BF)
    rest = v - hi.astype(F32)
    mid = rest.astype(BF)
    low = (rest - mid.astype(F32)).astype(BF)
    col = lax.broadcasted_iota(jnp.int32, v.shape, 1)
    zero = jnp.zeros_like(v)
    return jnp.where(col == 0, hi.astype(F32), jnp.where(col == 1, mid.astype(F32), jnp.where(col == 2, low.astype(F32), zero))).astype(BF)


def unpack_in_kernel(n, slots_ref, g_ref, bias_ref, token_ref, w1_ref, w1t_ref, f32_ref, mat_ref):
    ordered(n, slots_ref, g_ref, f32_ref)
    put_matrix(n, mat_ref, f32_ref, 0)
    D, F = mat_ref.shape
    w1_ref[...] = mat_ref[...].astype(BF)
    w1t_ref[:, :D] = flipped(w1_ref[...])
    w1t_ref[:, D:] = bias_block(bias_ref[0:1, :])


def unpack_in(n, slots, g, bias, token, D, F):
    sd = jax.ShapeDtypeStruct
    return pl.pallas_call(
        functools.partial(unpack_in_kernel, n),
        in_specs=[smem(), vmem(), vmem(), pl.BlockSpec(memory_space=pl.ANY)], out_specs=[vmem(), vmem()],
        out_shape=[sd((D, F), BF), sd((F, D + R), BF)],
        scratch_shapes=[pltpu.VMEM(g.shape, F32), pltpu.VMEM((D, F), F32)],
        compiler_params=pltpu.CompilerParams(vmem_limit_bytes=40 * 1024 * 1024), name="unpack_in",
        cost_estimate=cost(1e9, 6e6),
    )(slots, g, bias, token)


def unpack_rest_kernel(n, slots_ref, g_ref, bias_ref, wide_ref, wc_ref, wct_ref, w3_ref, w3t_ref, f32_ref, matc_ref, mat3_ref):
    F, D = mat3_ref.shape
    ordered(n, slots_ref, g_ref, f32_ref)
    put_matrix(n, matc_ref, f32_ref, 0)
    put_matrix(n, mat3_ref, f32_ref, unit_plan(n, 3 * F, F)[2])
    for k in range(3):
        tap = matc_ref[k * F:(k + 1) * F, :].astype(BF)
        wc_ref[:, k * F:(k + 1) * F] = tap
        wct_ref[:, k * F:(k + 1) * F] = flipped(tap)
    wct_ref[:, 3 * F:] = bias_block(bias_ref[2:3, :])
    w3_ref[...] = mat3_ref[...].astype(BF)
    w3t_ref[:, :F] = flipped(w3_ref[...])
    w3t_ref[:, F:] = bias_block(wide_ref[1:2, :])


def unpack_rest(n, slots, g, bias, wide_bias, D, F):
    sd = jax.ShapeDtypeStruct
    return pl.pallas_call(
        functools.partial(unpack_rest_kernel, n),
        in_specs=[smem()] + [vmem()] * 3, out_specs=[vmem()] * 4,
        out_shape=[sd((F, 3 * F), BF), sd((F, 3 * F + R), BF), sd((F, D), BF), sd((D, F + R), BF)],
        scratch_shapes=[pltpu.VMEM(g.shape, F32), pltpu.VMEM((3 * F, F), F32), pltpu.VMEM((F, D), F32)],
        compiler_params=pltpu.CompilerParams(vmem_limit_bytes=40 * 1024 * 1024), name="unpack_rest",
        cost_estimate=cost(2e9, 14e6),
    )(slots, g, bias, wide_bias)


def rim_store(ref, i, steps, cols):
    for s in range(2 * steps):
        @pl.when(i == s)
        def _(s=s):
            w = cols[0].shape[1]
            for q, v in enumerate(cols):
                at = (s % steps * len(cols) + q) * w
                ref[s // steps, :, at:at + w] = v


def rim_load(buf, i, steps, first, second):
    w = buf.shape[1]
    for s in range(2 * steps):
        @pl.when(i == s)
        def _(s=s):
            src = first() if s < steps else second()
            buf[...] = src[:, s % steps * w:(s % steps + 1) * w]


def wide_fwd_kernel(Q, start, x_ref, gain_ref, bias_ref, *refs):
    r1_ref, n0_ref, s0_ref, rstd_ref, token_ref, gtab, btab, rbuf = refs[-8:]
    D, N = x_ref.shape[1:]
    i = pl.program_id(0)

    @pl.when(i == 0)
    def _():
        fill_table(gtab, gain_ref[...] * 0.5)
        fill_table(btab, bias_ref[0:1, :] * 0.5)
        token_ref[...] = jnp.zeros_like(token_ref)

    read = lambda j: x_ref[0, rows_at(j), :].astype(F32)
    mean, rstd = col_stats(read, D, N, 10)
    rstd_ref[0] = rstd

    def act(j, _):
        rows = rows_at(j)
        n = (read(j) - mean) * rstd
        r, d = gate(n * spread(gtab, rows, N) + spread(btab, rows, N))
        n0_ref[0, rows, :] = n.astype(BF)
        s0_ref[0, rows, :] = d.astype(BF)
        rbuf[rows, :] = r.astype(BF)
        return 0

    loop(D // R, act, 0, 10)
    for q in range(Q):
        @pl.when(lax.rem(start + i, Q) == q)
        def _(q=q):
            r1_ref[0, :D, q * N:(q + 1) * N] = rbuf[...]
            r1_ref[0, D:, q * N:(q + 1) * N] = jnp.ones((r1_ref.shape[1] - D, N), BF)


def wide_fwd(xT, gain, bias, Q, start=0, steps=None, into=None, token=None):
    S, D, N = xT.shape
    steps = S if steps is None else steps
    sd = jax.ShapeDtypeStruct
    at = lambda i: (start + i, 0, 0)
    into = tuple(into or ())
    token = () if token is None else (token,)
    one = lambda rows: pl.BlockSpec((1, rows, N), at)
    return pl.pallas_call(
        functools.partial(wide_fwd_kernel, Q, start), grid=(steps,),
        in_specs=[one(D), fixed((1, D)), fixed((2, D))] + [pl.BlockSpec(memory_space=pl.ANY)] * len(into + token),
        out_specs=[pl.BlockSpec((1, D + R, Q * N), lambda i: ((start + i) // Q, 0, 0)), one(D), one(D), one(1), fixed((8, L))],
        out_shape=[sd((S // Q, D + R, Q * N), BF), sd((S, D, N), BF), sd((S, D, N), BF), sd((S, 1, N), F32), sd((8, L), F32)],
        scratch_shapes=[pltpu.VMEM((D, L), F32)] * 2 + [pltpu.VMEM((D, N), BF)],
        input_output_aliases={3 + j: j for j in range(len(into))},
        compiler_params=params(), name="wide_fwd", cost_estimate=cost(1e9 * steps, 5.5e6 * steps),
    )(xT, gain, bias, *into, *token)


CH = 384


def front_kernel(Q, steps, r1_ref, w1t_ref, gain_ref, bias_ref, u_ref, n_ref, s_ref, rstd_ref, tail_ref, h_ref, gtab, btab):
    F, N = h_ref.shape
    T = N // Q
    i = pl.program_id(0)

    @pl.when(i == 0)
    def _():
        fill_table(gtab, gain_ref[0:1, :] * 0.5)
        fill_table(btab, bias_ref[1:2, :] * 0.5)

    h_ref[...] = nn(w1t_ref[...], r1_ref[0])
    for ls in chunks(N, CH):
        W = ls.stop - ls.start
        read = lambda j: h_ref[rows_at(j), ls]
        mean, rstd = col_stats(read, F, W)
        rstd_ref[0, :, ls] = rstd

        def act(j, _):
            rows = rows_at(j)
            n = (read(j) - mean) * rstd
            r, d = gate(n * spread(gtab, rows, W) + spread(btab, rows, W))
            u_ref[0, rows, ls] = r.astype(BF)
            n_ref[0, rows, ls] = n.astype(BF)
            s_ref[0, rows, ls] = d.astype(BF)
            return 0

        loop(F // R, act, 0)
    rim_store(tail_ref, i, steps, [u_ref[0, :, (q + 1) * T - 2 * SHIFT:(q + 1) * T] for q in range(Q)])


def front(r1, w1t, gain, bias, Q):
    G, DE, N = r1.shape
    F = w1t.shape[0]
    sd = jax.ShapeDtypeStruct
    rim = (2, F, G // 2 * Q * 2 * SHIFT)
    return pl.pallas_call(
        functools.partial(front_kernel, Q, G // 2), grid=(G,),
        in_specs=[seq_spec(1, DE, N), fixed(w1t.shape), fixed(gain.shape), fixed(bias.shape)],
        out_specs=[seq_spec(1, F, N)] * 3 + [seq_spec(1, 1, N), fixed(rim)],
        out_shape=[sd((G, F, N), BF)] * 3 + [sd((G, 1, N), F32), sd(rim, BF)],
        scratch_shapes=[pltpu.VMEM((F, N), F32)] + [pltpu.VMEM((F, L), F32)] * 2,
        compiler_params=params(), name="front", cost_estimate=cost(4e9, 19e6),
    )(r1, w1t, gain, bias)


def pull(F, W, ls, d_ref, n_at, s_at, rstd, gtab, gacc, bacc, e_ref, unroll=25):
    def first(j, carry):
        m1, m2 = carry
        rows = rows_at(j)
        ds = d_ref[rows, ls] * s_at(rows).astype(F32)
        dn = ds * n_at(rows).astype(F32)
        gain = spread(gtab, rows, W)
        t = ds * gain
        d_ref[rows, ls] = t
        lane_sum(bacc, rows, ds)
        lane_sum(gacc, rows, dn)
        return m1 + fold(t), m2 + fold(dn * gain)

    zero = jnp.zeros((8, W), F32)
    m1, m2 = loop(F // R, first, (zero, zero), unroll)
    m1, m2 = total8(m1) * (1.0 / F) * rstd, total8(m2) * (1.0 / F) * rstd

    def second(j, _):
        rows = rows_at(j)
        e_ref[0, rows, ls] = ((d_ref[rows, ls] * rstd - m1) - n_at(rows).astype(F32) * m2).astype(BF)
        return 0

    loop(F // R, second, 0, unroll)


def middle_kernel(n, Q, steps, flags_ref, u_ref, below_ref, above_ref, tail_ref, c_ref, x_ref, wct_ref, w3_ref, w3t_ref,
                  gain_ref, bias_ref, e_ref, out_ref, pieces_ref, small_ref, head_ref,
                  ubuf, cbuf, rbuf, h_ref, d_ref, n_ref, s_ref, o_ref, gacc, bacc, gwo_ref, gwc_ref, hbuf, gtab, btab):
    F, N = h_ref.shape
    T = N // Q
    D = c_ref.shape[1]
    i = pl.program_id(0)

    @pl.when(i == 0)
    def _():
        fill_table(gtab, gain_ref[1:2, :] * 0.5)
        fill_table(btab, bias_ref[3:4, :] * 0.5)
        ubuf[3 * F:, :] = jnp.ones((R, N), BF)
        rbuf[F:, :] = jnp.ones((R, N), BF)
        gwo_ref[...] = jnp.zeros_like(gwo_ref)
        gwc_ref[...] = jnp.zeros_like(gwc_ref)
        gacc[...] = jnp.zeros_like(gacc)
        bacc[...] = jnp.zeros_like(bacc)

    rim_load(hbuf, i, steps,
             lambda: jnp.where(flags_ref[0] == 1, jnp.zeros_like(below_ref[...]), below_ref[...]),
             lambda: jnp.where(flags_ref[1] == 1, tail_ref[0], above_ref[...]))
    ubuf[:F, :] = u_ref[0]
    for k in (1, 2):
        w = k * SHIFT
        parts = []
        for q in range(Q):
            parts += [hbuf[:, (q + 1) * 2 * SHIFT - w:(q + 1) * 2 * SHIFT], u_ref[0, :, q * T:(q + 1) * T - w]]
        ubuf[k * F:(k + 1) * F, :] = jnp.concatenate(parts, axis=1)
    for q in range(Q):
        cbuf[:, q * T:(q + 1) * T] = c_ref[q]
    h_ref[...] = nn(wct_ref[...], ubuf[...])
    d_ref[...] = nn(w3_ref[...], cbuf[...])
    rstds = []
    for ls in chunks(N, CH):
        W = ls.stop - ls.start
        read = lambda j: h_ref[rows_at(j), ls]
        mean, rstd = col_stats(read, F, W)
        rstds.append(rstd)

        def act(j, _):
            rows = rows_at(j)
            v = (read(j) - mean) * rstd
            r, d = gate(v * spread(gtab, rows, W) + spread(btab, rows, W))
            rbuf[rows, ls] = r.astype(BF)
            n_ref[rows, ls] = v
            s_ref[rows, ls] = d
            return 0

        loop(F // R, act, 0)
    for q in range(Q):
        o_ref[q] = nn(w3t_ref[...], rbuf[:, q * T:(q + 1) * T])
    gwo_ref[...] += nt(rbuf[...], cbuf[...])
    for ls, rstd in zip(chunks(N, CH), rstds):
        pull(F, ls.stop - ls.start, ls, d_ref, lambda rows: n_ref[rows, ls], lambda rows: s_ref[rows, ls], rstd, gtab, gacc, bacc, e_ref)
    gwc_ref[...] += nt(ubuf[...], e_ref[0])
    for q in range(Q):
        def emit(j, _):
            rows = rows_at(j)
            out_ref[q, rows, :] = (o_ref[q, rows, :] + x_ref[q, rows, :].astype(F32)).astype(BF)
            return 0

        loop(D // R, emit, 0, 25)
    rim_store(head_ref, i, steps, [e_ref[0, :, q * T:q * T + 2 * SHIFT] for q in range(Q)])

    @pl.when(i == pl.num_programs(0) - 1)
    def _():
        small_ref[...] = jnp.zeros_like(small_ref)
        small_ref[0:1, :F] = lane_total(gacc[...]) * 0.5
        small_ref[0:1, F:] = lane_total(bacc[...]) * 0.5
        small_ref[1:2, :F] = gwc_ref[3 * F:3 * F + 1, :]
        small_ref[2:3, :] = gwo_ref[F:F + 1, :]
        put_pieces(n, pieces_ref, gwc_ref, 3 * F, F, 0)
        put_pieces(n, pieces_ref, gwo_ref, F, D, unit_plan(n, 3 * F, F)[2])


def middle(n, Q, flags, uT, below, above, tails, cT, xT, wct, w3, w3t, gain, bias, rows):
    G, F, N = uT.shape
    S, D, T = cT.shape
    sd = jax.ShapeDtypeStruct
    return pl.pallas_call(
        functools.partial(middle_kernel, n, Q, G // 2), grid=(G,),
        in_specs=[smem(), seq_spec(1, F, N), fixed(below.shape), fixed(above.shape), fixed(tails.shape), seq_spec(Q, D, T), seq_spec(Q, D, T),
                  fixed(wct.shape), fixed(w3.shape), fixed(w3t.shape), fixed(gain.shape), fixed(bias.shape)],
        out_specs=[seq_spec(1, F, N), seq_spec(Q, D, T), fixed((n, WIDE // L, rows, L)), fixed((8, D)), fixed(tails.shape)],
        out_shape=[sd((G, F, N), BF), sd((S, D, T), BF), sd((n, WIDE // L, rows, L), F32), sd((8, D), F32), sd(tails.shape, BF)],
        scratch_shapes=[pltpu.VMEM((3 * F + R, N), BF), pltpu.VMEM((D, N), BF), pltpu.VMEM((F + R, N), BF), pltpu.VMEM((F, N), F32),
                        pltpu.VMEM((F, N), F32), pltpu.VMEM((F, N), F32), pltpu.VMEM((F, N), F32), pltpu.VMEM((Q, D, T), F32),
                        pltpu.VMEM((F, L), F32), pltpu.VMEM((F, L), F32), pltpu.VMEM((F + R, D), F32),
                        pltpu.VMEM((3 * F + R, F), F32), pltpu.VMEM((F, Q * 2 * SHIFT), BF), pltpu.VMEM((F, L), F32), pltpu.VMEM((F, L), F32)],
        compiler_params=params(), name="middle", cost_estimate=cost(18e9, 36e6),
    )(flags, uT, below, above, tails, cT, xT, wct, w3, w3t, gain, bias)


def back_kernel(n, Q, steps, flags_ref, e_ref, below_ref, above_ref, head_ref, n_ref, s_ref, rstd_ref, r1_ref, wc_ref, gain_ref,
                small_in, e1_ref, pieces_ref, small_ref, ebuf, d_ref, gacc, bacc, gwi_ref, hbuf, gtab, e1buf):
    F, N = d_ref.shape
    T = N // Q
    D = gwi_ref.shape[0] - R
    i = pl.program_id(0)

    @pl.when(i == 0)
    def _():
        fill_table(gtab, gain_ref[0:1, :] * 0.5)
        gwi_ref[...] = jnp.zeros_like(gwi_ref)
        gacc[...] = jnp.zeros_like(gacc)
        bacc[...] = jnp.zeros_like(bacc)

    rim_load(hbuf, i, steps,
             lambda: jnp.where(flags_ref[1] == 1, head_ref[1], above_ref[...]),
             lambda: jnp.where(flags_ref[0] == 1, jnp.zeros_like(below_ref[...]), below_ref[...]))
    ebuf[:F, :] = e_ref[0]
    for k in (1, 2):
        w = k * SHIFT
        parts = []
        for q in range(Q):
            parts += [e_ref[0, :, q * T + w:(q + 1) * T], hbuf[:, q * 2 * SHIFT:q * 2 * SHIFT + w]]
        ebuf[k * F:(k + 1) * F, :] = jnp.concatenate(parts, axis=1)
    d_ref[...] = nn(wc_ref[...], ebuf[...])
    for ls in chunks(N, CH):
        pull(F, ls.stop - ls.start, ls, d_ref, lambda rows: n_ref[0, rows, ls], lambda rows: s_ref[0, rows, ls], rstd_ref[0, :, ls],
             gtab, gacc, bacc, e1buf)
    gwi_ref[...] += nt(r1_ref[0], e1buf[0])
    for q in range(Q):
        e1_ref[q] = e1buf[0, :, q * T:(q + 1) * T]

    @pl.when(i == pl.num_programs(0) - 1)
    def _():
        small_ref[...] = small_in[...]
        small_ref[1:2, F:] = gwi_ref[D:D + 1, :]
        small_ref[3:4, :F] = lane_total(gacc[...]) * 0.5
        small_ref[3:4, F:] = lane_total(bacc[...]) * 0.5
        put_pieces(n, pieces_ref, gwi_ref, D, F, 0)


def back(n, Q, flags, eT, below, above, heads, n1, s1, rstd1, r1, wc, gain, small, rows):
    G, F, N = eT.shape
    DE = r1.shape[1]
    sd = jax.ShapeDtypeStruct
    return pl.pallas_call(
        functools.partial(back_kernel, n, Q, G // 2), grid=(G,),
        in_specs=[smem(), seq_spec(1, F, N), fixed(below.shape), fixed(above.shape), fixed(heads.shape), seq_spec(1, F, N), seq_spec(1, F, N),
                  seq_spec(1, 1, N), seq_spec(1, DE, N), fixed(wc.shape), fixed(gain.shape), fixed(small.shape)],
        out_specs=[seq_spec(Q, F, N // Q), fixed((n, WIDE // L, rows, L)), fixed(small.shape)],
        out_shape=[sd((G * Q, F, N // Q), BF), sd((n, WIDE // L, rows, L), F32), sd(small.shape, F32)],
        scratch_shapes=[pltpu.VMEM((3 * F, N), BF), pltpu.VMEM((F, N), F32), pltpu.VMEM((F, L), F32), pltpu.VMEM((F, L), F32),
                        pltpu.VMEM((DE, F), F32), pltpu.VMEM((F, Q * 2 * SHIFT), BF), pltpu.VMEM((F, L), F32),
                        pltpu.VMEM((1, F, N), BF)],
        compiler_params=params(), name="back", cost_estimate=cost(8e9, 25e6),
    )(flags, eT, below, above, heads, n1, s1, rstd1, r1, wc, gain, small)


def wide_bwd_kernel(Q, e_ref, w1_ref, n_ref, s_ref, rstd_ref, c_ref, gain_ref, small_in, *refs):
    dx_ref, small_ref, gtab, gacc, bacc = refs[-5 - Q:-Q]
    d_refs = refs[-Q:]
    D, N = d_refs[0].shape
    i = pl.program_id(0)

    @pl.when(i == 0)
    def _():
        fill_table(gtab, gain_ref[...] * 0.5)
        gacc[...] = jnp.zeros_like(gacc)
        bacc[...] = jnp.zeros_like(bacc)

    def dot(q):
        d_refs[q][...] = nn(w1_ref[...], e_ref[q])

    def pull_wide(q):
        d_ref = d_refs[q]

        def first(j, carry):
            m1, m2 = carry
            rows = rows_at(j)
            ds = d_ref[rows, :] * s_ref[q, rows, :].astype(F32)
            dn = ds * n_ref[q, rows, :].astype(F32)
            gain = spread(gtab, rows, N)
            t = ds * gain
            d_ref[rows, :] = t
            lane_sum(bacc, rows, ds)
            lane_sum(gacc, rows, dn)
            return m1 + fold(t), m2 + fold(dn * gain)

        zero = jnp.zeros((8, N), F32)
        m1, m2 = loop(D // R, first, (zero, zero), 50)
        rstd = rstd_ref[q]
        m1, m2 = total8(m1) * (1.0 / D) * rstd, total8(m2) * (1.0 / D) * rstd

        def second(j, _):
            rows = rows_at(j)
            g = (d_ref[rows, :] * rstd - m1) - n_ref[q, rows, :].astype(F32) * m2
            dx_ref[q, rows, :] = (g + c_ref[q, rows, :].astype(F32)).astype(BF)
            return 0

        loop(D // R, second, 0, 50)

    dot(0)
    for q in range(Q):
        if q + 1 < Q:
            dot(q + 1)
        pull_wide(q)

    @pl.when(i == pl.num_programs(0) - 1)
    def _():
        small_ref[...] = small_in[...]
        small_ref[4:5, :] = small_in[4:5, :] + lane_total(gacc[...]) * 0.5
        small_ref[5:6, :] = small_in[5:6, :] + lane_total(bacc[...]) * 0.5


def wide_bwd(Q, e1, w1, n0, s0, rstd0, cT, gain, small, start=0, steps=None, into=None):
    S, D, N = cT.shape
    F = e1.shape[1]
    steps = S // Q if steps is None else steps
    sd = jax.ShapeDtypeStruct
    at = lambda i: (start + i, 0, 0)
    into = () if into is None else (into,)
    part = lambda rows: pl.BlockSpec((Q, rows, N), at)
    return pl.pallas_call(
        functools.partial(wide_bwd_kernel, Q), grid=(steps,),
        in_specs=[part(F), fixed(w1.shape), part(D), part(D), part(1), part(D),
                  fixed(gain.shape), fixed(small.shape)] + [pl.BlockSpec(memory_space=pl.ANY)] * len(into),
        out_specs=[part(D), fixed(small.shape)],
        out_shape=[sd((S, D, N), BF), sd(small.shape, F32)],
        scratch_shapes=[pltpu.VMEM((D, L), F32)] * 3 + [pltpu.VMEM((D, N), F32)] * Q,
        input_output_aliases={8: 0} if into else {},
        compiler_params=params(), name="wide_bwd", cost_estimate=cost(2e9 * steps, 8.4e6 * steps),
    )(e1, w1, n0, s0, rstd0, cT, gain, small, *into)


def swap(v, bit, n):
    return lax.ppermute(v, "ctx", [(i, i ^ bit) for i in range(n)])


def bits_of(n):
    out, b = [], 1
    while b < n:
        out.append(b)
        b *= 2
    return out


def together(*values):
    return lax.optimization_barrier(values)


def slot_table(n, me):
    diff = jnp.arange(n, dtype=jnp.int32) ^ me
    return sum((jnp.where((diff & bit) != 0, n // 2 // bit, 0) for bit in bits_of(n)), jnp.zeros_like(diff))


def split_for(full, bit, me):
    pairs = full.reshape((-1, 2) + full.shape[1:])
    mine = jnp.where((me & bit) == 0, 0, 1)
    keep = lax.dynamic_index_in_dim(pairs, mine, 1, keepdims=False)
    return keep, lax.dynamic_index_in_dim(pairs, 1 - mine, 1, keepdims=False).astype(BF)


def sum_all(v, n):
    for bit in bits_of(n):
        v = v + swap(v, bit, n)
    return v


def to_units(flat, n, M, C, rows=None):
    q, parts, units = unit_plan(n, M, C)
    return jnp.pad(flat.reshape(units, q), ((0, 0), (0, WIDE - q))).reshape(units, WIDE // L, L).transpose(1, 0, 2)


def round_up(v, m=8):
    return -(-v // m) * m


def on_device(block_input, cotangent, w_in, w_conv, w_out, wide_gain, wide_bias, narrow_gain, narrow_bias, dealing):
    slots, seqs, T, D = block_input.shape
    F = narrow_gain.shape[1]
    n = lax.axis_size("ctx")
    half = dealing.shape[0] // 2
    me = lax.axis_index("ctx")
    pair = jnp.sum(jnp.where(dealing[:half] == me, jnp.arange(half, dtype=jnp.int32), 0))
    flags = jnp.stack([pair == 0, pair == half - 1]).astype(jnp.int32)
    up = [(i, (i + 1) % n) for i in range(n)]
    down = [((i + 1) % n, i) for i in range(n)]
    table = slot_table(n, me)
    units_in, units_conv, units_out = (unit_plan(n, m, c)[2] for m, c in ((D, F), (3 * F, F), (F, D)))
    rows_in, rows_rest = round_up(units_in), round_up(units_conv + units_out)

    xT = block_input.transpose(0, 1, 3, 2).reshape(slots * seqs, D, T)
    cT = cotangent.transpose(0, 1, 3, 2).reshape(slots * seqs, D, T)

    piece_in = jnp.pad(to_units(w_in, n, D, F), ((0, 0), (0, rows_in - units_in), (0, 0)))
    piece_rest = jnp.concatenate([to_units(w_conv, n, 3 * F, F), to_units(w_out, n, F, D)], axis=1)
    piece_rest = jnp.pad(piece_rest, ((0, 0), (0, rows_rest - piece_rest.shape[1]), (0, 0)))
    gain0 = wide_gain.reshape(1, D)
    bits = bits_of(n)
    Q = 2
    steps = slots * seqs // Q

    buf_in, buf_rest = piece_in[None], piece_rest[None]
    acts, gain, done, token = (), gain0, 0, None
    far = list(reversed(bits))
    for s, bit in enumerate(far):
        got_in = swap(buf_in, bit, n)
        if s < len(far) - 2:
            got_rest = swap(buf_rest, bit, n)
        count = (steps * (s + 1)) // (len(far) - 1) * Q - done if s < len(far) - 1 else 0
        if count:
            *acts, token = wide_fwd(xT, gain, wide_bias, Q, done, count, acts, token)
            done += count
        buf_in = jnp.concatenate([buf_in, got_in], axis=0)
        if s < len(far) - 2:
            buf_rest = jnp.concatenate([buf_rest, got_rest], axis=0)
        buf_in, buf_rest, token, gain = together(buf_in, buf_rest, token, gain)
    r1, n0, s0, rstd0 = acts
    got_rest = swap(buf_rest, far[-2], n)
    w1, w1t = unpack_in(n, table, buf_in, narrow_bias, token, D, F)
    uT, n1, s1, rstd1, tails = front(r1, w1t, narrow_gain, narrow_bias, Q)
    buf_rest, tails = together(jnp.concatenate([buf_rest, got_rest], axis=0), tails)
    below = lax.ppermute(tails[0], "ctx", up)
    above = lax.ppermute(tails[1], "ctx", down)
    buf_rest = jnp.concatenate([buf_rest, swap(buf_rest, far[-1], n)], axis=0)
    wc, wct, w3, w3t = unpack_rest(n, table, buf_rest, narrow_bias, wide_bias, D, F)
    eT, outT, rest, small, heads = middle(n, Q, flags, uT, below, above, tails, cT, xT, wct, w3, w3t,
                                          narrow_gain, narrow_bias, rows_rest)

    keep, send = split_for(rest, bits[0], me)
    got = swap(send, bits[0], n)
    above = lax.ppermute(heads[0], "ctx", down)
    below = lax.ppermute(heads[1], "ctx", up)
    rest = keep + got.astype(F32)
    keep, send = split_for(rest, bits[1], me)
    send, gain1 = together(send, narrow_gain)
    got = swap(send, bits[1], n)
    e1, into, small = back(n, Q, flags, eT, below, above, heads, n1, s1, rstd1, r1, wc, gain1, small, rows_in)
    rest, small = together(keep + got.astype(F32), small)

    dxT, gain, halves = None, gain0, 2
    for s in range(halves):
        keep_i, send_i = split_for(into, bits[s], me)
        keep_r, send_r = split_for(rest, bits[s + 2], me)
        send_r, send_i, gain = together(send_r, send_i, gain)
        got_r, got_i = swap(send_r, bits[s + 2], n), swap(send_i, bits[s], n)
        dxT, small = wide_bwd(Q, e1, w1, n0, s0, rstd0, cT, gain, small, s * steps // halves, steps // halves, dxT)
        rest, into, small = together(keep_r + got_r.astype(F32), keep_i + got_i.astype(F32), small)
    rest_bits, in_bits = bits[2 + halves:], bits[halves:]
    for j in range(len(bits)):
        got = swap(small, bits[j], n)
        if j < len(rest_bits):
            keep_r, send_r = split_for(rest, rest_bits[j], me)
            rest = keep_r + swap(send_r, rest_bits[j], n).astype(F32)
        if j < len(in_bits):
            keep_i, send_i = split_for(into, in_bits[j], me)
            into = keep_i + swap(send_i, in_bits[j], n).astype(F32)
        small = small + got
        if j < len(in_bits):
            small, rest, into = together(small, rest, into)
    own_rest, own_in = rest[0], into[0]

    def owned(own, at, M, C):
        q, parts, units = unit_plan(n, M, C)
        return own[:, at:at + units].transpose(1, 0, 2).reshape(units, WIDE)[:, :q].reshape(-1)

    back4 = lambda v: v.reshape(slots, seqs, D, T).transpose(0, 1, 3, 2)
    return (back4(outT), back4(dxT), owned(own_in, 0, D, F), owned(own_rest, 0, 3 * F, F), owned(own_rest, units_conv, F, D),
            small[4], jnp.stack([small[5], small[2]]), jnp.stack([small[3, :F], small[0, :F]]),
            jnp.stack([small[1, F:], small[3, F:], small[1, :F], small[0, F:]]))


def solution(mesh):
    whole, flat, copied = P("ctx", None, None, None), P("ctx"), P()
    return jax.shard_map(
        on_device, mesh=mesh,
        in_specs=(whole, whole, flat, flat, flat, copied, copied, copied, copied, copied),
        out_specs=(whole, whole, flat, flat, flat, copied, copied, copied, copied),
        check_vma=False,
    )
```

```python
import functools
import math
import jax
import jax.numpy as jnp
from jax import lax
from jax.experimental import pallas as pl
from jax.experimental.pallas import tpu as pltpu
from jax.sharding import PartitionSpec as P

EPS = 1e-05
BF = jnp.bfloat16
F32 = jnp.float32
L = 128
R = 16
SHIFT = 16
WIDE = 256


def params(mb=52):
    return pltpu.CompilerParams(dimension_semantics=("arbitrary",), vmem_limit_bytes=mb * 1024 * 1024)


def cost(flops, nbytes, trans=0):
    return pl.CostEstimate(flops=int(flops), bytes_accessed=int(nbytes), transcendentals=int(trans))


def rows_at(i):
    return pl.ds(pl.multiple_of(i * R, R), R)


def loop(n, body, init, unroll=25):
    return lax.fori_loop(0, n, body, init, unroll=min(n, unroll))


def fold(v):
    return v[:8] + v[8:]


def total8(v):
    return jnp.sum(v, axis=0, keepdims=True)


def nt(a, b):
    return lax.dot_general(a, b, (((1,), (1,)), ((), ())), preferred_element_type=F32)


def nn(a, b):
    return jnp.dot(a, b, preferred_element_type=F32)


def chunks(N, width):
    return [slice(l, min(N, l + width)) for l in range(0, N, width)]


def spread(table, rows, w):
    return jnp.concatenate([table[rows, :]] * (-(-w // L)), axis=1)[:, :w]


def fill_table(table, row):
    table[...] = jnp.broadcast_to(row, (L, row.shape[1])).T


def col_stats(read, chans, N, unroll=25):
    acc = loop(chans // R, lambda i, a: a + fold(read(i)), jnp.zeros((8, N), F32), unroll)
    mean = total8(acc) * (1.0 / chans)

    def second(i, a):
        cen = read(i) - mean
        return a + fold(cen * cen)

    acc = loop(chans // R, second, jnp.zeros((8, N), F32), unroll)
    return mean, lax.rsqrt(total8(acc) * (1.0 / chans) + EPS)


def gate(h):
    t = jnp.tanh(h)
    r = h + h * t
    return r, (1.0 + t) + (r - r * t)


def lane_sum(acc_ref, rows, v):
    N = v.shape[1]
    full = N // L * L
    tot = v[:, :L]
    for j in range(L, full, L):
        tot = tot + v[:, j:j + L]
    if full < N:
        tot = tot + jnp.concatenate([v[:, full:], jnp.zeros((v.shape[0], L - (N - full)), v.dtype)], axis=1)
    acc_ref[rows, :] += tot


def seq_spec(B, rows, N):
    return pl.BlockSpec((B, rows, N), lambda i: (i, 0, 0))


def fixed(shape):
    zero = (0,) * len(shape)
    return pl.BlockSpec(shape, lambda i: zero)


def smem():
    return pl.BlockSpec(memory_space=pltpu.SMEM)


def vmem():
    return pl.BlockSpec(memory_space=pltpu.VMEM)


def lane_total(acc):
    return jnp.sum(acc.T, axis=0, keepdims=True)


def unit_plan(n, M, C):
    size = M * C // n
    whole = math.gcd(size, C)
    q = max(d for d in range(1, WIDE + 1) if whole % d == 0)
    return q, C // q, size // q


def unit_slices(n, M, C):
    q, parts, units = unit_plan(n, M, C)
    out = []
    for p in range(n):
        for h in range(parts):
            lo = -((h - units * p) // parts)
            hi = -((h - units * (p + 1)) // parts)
            if hi > lo:
                out.append((p, h, lo, hi - lo, lo * parts + h - units * p))
    return out


def strided(start, size, step):
    return pl.ds(start, size, stride=step) if step > 1 else pl.ds(start, size)


def planes(q):
    return [(j, j * L, min(q - j * L, L)) for j in range(-(-q // L))]


def put_matrix(n, mat_ref, f32_ref, off):
    M, C = mat_ref.shape
    q, parts, _ = unit_plan(n, M, C)
    for p, h, lo, cnt, u in unit_slices(n, M, C):
        for j, at, w in planes(q):
            mat_ref[lo:lo + cnt, h * q + at:h * q + at + w] = f32_ref[p, j, strided(off + u, cnt, parts), :][:, :w]


def put_pieces(n, out_ref, mat_ref, M, C, off):
    q, parts, _ = unit_plan(n, M, C)
    for p, h, lo, cnt, u in unit_slices(n, M, C):
        for j, at, w in planes(q):
            v = mat_ref[lo:lo + cnt, h * q + at:h * q + at + w]
            if w < L:
                v = jnp.concatenate([v, jnp.zeros((cnt, L - w), v.dtype)], axis=1)
            out_ref[p, j, strided(off + u, cnt, parts), :] = v


def flipped(mat):
    C = mat.shape[1]
    eye = (lax.broadcasted_iota(jnp.int32, (C, C), 0) == lax.broadcasted_iota(jnp.int32, (C, C), 1)).astype(BF)
    return nt(eye, mat).astype(BF)


def ordered(n, slots_ref, a_ref, b_ref, f32_ref):
    odd = slots_ref[n]
    for p in range(n):
        slot = slots_ref[p]
        piece = jnp.where(odd == p % 2, a_ref[slot].astype(F32), b_ref[slot].astype(F32))
        f32_ref[p] = piece


def bias_block(row):
    v = jnp.broadcast_to(row, (L, row.shape[1])).T[:, :R]
    hi = v.astype(BF)
    rest = v - hi.astype(F32)
    mid = rest.astype(BF)
    low = (rest - mid.astype(F32)).astype(BF)
    col = lax.broadcasted_iota(jnp.int32, v.shape, 1)
    zero = jnp.zeros_like(v)
    return jnp.where(col == 0, hi.astype(F32), jnp.where(col == 1, mid.astype(F32), jnp.where(col == 2, low.astype(F32), zero))).astype(BF)


def unpack_in_kernel(n, slots_ref, a_ref, b_ref, bias_ref, token_ref, w1_ref, w1t_ref, f32_ref, mat_ref):
    ordered(n, slots_ref, a_ref, b_ref, f32_ref)
    put_matrix(n, mat_ref, f32_ref, 0)
    D, F = mat_ref.shape
    w1_ref[...] = mat_ref[...].astype(BF)
    w1t_ref[:, :D] = flipped(w1_ref[...])
    w1t_ref[:, D:] = bias_block(bias_ref[0:1, :])


def unpack_in(n, slots, a, b, bias, token, D, F):
    sd = jax.ShapeDtypeStruct
    return pl.pallas_call(
        functools.partial(unpack_in_kernel, n),
        in_specs=[smem()] + [vmem()] * 3 + [pl.BlockSpec(memory_space=pl.ANY)], out_specs=[vmem(), vmem()],
        out_shape=[sd((D, F), BF), sd((F, D + R), BF)],
        scratch_shapes=[pltpu.VMEM((n,) + a.shape[1:], F32), pltpu.VMEM((D, F), F32)],
        compiler_params=pltpu.CompilerParams(vmem_limit_bytes=40 * 1024 * 1024), name="unpack_in",
        cost_estimate=cost(1e9, 6e6),
    )(slots, a, b, bias, token)


def unpack_rest_kernel(n, slots_ref, a_ref, b_ref, bias_ref, wide_ref, wc_ref, wct_ref, w3_ref, w3t_ref, f32_ref, matc_ref, mat3_ref):
    F, D = mat3_ref.shape
    ordered(n, slots_ref, a_ref, b_ref, f32_ref)
    put_matrix(n, matc_ref, f32_ref, 0)
    put_matrix(n, mat3_ref, f32_ref, unit_plan(n, 3 * F, F)[2])
    for k in range(3):
        tap = matc_ref[k * F:(k + 1) * F, :].astype(BF)
        wc_ref[:, k * F:(k + 1) * F] = tap
        wct_ref[:, k * F:(k + 1) * F] = flipped(tap)
    wct_ref[:, 3 * F:] = bias_block(bias_ref[2:3, :])
    w3_ref[...] = mat3_ref[...].astype(BF)
    w3t_ref[:, :F] = flipped(w3_ref[...])
    w3t_ref[:, F:] = bias_block(wide_ref[1:2, :])


def unpack_rest(n, slots, a, b, bias, wide_bias, D, F):
    sd = jax.ShapeDtypeStruct
    return pl.pallas_call(
        functools.partial(unpack_rest_kernel, n),
        in_specs=[smem()] + [vmem()] * 4, out_specs=[vmem()] * 4,
        out_shape=[sd((F, 3 * F), BF), sd((F, 3 * F + R), BF), sd((F, D), BF), sd((D, F + R), BF)],
        scratch_shapes=[pltpu.VMEM((n,) + a.shape[1:], F32), pltpu.VMEM((3 * F, F), F32), pltpu.VMEM((F, D), F32)],
        compiler_params=pltpu.CompilerParams(vmem_limit_bytes=40 * 1024 * 1024), name="unpack_rest",
        cost_estimate=cost(2e9, 14e6),
    )(slots, a, b, bias, wide_bias)


def rim_store(ref, i, steps, cols):
    for s in range(2 * steps):
        @pl.when(i == s)
        def _(s=s):
            w = cols[0].shape[1]
            for q, v in enumerate(cols):
                at = (s % steps * len(cols) + q) * w
                ref[s // steps, :, at:at + w] = v


def rim_load(buf, i, steps, first, second):
    w = buf.shape[1]
    for s in range(2 * steps):
        @pl.when(i == s)
        def _(s=s):
            src = first() if s < steps else second()
            buf[...] = src[:, s % steps * w:(s % steps + 1) * w]


def wide_fwd_kernel(Q, start, x_ref, gain_ref, bias_ref, *refs):
    r1_ref, n0_ref, s0_ref, rstd_ref, token_ref, gtab, btab, rbuf = refs[-8:]
    D, N = x_ref.shape[1:]
    i = pl.program_id(0)

    @pl.when(i == 0)
    def _():
        fill_table(gtab, gain_ref[...] * 0.5)
        fill_table(btab, bias_ref[0:1, :] * 0.5)
        token_ref[...] = jnp.zeros_like(token_ref)

    read = lambda j: x_ref[0, rows_at(j), :].astype(F32)
    mean, rstd = col_stats(read, D, N, 10)
    rstd_ref[0] = rstd

    def act(j, _):
        rows = rows_at(j)
        n = (read(j) - mean) * rstd
        r, d = gate(n * spread(gtab, rows, N) + spread(btab, rows, N))
        n0_ref[0, rows, :] = n.astype(BF)
        s0_ref[0, rows, :] = d.astype(BF)
        rbuf[rows, :] = r.astype(BF)
        return 0

    loop(D // R, act, 0, 10)
    for q in range(Q):
        @pl.when(lax.rem(start + i, Q) == q)
        def _(q=q):
            r1_ref[0, :D, q * N:(q + 1) * N] = rbuf[...]
            r1_ref[0, D:, q * N:(q + 1) * N] = jnp.ones((r1_ref.shape[1] - D, N), BF)


def wide_fwd(xT, gain, bias, Q, start=0, steps=None, into=None, token=None):
    S, D, N = xT.shape
    steps = S if steps is None else steps
    sd = jax.ShapeDtypeStruct
    at = lambda i: (start + i, 0, 0)
    into = tuple(into or ())
    token = () if token is None else (token,)
    one = lambda rows: pl.BlockSpec((1, rows, N), at)
    return pl.pallas_call(
        functools.partial(wide_fwd_kernel, Q, start), grid=(steps,),
        in_specs=[one(D), fixed((1, D)), fixed((2, D))] + [pl.BlockSpec(memory_space=pl.ANY)] * len(into + token),
        out_specs=[pl.BlockSpec((1, D + R, Q * N), lambda i: ((start + i) // Q, 0, 0)), one(D), one(D), one(1), fixed((8, L))],
        out_shape=[sd((S // Q, D + R, Q * N), BF), sd((S, D, N), BF), sd((S, D, N), BF), sd((S, 1, N), F32), sd((8, L), F32)],
        scratch_shapes=[pltpu.VMEM((D, L), F32)] * 2 + [pltpu.VMEM((D, N), BF)],
        input_output_aliases={3 + j: j for j in range(len(into))},
        compiler_params=params(), name="wide_fwd", cost_estimate=cost(1e9 * steps, 5.5e6 * steps),
    )(xT, gain, bias, *into, *token)


CH = 384


def front_kernel(Q, steps, r1_ref, w1t_ref, gain_ref, bias_ref, u_ref, n_ref, s_ref, rstd_ref, tail_ref, h_ref, gtab, btab):
    F, N = h_ref.shape
    T = N // Q
    i = pl.program_id(0)

    @pl.when(i == 0)
    def _():
        fill_table(gtab, gain_ref[0:1, :] * 0.5)
        fill_table(btab, bias_ref[1:2, :] * 0.5)

    h_ref[...] = nn(w1t_ref[...], r1_ref[0])
    for ls in chunks(N, CH):
        W = ls.stop - ls.start
        read = lambda j: h_ref[rows_at(j), ls]
        mean, rstd = col_stats(read, F, W)
        rstd_ref[0, :, ls] = rstd

        def act(j, _):
            rows = rows_at(j)
            n = (read(j) - mean) * rstd
            r, d = gate(n * spread(gtab, rows, W) + spread(btab, rows, W))
            u_ref[0, rows, ls] = r.astype(BF)
            n_ref[0, rows, ls] = n.astype(BF)
            s_ref[0, rows, ls] = d.astype(BF)
            return 0

        loop(F // R, act, 0)
    rim_store(tail_ref, i, steps, [u_ref[0, :, (q + 1) * T - 2 * SHIFT:(q + 1) * T] for q in range(Q)])


def front(r1, w1t, gain, bias, Q):
    G, DE, N = r1.shape
    F = w1t.shape[0]
    sd = jax.ShapeDtypeStruct
    rim = (2, F, G // 2 * Q * 2 * SHIFT)
    return pl.pallas_call(
        functools.partial(front_kernel, Q, G // 2), grid=(G,),
        in_specs=[seq_spec(1, DE, N), fixed(w1t.shape), fixed(gain.shape), fixed(bias.shape)],
        out_specs=[seq_spec(1, F, N)] * 3 + [seq_spec(1, 1, N), fixed(rim)],
        out_shape=[sd((G, F, N), BF)] * 3 + [sd((G, 1, N), F32), sd(rim, BF)],
        scratch_shapes=[pltpu.VMEM((F, N), F32)] + [pltpu.VMEM((F, L), F32)] * 2,
        compiler_params=params(), name="front", cost_estimate=cost(4e9, 19e6),
    )(r1, w1t, gain, bias)


def pull(F, W, ls, d_ref, n_at, s_at, rstd, gtab, gacc, bacc, e_ref, unroll=25):
    def first(j, carry):
        m1, m2 = carry
        rows = rows_at(j)
        ds = d_ref[rows, ls] * s_at(rows).astype(F32)
        dn = ds * n_at(rows).astype(F32)
        gain = spread(gtab, rows, W)
        t = ds * gain
        d_ref[rows, ls] = t
        lane_sum(bacc, rows, ds)
        lane_sum(gacc, rows, dn)
        return m1 + fold(t), m2 + fold(dn * gain)

    zero = jnp.zeros((8, W), F32)
    m1, m2 = loop(F // R, first, (zero, zero), unroll)
    m1, m2 = total8(m1) * (1.0 / F) * rstd, total8(m2) * (1.0 / F) * rstd

    def second(j, _):
        rows = rows_at(j)
        e_ref[0, rows, ls] = ((d_ref[rows, ls] * rstd - m1) - n_at(rows).astype(F32) * m2).astype(BF)
        return 0

    loop(F // R, second, 0, unroll)


def middle_kernel(n, Q, steps, flags_ref, u_ref, below_ref, above_ref, tail_ref, c_ref, x_ref, wct_ref, w3_ref, w3t_ref,
                  gain_ref, bias_ref, e_ref, out_ref, pieces_ref, small_ref, head_ref,
                  ubuf, cbuf, rbuf, h_ref, d_ref, n_ref, s_ref, o_ref, gacc, bacc, gwo_ref, gwc_ref, hbuf, gtab, btab):
    F, N = h_ref.shape
    T = N // Q
    D = c_ref.shape[1]
    i = pl.program_id(0)

    @pl.when(i == 0)
    def _():
        fill_table(gtab, gain_ref[1:2, :] * 0.5)
        fill_table(btab, bias_ref[3:4, :] * 0.5)
        ubuf[3 * F:, :] = jnp.ones((R, N), BF)
        rbuf[F:, :] = jnp.ones((R, N), BF)
        gwo_ref[...] = jnp.zeros_like(gwo_ref)
        gwc_ref[...] = jnp.zeros_like(gwc_ref)
        gacc[...] = jnp.zeros_like(gacc)
        bacc[...] = jnp.zeros_like(bacc)

    rim_load(hbuf, i, steps,
             lambda: jnp.where(flags_ref[0] == 1, jnp.zeros_like(below_ref[...]), below_ref[...]),
             lambda: jnp.where(flags_ref[1] == 1, tail_ref[0], above_ref[...]))
    ubuf[:F, :] = u_ref[0]
    for k in (1, 2):
        w = k * SHIFT
        parts = []
        for q in range(Q):
            parts += [hbuf[:, (q + 1) * 2 * SHIFT - w:(q + 1) * 2 * SHIFT], u_ref[0, :, q * T:(q + 1) * T - w]]
        ubuf[k * F:(k + 1) * F, :] = jnp.concatenate(parts, axis=1)
    for q in range(Q):
        cbuf[:, q * T:(q + 1) * T] = c_ref[q]
    h_ref[...] = nn(wct_ref[...], ubuf[...])
    d_ref[...] = nn(w3_ref[...], cbuf[...])
    rstds = []
    for ls in chunks(N, CH):
        W = ls.stop - ls.start
        read = lambda j: h_ref[rows_at(j), ls]
        mean, rstd = col_stats(read, F, W)
        rstds.append(rstd)

        def act(j, _):
            rows = rows_at(j)
            v = (read(j) - mean) * rstd
            r, d = gate(v * spread(gtab, rows, W) + spread(btab, rows, W))
            rbuf[rows, ls] = r.astype(BF)
            n_ref[rows, ls] = v
            s_ref[rows, ls] = d
            return 0

        loop(F // R, act, 0)
    o_ref[...] = nn(w3t_ref[...], rbuf[...])
    gwo_ref[...] += nt(rbuf[...], cbuf[...])
    for ls, rstd in zip(chunks(N, CH), rstds):
        pull(F, ls.stop - ls.start, ls, d_ref, lambda rows: n_ref[rows, ls], lambda rows: s_ref[rows, ls], rstd, gtab, gacc, bacc, e_ref)
    gwc_ref[...] += nt(ubuf[...], e_ref[0])
    for q in range(Q):
        def emit(j, _):
            rows = rows_at(j)
            out_ref[q, rows, :] = (o_ref[rows, q * T:(q + 1) * T] + x_ref[q, rows, :].astype(F32)).astype(BF)
            return 0

        loop(D // R, emit, 0, 50)
    rim_store(head_ref, i, steps, [e_ref[0, :, q * T:q * T + 2 * SHIFT] for q in range(Q)])

    @pl.when(i == pl.num_programs(0) - 1)
    def _():
        small_ref[...] = jnp.zeros_like(small_ref)
        small_ref[0:1, :F] = lane_total(gacc[...]) * 0.5
        small_ref[0:1, F:] = lane_total(bacc[...]) * 0.5
        small_ref[1:2, :F] = gwc_ref[3 * F:3 * F + 1, :]
        small_ref[2:3, :] = gwo_ref[F:F + 1, :]
        put_pieces(n, pieces_ref, gwc_ref, 3 * F, F, 0)
        put_pieces(n, pieces_ref, gwo_ref, F, D, unit_plan(n, 3 * F, F)[2])


def middle(n, Q, flags, uT, below, above, tails, cT, xT, wct, w3, w3t, gain, bias, rows):
    G, F, N = uT.shape
    S, D, T = cT.shape
    sd = jax.ShapeDtypeStruct
    return pl.pallas_call(
        functools.partial(middle_kernel, n, Q, G // 2), grid=(G,),
        in_specs=[smem(), seq_spec(1, F, N), fixed(below.shape), fixed(above.shape), fixed(tails.shape), seq_spec(Q, D, T), seq_spec(Q, D, T),
                  fixed(wct.shape), fixed(w3.shape), fixed(w3t.shape), fixed(gain.shape), fixed(bias.shape)],
        out_specs=[seq_spec(1, F, N), seq_spec(Q, D, T), fixed((n, WIDE // L, rows, L)), fixed((8, D)), fixed(tails.shape)],
        out_shape=[sd((G, F, N), BF), sd((S, D, T), BF), sd((n, WIDE // L, rows, L), F32), sd((8, D), F32), sd(tails.shape, BF)],
        scratch_shapes=[pltpu.VMEM((3 * F + R, N), BF), pltpu.VMEM((D, N), BF), pltpu.VMEM((F + R, N), BF), pltpu.VMEM((F, N), F32),
                        pltpu.VMEM((F, N), F32), pltpu.VMEM((F, N), F32), pltpu.VMEM((F, N), F32), pltpu.VMEM((D, N), F32),
                        pltpu.VMEM((F, L), F32), pltpu.VMEM((F, L), F32), pltpu.VMEM((F + R, D), F32),
                        pltpu.VMEM((3 * F + R, F), F32), pltpu.VMEM((F, Q * 2 * SHIFT), BF), pltpu.VMEM((F, L), F32), pltpu.VMEM((F, L), F32)],
        compiler_params=params(), name="middle", cost_estimate=cost(18e9, 36e6),
    )(flags, uT, below, above, tails, cT, xT, wct, w3, w3t, gain, bias)


def back_kernel(n, Q, steps, flags_ref, e_ref, below_ref, above_ref, head_ref, n_ref, s_ref, rstd_ref, r1_ref, wc_ref, gain_ref,
                small_in, e1_ref, pieces_ref, small_ref, ebuf, d_ref, gacc, bacc, gwi_ref, hbuf, gtab, e1buf):
    F, N = d_ref.shape
    T = N // Q
    D = gwi_ref.shape[0] - R
    i = pl.program_id(0)

    @pl.when(i == 0)
    def _():
        fill_table(gtab, gain_ref[0:1, :] * 0.5)
        gwi_ref[...] = jnp.zeros_like(gwi_ref)
        gacc[...] = jnp.zeros_like(gacc)
        bacc[...] = jnp.zeros_like(bacc)

    rim_load(hbuf, i, steps,
             lambda: jnp.where(flags_ref[1] == 1, head_ref[1], above_ref[...]),
             lambda: jnp.where(flags_ref[0] == 1, jnp.zeros_like(below_ref[...]), below_ref[...]))
    ebuf[:F, :] = e_ref[0]
    for k in (1, 2):
        w = k * SHIFT
        parts = []
        for q in range(Q):
            parts += [e_ref[0, :, q * T + w:(q + 1) * T], hbuf[:, q * 2 * SHIFT:q * 2 * SHIFT + w]]
        ebuf[k * F:(k + 1) * F, :] = jnp.concatenate(parts, axis=1)
    d_ref[...] = nn(wc_ref[...], ebuf[...])
    for ls in chunks(N, CH):
        pull(F, ls.stop - ls.start, ls, d_ref, lambda rows: n_ref[0, rows, ls], lambda rows: s_ref[0, rows, ls], rstd_ref[0, :, ls],
             gtab, gacc, bacc, e1buf)
    gwi_ref[...] += nt(r1_ref[0], e1buf[0])
    for q in range(Q):
        e1_ref[q] = e1buf[0, :, q * T:(q + 1) * T]

    @pl.when(i == pl.num_programs(0) - 1)
    def _():
        small_ref[...] = small_in[...]
        small_ref[1:2, F:] = gwi_ref[D:D + 1, :]
        small_ref[3:4, :F] = lane_total(gacc[...]) * 0.5
        small_ref[3:4, F:] = lane_total(bacc[...]) * 0.5
        put_pieces(n, pieces_ref, gwi_ref, D, F, 0)


def back(n, Q, flags, eT, below, above, heads, n1, s1, rstd1, r1, wc, gain, small, rows):
    G, F, N = eT.shape
    DE = r1.shape[1]
    sd = jax.ShapeDtypeStruct
    return pl.pallas_call(
        functools.partial(back_kernel, n, Q, G // 2), grid=(G,),
        in_specs=[smem(), seq_spec(1, F, N), fixed(below.shape), fixed(above.shape), fixed(heads.shape), seq_spec(1, F, N), seq_spec(1, F, N),
                  seq_spec(1, 1, N), seq_spec(1, DE, N), fixed(wc.shape), fixed(gain.shape), fixed(small.shape)],
        out_specs=[seq_spec(Q, F, N // Q), fixed((n, WIDE // L, rows, L)), fixed(small.shape)],
        out_shape=[sd((G * Q, F, N // Q), BF), sd((n, WIDE // L, rows, L), F32), sd(small.shape, F32)],
        scratch_shapes=[pltpu.VMEM((3 * F, N), BF), pltpu.VMEM((F, N), F32), pltpu.VMEM((F, L), F32), pltpu.VMEM((F, L), F32),
                        pltpu.VMEM((DE, F), F32), pltpu.VMEM((F, Q * 2 * SHIFT), BF), pltpu.VMEM((F, L), F32),
                        pltpu.VMEM((1, F, N), BF)],
        compiler_params=params(), name="back", cost_estimate=cost(8e9, 25e6),
    )(flags, eT, below, above, heads, n1, s1, rstd1, r1, wc, gain, small)


def wide_bwd_kernel(Q, e_ref, w1_ref, n_ref, s_ref, rstd_ref, c_ref, gain_ref, small_in, *refs):
    dx_ref, small_ref, gtab, gacc, bacc = refs[-5 - Q:-Q]
    d_refs = refs[-Q:]
    D, N = d_refs[0].shape
    i = pl.program_id(0)

    @pl.when(i == 0)
    def _():
        fill_table(gtab, gain_ref[...] * 0.5)
        gacc[...] = jnp.zeros_like(gacc)
        bacc[...] = jnp.zeros_like(bacc)

    def dot(q):
        d_refs[q][...] = nn(w1_ref[...], e_ref[q])

    def pull_wide(q):
        d_ref = d_refs[q]

        def first(j, carry):
            m1, m2 = carry
            rows = rows_at(j)
            ds = d_ref[rows, :] * s_ref[q, rows, :].astype(F32)
            dn = ds * n_ref[q, rows, :].astype(F32)
            gain = spread(gtab, rows, N)
            t = ds * gain
            d_ref[rows, :] = t
            lane_sum(bacc, rows, ds)
            lane_sum(gacc, rows, dn)
            return m1 + fold(t), m2 + fold(dn * gain)

        zero = jnp.zeros((8, N), F32)
        m1, m2 = loop(D // R, first, (zero, zero), 50)
        rstd = rstd_ref[q]
        m1, m2 = total8(m1) * (1.0 / D) * rstd, total8(m2) * (1.0 / D) * rstd

        def second(j, _):
            rows = rows_at(j)
            g = (d_ref[rows, :] * rstd - m1) - n_ref[q, rows, :].astype(F32) * m2
            dx_ref[q, rows, :] = (g + c_ref[q, rows, :].astype(F32)).astype(BF)
            return 0

        loop(D // R, second, 0, 50)

    dot(0)
    for q in range(Q):
        if q + 1 < Q:
            dot(q + 1)
        pull_wide(q)

    @pl.when(i == pl.num_programs(0) - 1)
    def _():
        small_ref[...] = small_in[...]
        small_ref[4:5, :] = small_in[4:5, :] + lane_total(gacc[...]) * 0.5
        small_ref[5:6, :] = small_in[5:6, :] + lane_total(bacc[...]) * 0.5


def wide_bwd(Q, e1, w1, n0, s0, rstd0, cT, gain, small, start=0, steps=None, into=None):
    S, D, N = cT.shape
    F = e1.shape[1]
    steps = S // Q if steps is None else steps
    sd = jax.ShapeDtypeStruct
    at = lambda i: (start + i, 0, 0)
    into = () if into is None else (into,)
    part = lambda rows: pl.BlockSpec((Q, rows, N), at)
    return pl.pallas_call(
        functools.partial(wide_bwd_kernel, Q), grid=(steps,),
        in_specs=[part(F), fixed(w1.shape), part(D), part(D), part(1), part(D),
                  fixed(gain.shape), fixed(small.shape)] + [pl.BlockSpec(memory_space=pl.ANY)] * len(into),
        out_specs=[part(D), fixed(small.shape)],
        out_shape=[sd((S, D, N), BF), sd(small.shape, F32)],
        scratch_shapes=[pltpu.VMEM((D, L), F32)] * 3 + [pltpu.VMEM((D, N), F32)] * Q,
        input_output_aliases={8: 0} if into else {},
        compiler_params=params(), name="wide_bwd", cost_estimate=cost(2e9 * steps, 8.4e6 * steps),
    )(e1, w1, n0, s0, rstd0, cT, gain, small, *into)


def swap(v, bit, n):
    return lax.ppermute(v, "ctx", [(i, i ^ bit) for i in range(n)])


def bits_of(n):
    out, b = [], 1
    while b < n:
        out.append(b)
        b *= 2
    return out


def together(*values):
    return lax.optimization_barrier(values)


def slot_table(n, me):
    diff = jnp.arange(n, dtype=jnp.int32) ^ me
    slots = sum((jnp.where((diff & bit) != 0, n // 2 // bit, 0) for bit in bits_of(n)[1:]), jnp.zeros_like(diff))
    return jnp.concatenate([slots, (me & 1)[None].astype(jnp.int32)])


def split_for(full, bit, me):
    pairs = full.reshape((-1, 2) + full.shape[1:])
    mine = jnp.where((me & bit) == 0, 0, 1)
    keep = lax.dynamic_index_in_dim(pairs, mine, 1, keepdims=False)
    return keep, lax.dynamic_index_in_dim(pairs, 1 - mine, 1, keepdims=False).astype(BF)


def sum_all(v, n):
    for bit in bits_of(n):
        v = v + swap(v, bit, n)
    return v


def to_units(flat, n, M, C, rows=None):
    q, parts, units = unit_plan(n, M, C)
    return jnp.pad(flat.reshape(units, q), ((0, 0), (0, WIDE - q))).reshape(units, WIDE // L, L).transpose(1, 0, 2)


def round_up(v, m=8):
    return -(-v // m) * m


def on_device(block_input, cotangent, w_in, w_conv, w_out, wide_gain, wide_bias, narrow_gain, narrow_bias, dealing):
    slots, seqs, T, D = block_input.shape
    F = narrow_gain.shape[1]
    n = lax.axis_size("ctx")
    half = dealing.shape[0] // 2
    me = lax.axis_index("ctx")
    pair = jnp.sum(jnp.where(dealing[:half] == me, jnp.arange(half, dtype=jnp.int32), 0))
    flags = jnp.stack([pair == 0, pair == half - 1]).astype(jnp.int32)
    up = [(i, (i + 1) % n) for i in range(n)]
    down = [((i + 1) % n, i) for i in range(n)]
    table = slot_table(n, me)
    units_in, units_conv, units_out = (unit_plan(n, m, c)[2] for m, c in ((D, F), (3 * F, F), (F, D)))
    rows_in, rows_rest = round_up(units_in), round_up(units_conv + units_out)

    xT = block_input.transpose(0, 1, 3, 2).reshape(slots * seqs, D, T)
    cT = cotangent.transpose(0, 1, 3, 2).reshape(slots * seqs, D, T)

    piece_in = jnp.pad(to_units(w_in, n, D, F), ((0, 0), (0, rows_in - units_in), (0, 0)))
    piece_rest = jnp.concatenate([to_units(w_conv, n, 3 * F, F), to_units(w_out, n, F, D)], axis=1)
    piece_rest = jnp.pad(piece_rest, ((0, 0), (0, rows_rest - piece_rest.shape[1]), (0, 0)))
    gain0 = wide_gain.reshape(1, D)
    bits = bits_of(n)
    Q = 2
    steps = slots * seqs // Q

    buf_in, buf_rest = piece_in[None], piece_rest[None]
    acts, gain, done, token = (), gain0, 0, None
    far = list(reversed(bits))
    for s, bit in enumerate(far):
        got_in = swap(buf_in, bit, n)
        if s < len(far) - 2:
            got_rest = swap(buf_rest, bit, n)
        count = (steps * (s + 1)) // (len(far) - 1) * Q - done if s < len(far) - 1 else 0
        if count:
            *acts, token = wide_fwd(xT, gain, wide_bias, Q, done, count, acts, token)
            done += count
        if s < len(far) - 1:
            buf_in = jnp.concatenate([buf_in, got_in], axis=0)
        if s < len(far) - 2:
            buf_rest = jnp.concatenate([buf_rest, got_rest], axis=0)
        buf_in, buf_rest, token, gain = together(buf_in, buf_rest, token, gain)
    r1, n0, s0, rstd0 = acts
    got_rest = swap(buf_rest, far[-2], n)
    w1, w1t = unpack_in(n, table, buf_in, got_in, narrow_bias, token, D, F)
    uT, n1, s1, rstd1, tails = front(r1, w1t, narrow_gain, narrow_bias, Q)
    buf_rest, tails = together(jnp.concatenate([buf_rest, got_rest], axis=0), tails)
    below = lax.ppermute(tails[0], "ctx", up)
    above = lax.ppermute(tails[1], "ctx", down)
    got_rest = swap(buf_rest, far[-1], n)
    wc, wct, w3, w3t = unpack_rest(n, table, buf_rest, got_rest, narrow_bias, wide_bias, D, F)
    eT, outT, rest, small, heads = middle(n, Q, flags, uT, below, above, tails, cT, xT, wct, w3, w3t,
                                          narrow_gain, narrow_bias, rows_rest)

    keep, send = split_for(rest, bits[0], me)
    got = swap(send, bits[0], n)
    above = lax.ppermute(heads[0], "ctx", down)
    below = lax.ppermute(heads[1], "ctx", up)
    rest = keep + got.astype(F32)
    keep, send = split_for(rest, bits[1], me)
    send, gain1 = together(send, narrow_gain)
    got = swap(send, bits[1], n)
    e1, into, small = back(n, Q, flags, eT, below, above, heads, n1, s1, rstd1, r1, wc, gain1, small, rows_in)
    rest, small = together(keep + got.astype(F32), small)

    dxT, gain, halves = None, gain0, 2
    for s in range(halves):
        keep_i, send_i = split_for(into, bits[s], me)
        keep_r, send_r = split_for(rest, bits[s + 2], me)
        send_r, send_i, gain = together(send_r, send_i, gain)
        got_r, got_i = swap(send_r, bits[s + 2], n), swap(send_i, bits[s], n)
        dxT, small = wide_bwd(Q, e1, w1, n0, s0, rstd0, cT, gain, small, s * steps // halves, steps // halves, dxT)
        rest, into, small = together(keep_r + got_r.astype(F32), keep_i + got_i.astype(F32), small)
    rest_bits, in_bits = bits[2 + halves:], bits[halves:]
    for j in range(len(bits)):
        got = swap(small, bits[j], n)
        if j < len(rest_bits):
            keep_r, send_r = split_for(rest, rest_bits[j], me)
            rest = keep_r + swap(send_r, rest_bits[j], n).astype(F32)
        if j < len(in_bits):
            keep_i, send_i = split_for(into, in_bits[j], me)
            into = keep_i + swap(send_i, in_bits[j], n).astype(F32)
        small = small + got
        if j < len(in_bits):
            small, rest, into = together(small, rest, into)
    own_rest, own_in = rest[0], into[0]

    def owned(own, at, M, C):
        q, parts, units = unit_plan(n, M, C)
        return own[:, at:at + units].transpose(1, 0, 2).reshape(units, WIDE)[:, :q].reshape(-1)

    back4 = lambda v: v.reshape(slots, seqs, D, T).transpose(0, 1, 3, 2)
    return (back4(outT), back4(dxT), owned(own_in, 0, D, F), owned(own_rest, 0, 3 * F, F), owned(own_rest, units_conv, F, D),
            small[4], jnp.stack([small[5], small[2]]), jnp.stack([small[3, :F], small[0, :F]]),
            jnp.stack([small[1, F:], small[3, F:], small[1, :F], small[0, F:]]))


def solution(mesh):
    whole, flat, copied = P("ctx", None, None, None), P("ctx"), P()
    return jax.shard_map(
        on_device, mesh=mesh,
        in_specs=(whole, whole, flat, flat, flat, copied, copied, copied, copied, copied),
        out_specs=(whole, whole, flat, flat, flat, copied, copied, copied, copied),
        check_vma=False,
    )
```

```python
import functools
import math
import jax
import jax.numpy as jnp
from jax import lax
from jax.experimental import pallas as pl
from jax.experimental.pallas import tpu as pltpu
from jax.sharding import PartitionSpec as P

EPS = 1e-05
BF = jnp.bfloat16
F32 = jnp.float32
L = 128
R = 16
SHIFT = 16
WIDE = 256


def params(mb=52):
    return pltpu.CompilerParams(dimension_semantics=("arbitrary",), vmem_limit_bytes=mb * 1024 * 1024)


def cost(flops, nbytes, trans=0):
    return pl.CostEstimate(flops=int(flops), bytes_accessed=int(nbytes), transcendentals=int(trans))


def rows_at(i):
    return pl.ds(pl.multiple_of(i * R, R), R)


def loop(n, body, init, unroll=25):
    return lax.fori_loop(0, n, body, init, unroll=min(n, unroll))


def fold(v):
    return v[:8] + v[8:]


def total8(v):
    return jnp.sum(v, axis=0, keepdims=True)


def nt(a, b):
    return lax.dot_general(a, b, (((1,), (1,)), ((), ())), preferred_element_type=F32)


def nn(a, b):
    return jnp.dot(a, b, preferred_element_type=F32)


def chunks(N, width):
    return [slice(l, min(N, l + width)) for l in range(0, N, width)]


def spread(table, rows, w):
    return jnp.concatenate([table[rows, :]] * (-(-w // L)), axis=1)[:, :w]


def fill_table(table, row):
    table[...] = jnp.broadcast_to(row, (L, row.shape[1])).T


def col_stats(read, chans, N, unroll=25):
    acc = loop(chans // R, lambda i, a: a + fold(read(i)), jnp.zeros((8, N), F32), unroll)
    mean = total8(acc) * (1.0 / chans)

    def second(i, a):
        cen = read(i) - mean
        return a + fold(cen * cen)

    acc = loop(chans // R, second, jnp.zeros((8, N), F32), unroll)
    return mean, lax.rsqrt(total8(acc) * (1.0 / chans) + EPS)


def gate(h):
    t = jnp.tanh(h)
    r = h + h * t
    return r, (1.0 + t) + (r - r * t)


def lane_sum(acc_ref, rows, v):
    N = v.shape[1]
    full = N // L * L
    tot = v[:, :L]
    for j in range(L, full, L):
        tot = tot + v[:, j:j + L]
    if full < N:
        tot = tot + jnp.concatenate([v[:, full:], jnp.zeros((v.shape[0], L - (N - full)), v.dtype)], axis=1)
    acc_ref[rows, :] += tot


def seq_spec(B, rows, N):
    return pl.BlockSpec((B, rows, N), lambda i: (i, 0, 0))


def fixed(shape):
    zero = (0,) * len(shape)
    return pl.BlockSpec(shape, lambda i: zero, pipeline_mode=pl.Buffered(1))


def smem():
    return pl.BlockSpec(memory_space=pltpu.SMEM)


def vmem():
    return pl.BlockSpec(memory_space=pltpu.VMEM)


def lane_total(acc):
    return jnp.sum(acc.T, axis=0, keepdims=True)


def unit_plan(n, M, C):
    size = M * C // n
    whole = math.gcd(size, C)
    q = max(d for d in range(1, WIDE + 1) if whole % d == 0)
    return q, C // q, size // q


def unit_slices(n, M, C):
    q, parts, units = unit_plan(n, M, C)
    out = []
    for p in range(n):
        for h in range(parts):
            lo = -((h - units * p) // parts)
            hi = -((h - units * (p + 1)) // parts)
            if hi > lo:
                out.append((p, h, lo, hi - lo, lo * parts + h - units * p))
    return out


def strided(start, size, step):
    return pl.ds(start, size, stride=step) if step > 1 else pl.ds(start, size)


def planes(q):
    return [(j, j * L, min(q - j * L, L)) for j in range(-(-q // L))]


def put_matrix(n, mat_ref, f32_ref, off):
    M, C = mat_ref.shape
    q, parts, _ = unit_plan(n, M, C)
    for p, h, lo, cnt, u in unit_slices(n, M, C):
        for j, at, w in planes(q):
            mat_ref[lo:lo + cnt, h * q + at:h * q + at + w] = f32_ref[p, j, strided(off + u, cnt, parts), :][:, :w]


def put_pieces(n, out_ref, mat_ref, M, C, off):
    q, parts, _ = unit_plan(n, M, C)
    for p, h, lo, cnt, u in unit_slices(n, M, C):
        for j, at, w in planes(q):
            v = mat_ref[lo:lo + cnt, h * q + at:h * q + at + w]
            if w < L:
                v = jnp.concatenate([v, jnp.zeros((cnt, L - w), v.dtype)], axis=1)
            out_ref[p, j, strided(off + u, cnt, parts), :] = v


def flipped(mat):
    C = mat.shape[1]
    eye = (lax.broadcasted_iota(jnp.int32, (C, C), 0) == lax.broadcasted_iota(jnp.int32, (C, C), 1)).astype(BF)
    return nt(eye, mat).astype(BF)


def ordered(n, slots_ref, a_ref, b_ref, f32_ref):
    odd = slots_ref[n]
    for p in range(n):
        slot = slots_ref[p]
        piece = jnp.where(odd == p % 2, a_ref[slot].astype(F32), b_ref[slot].astype(F32))
        f32_ref[p] = piece


def bias_block(row):
    v = jnp.broadcast_to(row, (L, row.shape[1])).T[:, :R]
    hi = v.astype(BF)
    rest = v - hi.astype(F32)
    mid = rest.astype(BF)
    low = (rest - mid.astype(F32)).astype(BF)
    col = lax.broadcasted_iota(jnp.int32, v.shape, 1)
    zero = jnp.zeros_like(v)
    return jnp.where(col == 0, hi.astype(F32), jnp.where(col == 1, mid.astype(F32), jnp.where(col == 2, low.astype(F32), zero))).astype(BF)


def unpack_in_kernel(n, slots_ref, a_ref, b_ref, bias_ref, token_ref, w1_ref, w1t_ref, f32_ref, mat_ref):
    ordered(n, slots_ref, a_ref, b_ref, f32_ref)
    put_matrix(n, mat_ref, f32_ref, 0)
    D, F = mat_ref.shape
    w1_ref[...] = mat_ref[...].astype(BF)
    w1t_ref[:, :D] = flipped(w1_ref[...])
    w1t_ref[:, D:] = bias_block(bias_ref[0:1, :])


def unpack_in(n, slots, a, b, bias, token, D, F):
    sd = jax.ShapeDtypeStruct
    return pl.pallas_call(
        functools.partial(unpack_in_kernel, n),
        in_specs=[smem()] + [vmem()] * 3 + [pl.BlockSpec(memory_space=pl.ANY)], out_specs=[vmem(), vmem()],
        out_shape=[sd((D, F), BF), sd((F, D + R), BF)],
        scratch_shapes=[pltpu.VMEM((n,) + a.shape[1:], F32), pltpu.VMEM((D, F), F32)],
        compiler_params=pltpu.CompilerParams(vmem_limit_bytes=40 * 1024 * 1024), name="unpack_in",
        cost_estimate=cost(1e9, 6e6),
    )(slots, a, b, bias, token)


def unpack_rest_kernel(n, slots_ref, a_ref, b_ref, bias_ref, wide_ref, wc_ref, wct_ref, w3_ref, w3t_ref, f32_ref, matc_ref, mat3_ref):
    F, D = mat3_ref.shape
    ordered(n, slots_ref, a_ref, b_ref, f32_ref)
    put_matrix(n, matc_ref, f32_ref, 0)
    put_matrix(n, mat3_ref, f32_ref, unit_plan(n, 3 * F, F)[2])
    for k in range(3):
        tap = matc_ref[k * F:(k + 1) * F, :].astype(BF)
        wc_ref[:, k * F:(k + 1) * F] = tap
        wct_ref[:, k * F:(k + 1) * F] = flipped(tap)
    wct_ref[:, 3 * F:] = bias_block(bias_ref[2:3, :])
    w3_ref[...] = mat3_ref[...].astype(BF)
    w3t_ref[:, :F] = flipped(w3_ref[...])
    w3t_ref[:, F:] = bias_block(wide_ref[1:2, :])


def unpack_rest(n, slots, a, b, bias, wide_bias, D, F):
    sd = jax.ShapeDtypeStruct
    return pl.pallas_call(
        functools.partial(unpack_rest_kernel, n),
        in_specs=[smem()] + [vmem()] * 4, out_specs=[vmem()] * 4,
        out_shape=[sd((F, 3 * F), BF), sd((F, 3 * F + R), BF), sd((F, D), BF), sd((D, F + R), BF)],
        scratch_shapes=[pltpu.VMEM((n,) + a.shape[1:], F32), pltpu.VMEM((3 * F, F), F32), pltpu.VMEM((F, D), F32)],
        compiler_params=pltpu.CompilerParams(vmem_limit_bytes=40 * 1024 * 1024), name="unpack_rest",
        cost_estimate=cost(2e9, 14e6),
    )(slots, a, b, bias, wide_bias)


def rim_store(ref, i, steps, cols):
    for s in range(2 * steps):
        @pl.when(i == s)
        def _(s=s):
            w = cols[0].shape[1]
            for q, v in enumerate(cols):
                at = (s % steps * len(cols) + q) * w
                ref[s // steps, :, at:at + w] = v


def rim_load(buf, i, steps, first, second):
    w = buf.shape[1]
    for s in range(2 * steps):
        @pl.when(i == s)
        def _(s=s):
            src = first() if s < steps else second()
            buf[...] = src[:, s % steps * w:(s % steps + 1) * w]


def wide_fwd_kernel(Q, start, x_ref, gain_ref, bias_ref, *refs):
    r1_ref, n0_ref, s0_ref, rstd_ref, token_ref, gtab, btab, rbuf = refs[-8:]
    D, N = x_ref.shape[1:]
    i = pl.program_id(0)

    @pl.when(i == 0)
    def _():
        fill_table(gtab, gain_ref[...] * 0.5)
        fill_table(btab, bias_ref[0:1, :] * 0.5)
        token_ref[...] = jnp.zeros_like(token_ref)

    read = lambda j: x_ref[0, rows_at(j), :].astype(F32)
    mean, rstd = col_stats(read, D, N, 10)
    rstd_ref[0] = rstd

    def act(j, _):
        rows = rows_at(j)
        n = (read(j) - mean) * rstd
        r, d = gate(n * spread(gtab, rows, N) + spread(btab, rows, N))
        n0_ref[0, rows, :] = n.astype(BF)
        s0_ref[0, rows, :] = d.astype(BF)
        rbuf[rows, :] = r.astype(BF)
        return 0

    loop(D // R, act, 0, 10)
    for q in range(Q):
        @pl.when(lax.rem(start + i, Q) == q)
        def _(q=q):
            r1_ref[0, :D, q * N:(q + 1) * N] = rbuf[...]
            r1_ref[0, D:, q * N:(q + 1) * N] = jnp.ones((r1_ref.shape[1] - D, N), BF)


def wide_fwd(xT, gain, bias, Q, start=0, steps=None, into=None, token=None):
    S, D, N = xT.shape
    steps = S if steps is None else steps
    sd = jax.ShapeDtypeStruct
    at = lambda i: (start + i, 0, 0)
    into = tuple(into or ())
    token = () if token is None else (token,)
    one = lambda rows: pl.BlockSpec((1, rows, N), at)
    return pl.pallas_call(
        functools.partial(wide_fwd_kernel, Q, start), grid=(steps,),
        in_specs=[one(D), fixed((1, D)), fixed((2, D))] + [pl.BlockSpec(memory_space=pl.ANY)] * len(into + token),
        out_specs=[pl.BlockSpec((1, D + R, Q * N), lambda i: ((start + i) // Q, 0, 0)), one(D), one(D), one(1), fixed((8, L))],
        out_shape=[sd((S // Q, D + R, Q * N), BF), sd((S, D, N), BF), sd((S, D, N), BF), sd((S, 1, N), F32), sd((8, L), F32)],
        scratch_shapes=[pltpu.VMEM((D, L), F32)] * 2 + [pltpu.VMEM((D, N), BF)],
        input_output_aliases={3 + j: j for j in range(len(into))},
        compiler_params=params(52), name="wide_fwd", cost_estimate=cost(1e9 * steps, 5.5e6 * steps),
    )(xT, gain, bias, *into, *token)


CH = 384


def front_kernel(Q, steps, r1_ref, w1t_ref, gain_ref, bias_ref, u_ref, n_ref, s_ref, rstd_ref, tail_ref, h_ref, gtab, btab):
    F, N = h_ref.shape
    T = N // Q
    i = pl.program_id(0)

    @pl.when(i == 0)
    def _():
        fill_table(gtab, gain_ref[0:1, :] * 0.5)
        fill_table(btab, bias_ref[1:2, :] * 0.5)

    h_ref[...] = nn(w1t_ref[...], r1_ref[0])
    for ls in chunks(N, CH):
        W = ls.stop - ls.start
        read = lambda j: h_ref[rows_at(j), ls]
        mean, rstd = col_stats(read, F, W)
        rstd_ref[0, :, ls] = rstd

        def act(j, _):
            rows = rows_at(j)
            n = (read(j) - mean) * rstd
            r, d = gate(n * spread(gtab, rows, W) + spread(btab, rows, W))
            u_ref[0, rows, ls] = r.astype(BF)
            n_ref[0, rows, ls] = n.astype(BF)
            s_ref[0, rows, ls] = d.astype(BF)
            return 0

        loop(F // R, act, 0)
    rim_store(tail_ref, i, steps, [u_ref[0, :, (q + 1) * T - 2 * SHIFT:(q + 1) * T] for q in range(Q)])


def front(r1, w1t, gain, bias, Q):
    G, DE, N = r1.shape
    F = w1t.shape[0]
    sd = jax.ShapeDtypeStruct
    rim = (2, F, G // 2 * Q * 2 * SHIFT)
    return pl.pallas_call(
        functools.partial(front_kernel, Q, G // 2), grid=(G,),
        in_specs=[seq_spec(1, DE, N), fixed(w1t.shape), fixed(gain.shape), fixed(bias.shape)],
        out_specs=[seq_spec(1, F, N)] * 3 + [seq_spec(1, 1, N), fixed(rim)],
        out_shape=[sd((G, F, N), BF)] * 3 + [sd((G, 1, N), F32), sd(rim, BF)],
        scratch_shapes=[pltpu.VMEM((F, N), F32)] + [pltpu.VMEM((F, L), F32)] * 2,
        compiler_params=params(52), name="front", cost_estimate=cost(4e9, 19e6),
    )(r1, w1t, gain, bias)


def pull(F, W, ls, d_ref, n_at, s_at, rstd, gtab, gacc, bacc, e_ref, unroll=25):
    def first(j, carry):
        m1, m2 = carry
        rows = rows_at(j)
        ds = d_ref[rows, ls] * s_at(rows).astype(F32)
        dn = ds * n_at(rows).astype(F32)
        gain = spread(gtab, rows, W)
        t = ds * gain
        d_ref[rows, ls] = t
        lane_sum(bacc, rows, ds)
        lane_sum(gacc, rows, dn)
        return m1 + fold(t), m2 + fold(dn * gain)

    zero = jnp.zeros((8, W), F32)
    m1, m2 = loop(F // R, first, (zero, zero), unroll)
    m1, m2 = total8(m1) * (1.0 / F) * rstd, total8(m2) * (1.0 / F) * rstd

    def second(j, _):
        rows = rows_at(j)
        e_ref[0, rows, ls] = ((d_ref[rows, ls] * rstd - m1) - n_at(rows).astype(F32) * m2).astype(BF)
        return 0

    loop(F // R, second, 0, unroll)


def middle_kernel(n, Q, steps, flags_ref, u_ref, below_ref, above_ref, tail_ref, c_ref, x_ref, wct_ref, w3_ref, w3t_ref,
                  gain_ref, bias_ref, e_ref, out_ref, pieces_ref, small_ref, head_ref,
                  ubuf, cbuf, rbuf, h_ref, d_ref, n_ref, s_ref, o_ref, gacc, bacc, gwo_ref, gwc_ref, hbuf, gtab, btab, pieces32):
    F, N = h_ref.shape
    T = N // Q
    D = c_ref.shape[1]
    i = pl.program_id(0)

    @pl.when(i == 0)
    def _():
        fill_table(gtab, gain_ref[1:2, :] * 0.5)
        fill_table(btab, bias_ref[3:4, :] * 0.5)
        ubuf[3 * F:, :] = jnp.ones((R, N), BF)
        rbuf[F:, :] = jnp.ones((R, N), BF)
        gwo_ref[...] = jnp.zeros_like(gwo_ref)
        gwc_ref[...] = jnp.zeros_like(gwc_ref)
        gacc[...] = jnp.zeros_like(gacc)
        bacc[...] = jnp.zeros_like(bacc)

    rim_load(hbuf, i, steps,
             lambda: jnp.where(flags_ref[0] == 1, jnp.zeros_like(below_ref[...]), below_ref[...]),
             lambda: jnp.where(flags_ref[1] == 1, tail_ref[0], above_ref[...]))
    ubuf[:F, :] = u_ref[0]
    for k in (1, 2):
        w = k * SHIFT
        parts = []
        for q in range(Q):
            parts += [hbuf[:, (q + 1) * 2 * SHIFT - w:(q + 1) * 2 * SHIFT], u_ref[0, :, q * T:(q + 1) * T - w]]
        ubuf[k * F:(k + 1) * F, :] = jnp.concatenate(parts, axis=1)
    for q in range(Q):
        cbuf[:, q * T:(q + 1) * T] = c_ref[q]
    h_ref[...] = nn(wct_ref[...], ubuf[...])
    d_ref[...] = nn(w3_ref[...], cbuf[...])
    rstds = []
    for ls in chunks(N, CH):
        W = ls.stop - ls.start
        read = lambda j: h_ref[rows_at(j), ls]
        mean, rstd = col_stats(read, F, W)
        rstds.append(rstd)

        def act(j, _):
            rows = rows_at(j)
            v = (read(j) - mean) * rstd
            r, d = gate(v * spread(gtab, rows, W) + spread(btab, rows, W))
            rbuf[rows, ls] = r.astype(BF)
            n_ref[rows, ls] = v
            s_ref[rows, ls] = d
            return 0

        loop(F // R, act, 0)
    o_ref[...] = nn(w3t_ref[...], rbuf[...])
    gwo_ref[...] += nt(rbuf[...], cbuf[...])
    for ls, rstd in zip(chunks(N, CH), rstds):
        pull(F, ls.stop - ls.start, ls, d_ref, lambda rows: n_ref[rows, ls], lambda rows: s_ref[rows, ls], rstd, gtab, gacc, bacc, e_ref)
    gwc_ref[...] += nt(ubuf[...], e_ref[0])
    for q in range(Q):
        def emit(j, _):
            rows = rows_at(j)
            out_ref[q, rows, :] = (o_ref[rows, q * T:(q + 1) * T] + x_ref[q, rows, :].astype(F32)).astype(BF)
            return 0

        loop(D // R, emit, 0, 50)
    rim_store(head_ref, i, steps, [e_ref[0, :, q * T:q * T + 2 * SHIFT] for q in range(Q)])

    @pl.when(i == pl.num_programs(0) - 1)
    def _():
        small_ref[...] = jnp.zeros_like(small_ref)
        small_ref[0:1, :F] = lane_total(gacc[...]) * 0.5
        small_ref[0:1, F:] = lane_total(bacc[...]) * 0.5
        small_ref[1:2, :F] = gwc_ref[3 * F:3 * F + 1, :]
        small_ref[2:3, :] = gwo_ref[F:F + 1, :]
        put_pieces(n, pieces32, gwc_ref, 3 * F, F, 0)
        put_pieces(n, pieces32, gwo_ref, F, D, unit_plan(n, 3 * F, F)[2])
        pieces_ref[...] = pieces32[...].astype(BF)


def middle(n, Q, flags, uT, below, above, tails, cT, xT, wct, w3, w3t, gain, bias, rows):
    G, F, N = uT.shape
    S, D, T = cT.shape
    sd = jax.ShapeDtypeStruct
    return pl.pallas_call(
        functools.partial(middle_kernel, n, Q, G // 2), grid=(G,),
        in_specs=[smem(), seq_spec(1, F, N), fixed(below.shape), fixed(above.shape), fixed(tails.shape), seq_spec(Q, D, T), seq_spec(Q, D, T),
                  fixed(wct.shape), fixed(w3.shape), fixed(w3t.shape), fixed(gain.shape), fixed(bias.shape)],
        out_specs=[seq_spec(1, F, N), seq_spec(Q, D, T), fixed((n, WIDE // L, rows, L)), fixed((8, D)), fixed(tails.shape)],
        out_shape=[sd((G, F, N), BF), sd((S, D, T), BF), sd((n, WIDE // L, rows, L), BF), sd((8, D), F32), sd(tails.shape, BF)],
        scratch_shapes=[pltpu.VMEM((3 * F + R, N), BF), pltpu.VMEM((D, N), BF), pltpu.VMEM((F + R, N), BF), pltpu.VMEM((F, N), F32),
                        pltpu.VMEM((F, N), F32), pltpu.VMEM((F, N), F32), pltpu.VMEM((F, N), F32), pltpu.VMEM((D, N), F32),
                        pltpu.VMEM((F, L), F32), pltpu.VMEM((F, L), F32), pltpu.VMEM((F + R, D), F32),
                        pltpu.VMEM((3 * F + R, F), F32), pltpu.VMEM((F, Q * 2 * SHIFT), BF), pltpu.VMEM((F, L), F32), pltpu.VMEM((F, L), F32),
                        pltpu.VMEM((n, WIDE // L, rows, L), F32)],
        compiler_params=params(46 if n <= 32 else 60), name="middle", cost_estimate=cost(18e9, 36e6),
    )(flags, uT, below, above, tails, cT, xT, wct, w3, w3t, gain, bias)


def back_kernel(n, Q, steps, flags_ref, e_ref, below_ref, above_ref, head_ref, n_ref, s_ref, rstd_ref, r1_ref, wc_ref, gain_ref,
                small_in, e1_ref, pieces_ref, small_ref, ebuf, d_ref, gacc, bacc, gwi_ref, hbuf, gtab, e1buf, pieces32):
    F, N = d_ref.shape
    T = N // Q
    D = gwi_ref.shape[0] - R
    i = pl.program_id(0)

    @pl.when(i == 0)
    def _():
        fill_table(gtab, gain_ref[0:1, :] * 0.5)
        gwi_ref[...] = jnp.zeros_like(gwi_ref)
        gacc[...] = jnp.zeros_like(gacc)
        bacc[...] = jnp.zeros_like(bacc)

    rim_load(hbuf, i, steps,
             lambda: jnp.where(flags_ref[1] == 1, head_ref[1], above_ref[...]),
             lambda: jnp.where(flags_ref[0] == 1, jnp.zeros_like(below_ref[...]), below_ref[...]))
    ebuf[:F, :] = e_ref[0]
    for k in (1, 2):
        w = k * SHIFT
        parts = []
        for q in range(Q):
            parts += [e_ref[0, :, q * T + w:(q + 1) * T], hbuf[:, q * 2 * SHIFT:q * 2 * SHIFT + w]]
        ebuf[k * F:(k + 1) * F, :] = jnp.concatenate(parts, axis=1)
    d_ref[...] = nn(wc_ref[...], ebuf[...])
    for ls in chunks(N, CH):
        pull(F, ls.stop - ls.start, ls, d_ref, lambda rows: n_ref[0, rows, ls], lambda rows: s_ref[0, rows, ls], rstd_ref[0, :, ls],
             gtab, gacc, bacc, e1buf)
    gwi_ref[...] += nt(r1_ref[0], e1buf[0])
    for q in range(Q):
        e1_ref[q] = e1buf[0, :, q * T:(q + 1) * T]

    @pl.when(i == pl.num_programs(0) - 1)
    def _():
        small_ref[...] = small_in[...]
        small_ref[1:2, F:] = gwi_ref[D:D + 1, :]
        small_ref[3:4, :F] = lane_total(gacc[...]) * 0.5
        small_ref[3:4, F:] = lane_total(bacc[...]) * 0.5
        put_pieces(n, pieces32, gwi_ref, D, F, 0)
        pieces_ref[...] = pieces32[...].astype(BF)


def back(n, Q, flags, eT, below, above, heads, n1, s1, rstd1, r1, wc, gain, small, rows):
    G, F, N = eT.shape
    DE = r1.shape[1]
    sd = jax.ShapeDtypeStruct
    return pl.pallas_call(
        functools.partial(back_kernel, n, Q, G // 2), grid=(G,),
        in_specs=[smem(), seq_spec(1, F, N), fixed(below.shape), fixed(above.shape), fixed(heads.shape), seq_spec(1, F, N), seq_spec(1, F, N),
                  seq_spec(1, 1, N), seq_spec(1, DE, N), fixed(wc.shape), fixed(gain.shape), fixed(small.shape)],
        out_specs=[seq_spec(Q, F, N // Q), fixed((n, WIDE // L, rows, L)), fixed(small.shape)],
        out_shape=[sd((G * Q, F, N // Q), BF), sd((n, WIDE // L, rows, L), BF), sd(small.shape, F32)],
        scratch_shapes=[pltpu.VMEM((3 * F, N), BF), pltpu.VMEM((F, N), F32), pltpu.VMEM((F, L), F32), pltpu.VMEM((F, L), F32),
                        pltpu.VMEM((DE, F), F32), pltpu.VMEM((F, Q * 2 * SHIFT), BF), pltpu.VMEM((F, L), F32),
                        pltpu.VMEM((1, F, N), BF), pltpu.VMEM((n, WIDE // L, rows, L), F32)],
        compiler_params=params(52), name="back", cost_estimate=cost(8e9, 25e6),
    )(flags, eT, below, above, heads, n1, s1, rstd1, r1, wc, gain, small)


def wide_bwd_kernel(Q, e_ref, w1_ref, n_ref, s_ref, rstd_ref, c_ref, gain_ref, small_in, *refs):
    dx_ref, small_ref, gtab, gacc, bacc = refs[-5 - Q:-Q]
    d_refs = refs[-Q:]
    D, N = d_refs[0].shape
    i = pl.program_id(0)

    @pl.when(i == 0)
    def _():
        fill_table(gtab, gain_ref[...] * 0.5)
        gacc[...] = jnp.zeros_like(gacc)
        bacc[...] = jnp.zeros_like(bacc)

    def dot(q):
        d_refs[q][...] = nn(w1_ref[...], e_ref[q])

    def pull_wide(q):
        d_ref = d_refs[q]

        def first(j, carry):
            m1, m2 = carry
            rows = rows_at(j)
            ds = d_ref[rows, :] * s_ref[q, rows, :].astype(F32)
            dn = ds * n_ref[q, rows, :].astype(F32)
            gain = spread(gtab, rows, N)
            t = ds * gain
            d_ref[rows, :] = t
            lane_sum(bacc, rows, ds)
            lane_sum(gacc, rows, dn)
            return m1 + fold(t), m2 + fold(dn * gain)

        zero = jnp.zeros((8, N), F32)
        m1, m2 = loop(D // R, first, (zero, zero), 50)
        rstd = rstd_ref[q]
        m1, m2 = total8(m1) * (1.0 / D) * rstd, total8(m2) * (1.0 / D) * rstd

        def second(j, _):
            rows = rows_at(j)
            g = (d_ref[rows, :] * rstd - m1) - n_ref[q, rows, :].astype(F32) * m2
            dx_ref[q, rows, :] = (g + c_ref[q, rows, :].astype(F32)).astype(BF)
            return 0

        loop(D // R, second, 0, 50)

    dot(0)
    for q in range(Q):
        if q + 1 < Q:
            dot(q + 1)
        pull_wide(q)

    @pl.when(i == pl.num_programs(0) - 1)
    def _():
        small_ref[...] = small_in[...]
        small_ref[4:5, :] = small_in[4:5, :] + lane_total(gacc[...]) * 0.5
        small_ref[5:6, :] = small_in[5:6, :] + lane_total(bacc[...]) * 0.5


def wide_bwd(Q, e1, w1, n0, s0, rstd0, cT, gain, small, start=0, steps=None, into=None):
    S, D, N = cT.shape
    F = e1.shape[1]
    steps = S // Q if steps is None else steps
    sd = jax.ShapeDtypeStruct
    at = lambda i: (start + i, 0, 0)
    into = () if into is None else (into,)
    part = lambda rows: pl.BlockSpec((Q, rows, N), at)
    return pl.pallas_call(
        functools.partial(wide_bwd_kernel, Q), grid=(steps,),
        in_specs=[part(F), fixed(w1.shape), part(D), part(D), part(1), part(D),
                  fixed(gain.shape), fixed(small.shape)] + [pl.BlockSpec(memory_space=pl.ANY)] * len(into),
        out_specs=[part(D), fixed(small.shape)],
        out_shape=[sd((S, D, N), BF), sd(small.shape, F32)],
        scratch_shapes=[pltpu.VMEM((D, L), F32)] * 3 + [pltpu.VMEM((D, N), F32)] * Q,
        input_output_aliases={8: 0} if into else {},
        compiler_params=params(52), name="wide_bwd", cost_estimate=cost(2e9 * steps, 8.4e6 * steps),
    )(e1, w1, n0, s0, rstd0, cT, gain, small, *into)


def swap(v, bit, n):
    return lax.ppermute(v, "ctx", [(i, i ^ bit) for i in range(n)])


def bits_of(n):
    out, b = [], 1
    while b < n:
        out.append(b)
        b *= 2
    return out


def together(*values):
    return lax.optimization_barrier(values)


def slot_table(n, me):
    diff = jnp.arange(n, dtype=jnp.int32) ^ me
    slots = sum((jnp.where((diff & bit) != 0, n // 2 // bit, 0) for bit in bits_of(n)[1:]), jnp.zeros_like(diff))
    return jnp.concatenate([slots, (me & 1)[None].astype(jnp.int32)])


def split_for(full, bit, me):
    pairs = full.reshape((-1, 2) + full.shape[1:])
    mine = jnp.where((me & bit) == 0, 0, 1)
    keep = lax.dynamic_index_in_dim(pairs, mine, 1, keepdims=False)
    return keep, lax.dynamic_index_in_dim(pairs, 1 - mine, 1, keepdims=False).astype(BF)


def sum_all(v, n):
    for bit in bits_of(n):
        v = v + swap(v, bit, n)
    return v


def to_units(flat, n, M, C, rows=None):
    q, parts, units = unit_plan(n, M, C)
    return jnp.pad(flat.reshape(units, q), ((0, 0), (0, WIDE - q))).reshape(units, WIDE // L, L).transpose(1, 0, 2)


def round_up(v, m=8):
    return -(-v // m) * m


def on_device(block_input, cotangent, w_in, w_conv, w_out, wide_gain, wide_bias, narrow_gain, narrow_bias, dealing):
    slots, seqs, T, D = block_input.shape
    F = narrow_gain.shape[1]
    n = lax.axis_size("ctx")
    half = dealing.shape[0] // 2
    me = lax.axis_index("ctx")
    pair = jnp.sum(jnp.where(dealing[:half] == me, jnp.arange(half, dtype=jnp.int32), 0))
    flags = jnp.stack([pair == 0, pair == half - 1]).astype(jnp.int32)
    up = [(i, (i + 1) % n) for i in range(n)]
    down = [((i + 1) % n, i) for i in range(n)]
    table = slot_table(n, me)
    units_in, units_conv, units_out = (unit_plan(n, m, c)[2] for m, c in ((D, F), (3 * F, F), (F, D)))
    rows_in, rows_rest = round_up(units_in), round_up(units_conv + units_out)

    xT = block_input.transpose(0, 1, 3, 2).reshape(slots * seqs, D, T)
    cT = cotangent.transpose(0, 1, 3, 2).reshape(slots * seqs, D, T)

    piece_in = jnp.pad(to_units(w_in, n, D, F), ((0, 0), (0, rows_in - units_in), (0, 0)))
    piece_rest = jnp.concatenate([to_units(w_conv, n, 3 * F, F), to_units(w_out, n, F, D)], axis=1)
    piece_rest = jnp.pad(piece_rest, ((0, 0), (0, rows_rest - piece_rest.shape[1]), (0, 0)))
    gain0 = wide_gain.reshape(1, D)
    bits = bits_of(n)
    Q = 2
    steps = slots * seqs // Q

    buf_in, buf_rest = piece_in[None], piece_rest[None]
    acts, gain, done, token = (), gain0, 0, None
    far = list(reversed(bits))
    for s, bit in enumerate(far):
        got_in = swap(buf_in, bit, n)
        if s < len(far) - 2:
            got_rest = swap(buf_rest, bit, n)
        count = (steps * (s + 1)) // (len(far) - 1) * Q - done if s < len(far) - 1 else 0
        if count:
            *acts, token = wide_fwd(xT, gain, wide_bias, Q, done, count, acts, token)
            done += count
        if s < len(far) - 1:
            buf_in = jnp.concatenate([buf_in, got_in], axis=0)
        if s < len(far) - 2:
            buf_rest = jnp.concatenate([buf_rest, got_rest], axis=0)
        buf_in, buf_rest, token, gain = together(buf_in, buf_rest, token, gain)
    r1, n0, s0, rstd0 = acts
    got_rest = swap(buf_rest, far[-2], n)
    w1, w1t = unpack_in(n, table, buf_in, got_in, narrow_bias, token, D, F)
    uT, n1, s1, rstd1, tails = front(r1, w1t, narrow_gain, narrow_bias, Q)
    buf_rest, tails = together(jnp.concatenate([buf_rest, got_rest], axis=0), tails)
    below = lax.ppermute(tails[0], "ctx", up)
    above = lax.ppermute(tails[1], "ctx", down)
    got_rest = swap(buf_rest, far[-1], n)
    wc, wct, w3, w3t = unpack_rest(n, table, buf_rest, got_rest, narrow_bias, wide_bias, D, F)
    eT, outT, rest, small, heads = middle(n, Q, flags, uT, below, above, tails, cT, xT, wct, w3, w3t,
                                          narrow_gain, narrow_bias, rows_rest)

    keep, send = split_for(rest, bits[0], me)
    got = swap(send, bits[0], n)
    above = lax.ppermute(heads[0], "ctx", down)
    below = lax.ppermute(heads[1], "ctx", up)
    rest = keep + got.astype(F32)
    keep, send = split_for(rest, bits[1], me)
    send, gain1 = together(send, narrow_gain)
    got = swap(send, bits[1], n)
    e1, into, small = back(n, Q, flags, eT, below, above, heads, n1, s1, rstd1, r1, wc, gain1, small, rows_in)
    rest, small = together(keep + got.astype(F32), small)

    dxT, gain, halves = None, gain0, 2
    for s in range(halves):
        keep_i, send_i = split_for(into, bits[s], me)
        keep_r, send_r = split_for(rest, bits[s + 2], me)
        send_r, send_i, gain = together(send_r, send_i, gain)
        got_r, got_i = swap(send_r, bits[s + 2], n), swap(send_i, bits[s], n)
        dxT, small = wide_bwd(Q, e1, w1, n0, s0, rstd0, cT, gain, small, s * steps // halves, steps // halves, dxT)
        rest, into, small = together(keep_r + got_r.astype(F32), keep_i + got_i.astype(F32), small)
    rest_bits, in_bits = bits[2 + halves:], bits[halves:]
    for j in range(len(bits)):
        got = swap(small, bits[j], n)
        if j < len(rest_bits):
            keep_r, send_r = split_for(rest, rest_bits[j], me)
            rest = keep_r + swap(send_r, rest_bits[j], n).astype(F32)
        if j < len(in_bits):
            keep_i, send_i = split_for(into, in_bits[j], me)
            into = keep_i + swap(send_i, in_bits[j], n).astype(F32)
        small = small + got
        if j < len(in_bits):
            small, rest, into = together(small, rest, into)
    own_rest, own_in = rest[0], into[0]

    def owned(own, at, M, C):
        q, parts, units = unit_plan(n, M, C)
        return own[:, at:at + units].transpose(1, 0, 2).reshape(units, WIDE)[:, :q].reshape(-1)

    back4 = lambda v: v.reshape(slots, seqs, D, T).transpose(0, 1, 3, 2)
    return (back4(outT), back4(dxT), owned(own_in, 0, D, F), owned(own_rest, 0, 3 * F, F), owned(own_rest, units_conv, F, D),
            small[4], jnp.stack([small[5], small[2]]), jnp.stack([small[3, :F], small[0, :F]]),
            jnp.stack([small[1, F:], small[3, F:], small[1, :F], small[0, F:]]))


def solution(mesh):
    whole, flat, copied = P("ctx", None, None, None), P("ctx"), P()
    return jax.shard_map(
        on_device, mesh=mesh,
        in_specs=(whole, whole, flat, flat, flat, copied, copied, copied, copied, copied),
        out_specs=(whole, whole, flat, flat, flat, copied, copied, copied, copied),
        check_vma=False,
    )
```

```python
import functools
import math
import jax
import jax.numpy as jnp
from jax import lax
from jax.experimental import pallas as pl
from jax.experimental.pallas import tpu as pltpu
from jax.sharding import PartitionSpec as P

EPS = 1e-05
BF = jnp.bfloat16
F32 = jnp.float32
L = 128
R = 16
SHIFT = 16
WIDE = 256


def params(mb=52):
    return pltpu.CompilerParams(dimension_semantics=("arbitrary",), vmem_limit_bytes=mb * 1024 * 1024)


def cost(flops, nbytes, trans=0):
    return pl.CostEstimate(flops=int(flops), bytes_accessed=int(nbytes), transcendentals=int(trans))


def rows_at(i):
    return pl.ds(pl.multiple_of(i * R, R), R)


def loop(n, body, init, unroll=25):
    return lax.fori_loop(0, n, body, init, unroll=min(n, unroll))


def fold(v):
    return v[:8] + v[8:]


def total8(v):
    return jnp.sum(v, axis=0, keepdims=True)


def nt(a, b):
    return lax.dot_general(a, b, (((1,), (1,)), ((), ())), preferred_element_type=F32)


def nn(a, b):
    return jnp.dot(a, b, preferred_element_type=F32)


def chunks(N, width):
    return [slice(l, min(N, l + width)) for l in range(0, N, width)]


def spread(table, rows, w):
    return jnp.concatenate([table[rows, :]] * (-(-w // L)), axis=1)[:, :w]


def fill_table(table, row):
    table[...] = jnp.broadcast_to(row, (L, row.shape[1])).T


def col_stats(read, chans, N, unroll=25):
    acc = loop(chans // R, lambda i, a: a + fold(read(i)), jnp.zeros((8, N), F32), unroll)
    mean = total8(acc) * (1.0 / chans)

    def second(i, a):
        cen = read(i) - mean
        return a + fold(cen * cen)

    acc = loop(chans // R, second, jnp.zeros((8, N), F32), unroll)
    return mean, lax.rsqrt(total8(acc) * (1.0 / chans) + EPS)


def gate(h):
    t = jnp.tanh(h)
    r = h + h * t
    return r, (1.0 + t) + (r - r * t)


def lane_sum(acc_ref, rows, v):
    N = v.shape[1]
    full = N // L * L
    tot = v[:, :L]
    for j in range(L, full, L):
        tot = tot + v[:, j:j + L]
    if full < N:
        tot = tot + jnp.concatenate([v[:, full:], jnp.zeros((v.shape[0], L - (N - full)), v.dtype)], axis=1)
    acc_ref[rows, :] += tot


def seq_spec(B, rows, N):
    return pl.BlockSpec((B, rows, N), lambda i: (i, 0, 0))


def fixed(shape):
    zero = (0,) * len(shape)
    return pl.BlockSpec(shape, lambda i: zero, pipeline_mode=pl.Buffered(1))


def smem():
    return pl.BlockSpec(memory_space=pltpu.SMEM)


def vmem():
    return pl.BlockSpec(memory_space=pltpu.VMEM)


def lane_total(acc):
    return jnp.sum(acc.T, axis=0, keepdims=True)


def unit_plan(n, M, C):
    size = M * C // n
    whole = math.gcd(size, C)
    q = max(d for d in range(1, WIDE + 1) if whole % d == 0)
    return q, C // q, size // q


def unit_slices(n, M, C):
    q, parts, units = unit_plan(n, M, C)
    out = []
    for p in range(n):
        for h in range(parts):
            lo = -((h - units * p) // parts)
            hi = -((h - units * (p + 1)) // parts)
            if hi > lo:
                out.append((p, h, lo, hi - lo, lo * parts + h - units * p))
    return out


def strided(start, size, step):
    return pl.ds(start, size, stride=step) if step > 1 else pl.ds(start, size)


def planes(q):
    return [(j, j * L, min(q - j * L, L)) for j in range(-(-q // L))]


def put_matrix(n, mat_ref, f32_ref, off):
    M, C = mat_ref.shape
    q, parts, _ = unit_plan(n, M, C)
    for p, h, lo, cnt, u in unit_slices(n, M, C):
        for j, at, w in planes(q):
            mat_ref[lo:lo + cnt, h * q + at:h * q + at + w] = f32_ref[p, j, strided(off + u, cnt, parts), :][:, :w]


def put_pieces(n, out_ref, mat_ref, M, C, off):
    q, parts, _ = unit_plan(n, M, C)
    for p, h, lo, cnt, u in unit_slices(n, M, C):
        for j, at, w in planes(q):
            v = mat_ref[lo:lo + cnt, h * q + at:h * q + at + w]
            if w < L:
                v = jnp.concatenate([v, jnp.zeros((cnt, L - w), v.dtype)], axis=1)
            out_ref[p, j, strided(off + u, cnt, parts), :] = v


def flipped(mat):
    C = mat.shape[1]
    eye = (lax.broadcasted_iota(jnp.int32, (C, C), 0) == lax.broadcasted_iota(jnp.int32, (C, C), 1)).astype(BF)
    return nt(eye, mat).astype(BF)


def ordered(n, slots_ref, a_ref, b_ref, f32_ref):
    odd = slots_ref[n]
    for p in range(n):
        slot = slots_ref[p]
        piece = jnp.where(odd == p % 2, a_ref[slot].astype(F32), b_ref[slot].astype(F32))
        f32_ref[p] = piece


def bias_block(row):
    v = jnp.broadcast_to(row, (L, row.shape[1])).T[:, :R]
    hi = v.astype(BF)
    rest = v - hi.astype(F32)
    mid = rest.astype(BF)
    low = (rest - mid.astype(F32)).astype(BF)
    col = lax.broadcasted_iota(jnp.int32, v.shape, 1)
    zero = jnp.zeros_like(v)
    return jnp.where(col == 0, hi.astype(F32), jnp.where(col == 1, mid.astype(F32), jnp.where(col == 2, low.astype(F32), zero))).astype(BF)


def unpack_in_kernel(n, slots_ref, a_ref, b_ref, bias_ref, token_ref, w1_ref, w1t_ref, f32_ref, mat_ref):
    ordered(n, slots_ref, a_ref, b_ref, f32_ref)
    put_matrix(n, mat_ref, f32_ref, 0)
    D, F = mat_ref.shape
    w1_ref[...] = mat_ref[...].astype(BF)
    w1t_ref[:, :D] = flipped(w1_ref[...])
    w1t_ref[:, D:] = bias_block(bias_ref[0:1, :])


def unpack_in(n, slots, a, b, bias, token, D, F):
    sd = jax.ShapeDtypeStruct
    return pl.pallas_call(
        functools.partial(unpack_in_kernel, n),
        in_specs=[smem()] + [vmem()] * 3 + [pl.BlockSpec(memory_space=pl.ANY)], out_specs=[vmem(), vmem()],
        out_shape=[sd((D, F), BF), sd((F, D + R), BF)],
        scratch_shapes=[pltpu.VMEM((n,) + a.shape[1:], F32), pltpu.VMEM((D, F), F32)],
        compiler_params=pltpu.CompilerParams(vmem_limit_bytes=40 * 1024 * 1024), name="unpack_in",
        cost_estimate=cost(1e9, 6e6),
    )(slots, a, b, bias, token)


def unpack_rest_kernel(n, slots_ref, a_ref, b_ref, bias_ref, wide_ref, wc_ref, wct_ref, w3_ref, w3t_ref, f32_ref, matc_ref, mat3_ref):
    F, D = mat3_ref.shape
    ordered(n, slots_ref, a_ref, b_ref, f32_ref)
    put_matrix(n, matc_ref, f32_ref, 0)
    put_matrix(n, mat3_ref, f32_ref, unit_plan(n, 3 * F, F)[2])
    for k in range(3):
        tap = matc_ref[k * F:(k + 1) * F, :].astype(BF)
        wc_ref[:, k * F:(k + 1) * F] = tap
        wct_ref[:, k * F:(k + 1) * F] = flipped(tap)
    wct_ref[:, 3 * F:] = bias_block(bias_ref[2:3, :])
    w3_ref[...] = mat3_ref[...].astype(BF)
    w3t_ref[:, :F] = flipped(w3_ref[...])
    w3t_ref[:, F:] = bias_block(wide_ref[1:2, :])


def unpack_rest(n, slots, a, b, bias, wide_bias, D, F):
    sd = jax.ShapeDtypeStruct
    return pl.pallas_call(
        functools.partial(unpack_rest_kernel, n),
        in_specs=[smem()] + [vmem()] * 4, out_specs=[vmem()] * 4,
        out_shape=[sd((F, 3 * F), BF), sd((F, 3 * F + R), BF), sd((F, D), BF), sd((D, F + R), BF)],
        scratch_shapes=[pltpu.VMEM((n,) + a.shape[1:], F32), pltpu.VMEM((3 * F, F), F32), pltpu.VMEM((F, D), F32)],
        compiler_params=pltpu.CompilerParams(vmem_limit_bytes=40 * 1024 * 1024), name="unpack_rest",
        cost_estimate=cost(2e9, 14e6),
    )(slots, a, b, bias, wide_bias)


def rim_store(ref, i, steps, cols):
    for s in range(2 * steps):
        @pl.when(i == s)
        def _(s=s):
            w = cols[0].shape[1]
            for q, v in enumerate(cols):
                at = (s % steps * len(cols) + q) * w
                ref[s // steps, :, at:at + w] = v


def rim_load(buf, i, steps, first, second):
    w = buf.shape[1]
    for s in range(2 * steps):
        @pl.when(i == s)
        def _(s=s):
            src = first() if s < steps else second()
            buf[...] = src[:, s % steps * w:(s % steps + 1) * w]


def wide_fwd_kernel(Q, start, x_ref, gain_ref, bias_ref, *refs):
    r1_ref, n0_ref, s0_ref, rstd_ref, token_ref, gtab, btab, rbuf = refs[-8:]
    D, N = x_ref.shape[1:]
    i = pl.program_id(0)

    @pl.when(i == 0)
    def _():
        fill_table(gtab, gain_ref[...].reshape(1, D) * 0.5)
        fill_table(btab, bias_ref[0:1, :] * 0.5)
        token_ref[...] = jnp.zeros_like(token_ref)

    read = lambda j: x_ref[0, rows_at(j), :].astype(F32)
    mean, rstd = col_stats(read, D, N, 10)
    rstd_ref[0] = rstd

    def act(j, _):
        rows = rows_at(j)
        n = (read(j) - mean) * rstd
        r, d = gate(n * spread(gtab, rows, N) + spread(btab, rows, N))
        n0_ref[0, rows, :] = n.astype(BF)
        s0_ref[0, rows, :] = d.astype(BF)
        rbuf[rows, :] = r.astype(BF)
        return 0

    loop(D // R, act, 0, 10)
    for q in range(Q):
        @pl.when(lax.rem(start + i, Q) == q)
        def _(q=q):
            r1_ref[0, :D, q * N:(q + 1) * N] = rbuf[...]
            r1_ref[0, D:, q * N:(q + 1) * N] = jnp.ones((r1_ref.shape[1] - D, N), BF)


def wide_fwd(xT, gain, bias, Q, start=0, steps=None, into=None, token=None):
    S, D, N = xT.shape
    steps = S if steps is None else steps
    sd = jax.ShapeDtypeStruct
    at = lambda i: (start + i, 0, 0)
    into = tuple(into or ())
    token = () if token is None else (token,)
    one = lambda rows: pl.BlockSpec((1, rows, N), at)
    return pl.pallas_call(
        functools.partial(wide_fwd_kernel, Q, start), grid=(steps,),
        in_specs=[one(D), fixed((D,)), fixed((2, D))] + [pl.BlockSpec(memory_space=pl.ANY)] * len(into + token),
        out_specs=[pl.BlockSpec((1, D + R, Q * N), lambda i: ((start + i) // Q, 0, 0)), one(D), one(D), one(1), fixed((8, L))],
        out_shape=[sd((S // Q, D + R, Q * N), BF), sd((S, D, N), BF), sd((S, D, N), BF), sd((S, 1, N), F32), sd((8, L), F32)],
        scratch_shapes=[pltpu.VMEM((D, L), F32)] * 2 + [pltpu.VMEM((D, N), BF)],
        input_output_aliases={3 + j: j for j in range(len(into))},
        compiler_params=params(52), name="wide_fwd", cost_estimate=cost(1e9 * steps, 5.5e6 * steps),
    )(xT, gain, bias, *into, *token)


CH = 384


def front_kernel(Q, steps, r1_ref, w1t_ref, gain_ref, bias_ref, u_ref, n_ref, s_ref, rstd_ref, tail_ref, h_ref, gtab, btab):
    F, N = h_ref.shape
    T = N // Q
    i = pl.program_id(0)

    @pl.when(i == 0)
    def _():
        fill_table(gtab, gain_ref[0:1, :] * 0.5)
        fill_table(btab, bias_ref[1:2, :] * 0.5)

    h_ref[...] = nn(w1t_ref[...], r1_ref[0])
    for ls in chunks(N, CH):
        W = ls.stop - ls.start
        read = lambda j: h_ref[rows_at(j), ls]
        mean, rstd = col_stats(read, F, W)
        rstd_ref[0, :, ls] = rstd

        def act(j, _):
            rows = rows_at(j)
            n = (read(j) - mean) * rstd
            r, d = gate(n * spread(gtab, rows, W) + spread(btab, rows, W))
            u_ref[0, rows, ls] = r.astype(BF)
            n_ref[0, rows, ls] = n.astype(BF)
            s_ref[0, rows, ls] = d.astype(BF)
            return 0

        loop(F // R, act, 0)
    rim_store(tail_ref, i, steps, [u_ref[0, :, (q + 1) * T - 2 * SHIFT:(q + 1) * T] for q in range(Q)])


def front(r1, w1t, gain, bias, Q):
    G, DE, N = r1.shape
    F = w1t.shape[0]
    sd = jax.ShapeDtypeStruct
    rim = (2, F, G // 2 * Q * 2 * SHIFT)
    return pl.pallas_call(
        functools.partial(front_kernel, Q, G // 2), grid=(G,),
        in_specs=[seq_spec(1, DE, N), fixed(w1t.shape), fixed(gain.shape), fixed(bias.shape)],
        out_specs=[seq_spec(1, F, N)] * 3 + [seq_spec(1, 1, N), fixed(rim)],
        out_shape=[sd((G, F, N), BF)] * 3 + [sd((G, 1, N), F32), sd(rim, BF)],
        scratch_shapes=[pltpu.VMEM((F, N), F32)] + [pltpu.VMEM((F, L), F32)] * 2,
        compiler_params=params(52), name="front", cost_estimate=cost(4e9, 19e6),
    )(r1, w1t, gain, bias)


def pull(F, W, ls, d_ref, n_at, s_at, rstd, gtab, gacc, bacc, e_ref, unroll=25):
    def first(j, carry):
        m1, m2 = carry
        rows = rows_at(j)
        ds = d_ref[rows, ls] * s_at(rows).astype(F32)
        dn = ds * n_at(rows).astype(F32)
        gain = spread(gtab, rows, W)
        t = ds * gain
        d_ref[rows, ls] = t
        lane_sum(bacc, rows, ds)
        lane_sum(gacc, rows, dn)
        return m1 + fold(t), m2 + fold(dn * gain)

    zero = jnp.zeros((8, W), F32)
    m1, m2 = loop(F // R, first, (zero, zero), unroll)
    m1, m2 = total8(m1) * (1.0 / F) * rstd, total8(m2) * (1.0 / F) * rstd

    def second(j, _):
        rows = rows_at(j)
        e_ref[0, rows, ls] = ((d_ref[rows, ls] * rstd - m1) - n_at(rows).astype(F32) * m2).astype(BF)
        return 0

    loop(F // R, second, 0, unroll)


def middle_kernel(n, Q, steps, flags_ref, u_ref, below_ref, above_ref, tail_ref, c_ref, x_ref, wct_ref, w3_ref, w3t_ref,
                  gain_ref, bias_ref, e_ref, out_ref, pieces_ref, small_ref, head_ref,
                  ubuf, cbuf, rbuf, h_ref, d_ref, n_ref, s_ref, o_ref, gacc, bacc, gwo_ref, gwc_ref, hbuf, gtab, btab, pieces32):
    F, N = h_ref.shape
    T = N // Q
    D = c_ref.shape[1]
    i = pl.program_id(0)

    @pl.when(i == 0)
    def _():
        fill_table(gtab, gain_ref[1:2, :] * 0.5)
        fill_table(btab, bias_ref[3:4, :] * 0.5)
        ubuf[3 * F:, :] = jnp.ones((R, N), BF)
        rbuf[F:, :] = jnp.ones((R, N), BF)
        gwo_ref[...] = jnp.zeros_like(gwo_ref)
        gwc_ref[...] = jnp.zeros_like(gwc_ref)
        gacc[...] = jnp.zeros_like(gacc)
        bacc[...] = jnp.zeros_like(bacc)

    rim_load(hbuf, i, steps,
             lambda: jnp.where(flags_ref[0] == 1, jnp.zeros_like(below_ref[...]), below_ref[...]),
             lambda: jnp.where(flags_ref[1] == 1, tail_ref[0], above_ref[...]))
    ubuf[:F, :] = u_ref[0]
    for k in (1, 2):
        w = k * SHIFT
        parts = []
        for q in range(Q):
            parts += [hbuf[:, (q + 1) * 2 * SHIFT - w:(q + 1) * 2 * SHIFT], u_ref[0, :, q * T:(q + 1) * T - w]]
        ubuf[k * F:(k + 1) * F, :] = jnp.concatenate(parts, axis=1)
    for q in range(Q):
        cbuf[:, q * T:(q + 1) * T] = c_ref[q]
    h_ref[...] = nn(wct_ref[...], ubuf[...])
    d_ref[...] = nn(w3_ref[...], cbuf[...])
    rstds = []
    for ls in chunks(N, CH):
        W = ls.stop - ls.start
        read = lambda j: h_ref[rows_at(j), ls]
        mean, rstd = col_stats(read, F, W)
        rstds.append(rstd)

        def act(j, _):
            rows = rows_at(j)
            v = (read(j) - mean) * rstd
            r, d = gate(v * spread(gtab, rows, W) + spread(btab, rows, W))
            rbuf[rows, ls] = r.astype(BF)
            n_ref[rows, ls] = v
            s_ref[rows, ls] = d
            return 0

        loop(F // R, act, 0)
    o_ref[...] = nn(w3t_ref[...], rbuf[...])
    gwo_ref[...] += nt(rbuf[...], cbuf[...])
    for ls, rstd in zip(chunks(N, CH), rstds):
        pull(F, ls.stop - ls.start, ls, d_ref, lambda rows: n_ref[rows, ls], lambda rows: s_ref[rows, ls], rstd, gtab, gacc, bacc, e_ref)
    gwc_ref[...] += nt(ubuf[...], e_ref[0])
    for q in range(Q):
        def emit(j, _):
            rows = rows_at(j)
            out_ref[q, rows, :] = (o_ref[rows, q * T:(q + 1) * T] + x_ref[q, rows, :].astype(F32)).astype(BF)
            return 0

        loop(D // R, emit, 0, 50)
    rim_store(head_ref, i, steps, [e_ref[0, :, q * T:q * T + 2 * SHIFT] for q in range(Q)])

    @pl.when(i == pl.num_programs(0) - 1)
    def _():
        small_ref[...] = jnp.zeros_like(small_ref)
        small_ref[0:1, :F] = lane_total(gacc[...]) * 0.5
        small_ref[0:1, F:] = lane_total(bacc[...]) * 0.5
        small_ref[1:2, :F] = gwc_ref[3 * F:3 * F + 1, :]
        small_ref[2:3, :] = gwo_ref[F:F + 1, :]
        put_pieces(n, pieces32, gwc_ref, 3 * F, F, 0)
        put_pieces(n, pieces32, gwo_ref, F, D, unit_plan(n, 3 * F, F)[2])
        pieces_ref[...] = pieces32[...].astype(BF)


def middle(n, Q, flags, uT, below, above, tails, cT, xT, wct, w3, w3t, gain, bias, rows):
    G, F, N = uT.shape
    S, D, T = cT.shape
    sd = jax.ShapeDtypeStruct
    return pl.pallas_call(
        functools.partial(middle_kernel, n, Q, G // 2), grid=(G,),
        in_specs=[smem(), seq_spec(1, F, N), fixed(below.shape), fixed(above.shape), fixed(tails.shape), seq_spec(Q, D, T), seq_spec(Q, D, T),
                  fixed(wct.shape), fixed(w3.shape), fixed(w3t.shape), fixed(gain.shape), fixed(bias.shape)],
        out_specs=[seq_spec(1, F, N), seq_spec(Q, D, T), fixed((n, WIDE // L, rows, L)), fixed((8, D)), fixed(tails.shape)],
        out_shape=[sd((G, F, N), BF), sd((S, D, T), BF), sd((n, WIDE // L, rows, L), BF), sd((8, D), F32), sd(tails.shape, BF)],
        scratch_shapes=[pltpu.VMEM((3 * F + R, N), BF), pltpu.VMEM((D, N), BF), pltpu.VMEM((F + R, N), BF), pltpu.VMEM((F, N), F32),
                        pltpu.VMEM((F, N), F32), pltpu.VMEM((F, N), F32), pltpu.VMEM((F, N), F32), pltpu.VMEM((D, N), F32),
                        pltpu.VMEM((F, L), F32), pltpu.VMEM((F, L), F32), pltpu.VMEM((F + R, D), F32),
                        pltpu.VMEM((3 * F + R, F), F32), pltpu.VMEM((F, Q * 2 * SHIFT), BF), pltpu.VMEM((F, L), F32), pltpu.VMEM((F, L), F32),
                        pltpu.VMEM((n, WIDE // L, rows, L), F32)],
        compiler_params=params(46 if n <= 32 else 60), name="middle", cost_estimate=cost(18e9, 36e6),
    )(flags, uT, below, above, tails, cT, xT, wct, w3, w3t, gain, bias)


def back_kernel(n, Q, steps, flags_ref, e_ref, below_ref, above_ref, head_ref, n_ref, s_ref, rstd_ref, r1_ref, wc_ref, gain_ref,
                small_in, e1_ref, pieces_ref, small_ref, ebuf, d_ref, gacc, bacc, gwi_ref, hbuf, gtab, e1buf, pieces32):
    F, N = d_ref.shape
    T = N // Q
    D = gwi_ref.shape[0] - R
    i = pl.program_id(0)

    @pl.when(i == 0)
    def _():
        fill_table(gtab, gain_ref[0:1, :] * 0.5)
        gwi_ref[...] = jnp.zeros_like(gwi_ref)
        gacc[...] = jnp.zeros_like(gacc)
        bacc[...] = jnp.zeros_like(bacc)

    rim_load(hbuf, i, steps,
             lambda: jnp.where(flags_ref[1] == 1, head_ref[1], above_ref[...]),
             lambda: jnp.where(flags_ref[0] == 1, jnp.zeros_like(below_ref[...]), below_ref[...]))
    ebuf[:F, :] = e_ref[0]
    for k in (1, 2):
        w = k * SHIFT
        parts = []
        for q in range(Q):
            parts += [e_ref[0, :, q * T + w:(q + 1) * T], hbuf[:, q * 2 * SHIFT:q * 2 * SHIFT + w]]
        ebuf[k * F:(k + 1) * F, :] = jnp.concatenate(parts, axis=1)
    d_ref[...] = nn(wc_ref[...], ebuf[...])
    for ls in chunks(N, CH):
        pull(F, ls.stop - ls.start, ls, d_ref, lambda rows: n_ref[0, rows, ls], lambda rows: s_ref[0, rows, ls], rstd_ref[0, :, ls],
             gtab, gacc, bacc, e1buf)
    gwi_ref[...] += nt(r1_ref[0], e1buf[0])
    for q in range(Q):
        e1_ref[q] = e1buf[0, :, q * T:(q + 1) * T]

    @pl.when(i == pl.num_programs(0) - 1)
    def _():
        small_ref[...] = small_in[...]
        small_ref[1:2, F:] = gwi_ref[D:D + 1, :]
        small_ref[3:4, :F] = lane_total(gacc[...]) * 0.5
        small_ref[3:4, F:] = lane_total(bacc[...]) * 0.5
        put_pieces(n, pieces32, gwi_ref, D, F, 0)
        pieces_ref[...] = pieces32[...].astype(BF)


def back(n, Q, flags, eT, below, above, heads, n1, s1, rstd1, r1, wc, gain, small, rows):
    G, F, N = eT.shape
    DE = r1.shape[1]
    sd = jax.ShapeDtypeStruct
    return pl.pallas_call(
        functools.partial(back_kernel, n, Q, G // 2), grid=(G,),
        in_specs=[smem(), seq_spec(1, F, N), fixed(below.shape), fixed(above.shape), fixed(heads.shape), seq_spec(1, F, N), seq_spec(1, F, N),
                  seq_spec(1, 1, N), seq_spec(1, DE, N), fixed(wc.shape), fixed(gain.shape), fixed(small.shape)],
        out_specs=[seq_spec(Q, F, N // Q), fixed((n, WIDE // L, rows, L)), fixed(small.shape)],
        out_shape=[sd((G * Q, F, N // Q), BF), sd((n, WIDE // L, rows, L), BF), sd(small.shape, F32)],
        scratch_shapes=[pltpu.VMEM((3 * F, N), BF), pltpu.VMEM((F, N), F32), pltpu.VMEM((F, L), F32), pltpu.VMEM((F, L), F32),
                        pltpu.VMEM((DE, F), F32), pltpu.VMEM((F, Q * 2 * SHIFT), BF), pltpu.VMEM((F, L), F32),
                        pltpu.VMEM((1, F, N), BF), pltpu.VMEM((n, WIDE // L, rows, L), F32)],
        compiler_params=params(52), name="back", cost_estimate=cost(8e9, 25e6),
    )(flags, eT, below, above, heads, n1, s1, rstd1, r1, wc, gain, small)


def wide_bwd_kernel(Q, e_ref, w1_ref, n_ref, s_ref, rstd_ref, c_ref, gain_ref, small_in, *refs):
    dx_ref, small_ref, gtab, gacc, bacc = refs[-5 - Q:-Q]
    d_refs = refs[-Q:]
    D, N = d_refs[0].shape
    i = pl.program_id(0)

    @pl.when(i == 0)
    def _():
        fill_table(gtab, gain_ref[...].reshape(1, D) * 0.5)
        gacc[...] = jnp.zeros_like(gacc)
        bacc[...] = jnp.zeros_like(bacc)

    def dot(q):
        d_refs[q][...] = nn(w1_ref[...], e_ref[q])

    def pull_wide(q):
        d_ref = d_refs[q]

        def first(j, carry):
            m1, m2 = carry
            rows = rows_at(j)
            ds = d_ref[rows, :] * s_ref[q, rows, :].astype(F32)
            dn = ds * n_ref[q, rows, :].astype(F32)
            gain = spread(gtab, rows, N)
            t = ds * gain
            d_ref[rows, :] = t
            lane_sum(bacc, rows, ds)
            lane_sum(gacc, rows, dn)
            return m1 + fold(t), m2 + fold(dn * gain)

        zero = jnp.zeros((8, N), F32)
        m1, m2 = loop(D // R, first, (zero, zero), 50)
        rstd = rstd_ref[q]
        m1, m2 = total8(m1) * (1.0 / D) * rstd, total8(m2) * (1.0 / D) * rstd

        def second(j, _):
            rows = rows_at(j)
            g = (d_ref[rows, :] * rstd - m1) - n_ref[q, rows, :].astype(F32) * m2
            dx_ref[q, rows, :] = (g + c_ref[q, rows, :].astype(F32)).astype(BF)
            return 0

        loop(D // R, second, 0, 50)

    dot(0)
    for q in range(Q):
        if q + 1 < Q:
            dot(q + 1)
        pull_wide(q)

    @pl.when(i == pl.num_programs(0) - 1)
    def _():
        small_ref[...] = small_in[...]
        small_ref[4:5, :] = small_in[4:5, :] + lane_total(gacc[...]) * 0.5
        small_ref[5:6, :] = small_in[5:6, :] + lane_total(bacc[...]) * 0.5


def wide_bwd(Q, e1, w1, n0, s0, rstd0, cT, gain, small, start=0, steps=None, into=None):
    S, D, N = cT.shape
    F = e1.shape[1]
    steps = S // Q if steps is None else steps
    sd = jax.ShapeDtypeStruct
    at = lambda i: (start + i, 0, 0)
    into = () if into is None else (into,)
    part = lambda rows: pl.BlockSpec((Q, rows, N), at)
    return pl.pallas_call(
        functools.partial(wide_bwd_kernel, Q), grid=(steps,),
        in_specs=[part(F), fixed(w1.shape), part(D), part(D), part(1), part(D),
                  fixed(gain.shape), fixed(small.shape)] + [pl.BlockSpec(memory_space=pl.ANY)] * len(into),
        out_specs=[part(D), fixed(small.shape)],
        out_shape=[sd((S, D, N), BF), sd(small.shape, F32)],
        scratch_shapes=[pltpu.VMEM((D, L), F32)] * 3 + [pltpu.VMEM((D, N), F32)] * Q,
        input_output_aliases={8: 0} if into else {},
        compiler_params=params(52), name="wide_bwd", cost_estimate=cost(2e9 * steps, 8.4e6 * steps),
    )(e1, w1, n0, s0, rstd0, cT, gain, small, *into)


def swap(v, bit, n):
    return lax.ppermute(v, "ctx", [(i, i ^ bit) for i in range(n)])


def bits_of(n):
    out, b = [], 1
    while b < n:
        out.append(b)
        b *= 2
    return out


def together(*values):
    return lax.optimization_barrier(values)


def slot_table(n, me):
    diff = jnp.arange(n, dtype=jnp.int32) ^ me
    slots = sum((jnp.where((diff & bit) != 0, n // 2 // bit, 0) for bit in bits_of(n)[1:]), jnp.zeros_like(diff))
    return jnp.concatenate([slots, (me & 1)[None].astype(jnp.int32)])


def split_for(full, bit, me):
    pairs = full.reshape((-1, 2) + full.shape[1:])
    mine = jnp.where((me & bit) == 0, 0, 1)
    keep = lax.dynamic_index_in_dim(pairs, mine, 1, keepdims=False)
    return keep, lax.dynamic_index_in_dim(pairs, 1 - mine, 1, keepdims=False).astype(BF)


def sum_all(v, n):
    for bit in bits_of(n):
        v = v + swap(v, bit, n)
    return v


def to_units(flat, n, M, C, rows=None):
    q, parts, units = unit_plan(n, M, C)
    return jnp.pad(flat.reshape(units, q), ((0, 0), (0, WIDE - q))).reshape(units, WIDE // L, L).transpose(1, 0, 2)


def round_up(v, m=8):
    return -(-v // m) * m


def on_device(block_input, cotangent, w_in, w_conv, w_out, wide_gain, wide_bias, narrow_gain, narrow_bias, dealing):
    slots, seqs, T, D = block_input.shape
    F = narrow_gain.shape[1]
    n = lax.axis_size("ctx")
    half = dealing.shape[0] // 2
    me = lax.axis_index("ctx")
    pair = jnp.sum(jnp.where(dealing[:half] == me, jnp.arange(half, dtype=jnp.int32), 0))
    flags = jnp.stack([pair == 0, pair == half - 1]).astype(jnp.int32)
    up = [(i, (i + 1) % n) for i in range(n)]
    down = [((i + 1) % n, i) for i in range(n)]
    table = slot_table(n, me)
    units_in, units_conv, units_out = (unit_plan(n, m, c)[2] for m, c in ((D, F), (3 * F, F), (F, D)))
    rows_in, rows_rest = round_up(units_in), round_up(units_conv + units_out)

    xT = block_input.transpose(0, 1, 3, 2).reshape(slots * seqs, D, T)
    cT = cotangent.transpose(0, 1, 3, 2).reshape(slots * seqs, D, T)

    piece_in = jnp.pad(to_units(w_in, n, D, F), ((0, 0), (0, rows_in - units_in), (0, 0)))
    piece_rest = jnp.concatenate([to_units(w_conv, n, 3 * F, F), to_units(w_out, n, F, D)], axis=1)
    piece_rest = jnp.pad(piece_rest, ((0, 0), (0, rows_rest - piece_rest.shape[1]), (0, 0)))
    gain0 = wide_gain
    bits = bits_of(n)
    Q = 2
    steps = slots * seqs // Q

    buf_in, buf_rest = piece_in[None], piece_rest[None]
    acts, gain, done, token = (), gain0, 0, None
    far = list(reversed(bits))
    for s, bit in enumerate(far):
        got_in = swap(buf_in, bit, n)
        if s < len(far) - 2:
            got_rest = swap(buf_rest, bit, n)
        count = (steps * (s + 1)) // (len(far) - 1) * Q - done if s < len(far) - 1 else 0
        if count:
            *acts, token = wide_fwd(xT, gain, wide_bias, Q, done, count, acts, token)
            done += count
        if s < len(far) - 1:
            buf_in = jnp.concatenate([buf_in, got_in], axis=0)
        if s < len(far) - 2:
            buf_rest = jnp.concatenate([buf_rest, got_rest], axis=0)
        buf_in, buf_rest, token, gain = together(buf_in, buf_rest, token, gain)
    r1, n0, s0, rstd0 = acts
    got_rest = swap(buf_rest, far[-2], n)
    w1, w1t = unpack_in(n, table, buf_in, got_in, narrow_bias, token, D, F)
    uT, n1, s1, rstd1, tails = front(r1, w1t, narrow_gain, narrow_bias, Q)
    buf_rest, tails = together(jnp.concatenate([buf_rest, got_rest], axis=0), tails)
    below = lax.ppermute(tails[0], "ctx", up)
    above = lax.ppermute(tails[1], "ctx", down)
    got_rest = swap(buf_rest, far[-1], n)
    wc, wct, w3, w3t = unpack_rest(n, table, buf_rest, got_rest, narrow_bias, wide_bias, D, F)
    eT, outT, rest, small, heads = middle(n, Q, flags, uT, below, above, tails, cT, xT, wct, w3, w3t,
                                          narrow_gain, narrow_bias, rows_rest)

    keep, send = split_for(rest, bits[0], me)
    got = swap(send, bits[0], n)
    above = lax.ppermute(heads[0], "ctx", down)
    below = lax.ppermute(heads[1], "ctx", up)
    rest = keep + got.astype(F32)
    keep, send = split_for(rest, bits[1], me)
    send, gain1 = together(send, narrow_gain)
    got = swap(send, bits[1], n)
    e1, into, small = back(n, Q, flags, eT, below, above, heads, n1, s1, rstd1, r1, wc, gain1, small, rows_in)
    rest, small = together(keep + got.astype(F32), small)

    dxT, gain, halves = None, gain0, 2
    for s in range(halves):
        keep_i, send_i = split_for(into, bits[s], me)
        keep_r, send_r = split_for(rest, bits[s + 2], me)
        send_r, send_i, gain = together(send_r, send_i, gain)
        got_r, got_i = swap(send_r, bits[s + 2], n), swap(send_i, bits[s], n)
        dxT, small = wide_bwd(Q, e1, w1, n0, s0, rstd0, cT, gain, small, s * steps // halves, steps // halves, dxT)
        rest, into, small = together(keep_r + got_r.astype(F32), keep_i + got_i.astype(F32), small)
    def owned(own, at, M, C):
        q, parts, units = unit_plan(n, M, C)
        return own[:, at:at + units].transpose(1, 0, 2).reshape(units, WIDE)[:, :q].reshape(-1)


    rest_bits, in_bits = bits[2 + halves:], bits[halves:]
    flat = {}
    for j in range(len(bits)):
        if j == len(in_bits) + 1:
            small, flat["in"], flat["conv"] = together(small, owned(into[0], 0, D, F), owned(rest[0], 0, 3 * F, F))
        got = swap(small, bits[j], n)
        if j < len(rest_bits):
            keep_r, send_r = split_for(rest, rest_bits[j], me)
            rest = keep_r + swap(send_r, rest_bits[j], n).astype(F32)
        if j < len(in_bits):
            keep_i, send_i = split_for(into, in_bits[j], me)
            into = keep_i + swap(send_i, in_bits[j], n).astype(F32)
        small = small + got
        if j < len(in_bits):
            small, rest, into = together(small, rest, into)

    back4 = lambda v: v.reshape(slots, seqs, D, T).transpose(0, 1, 3, 2)
    return (back4(outT), back4(dxT), flat["in"], flat["conv"], owned(rest[0], units_conv, F, D),
            small[4], jnp.stack([small[5], small[2]]), jnp.stack([small[3, :F], small[0, :F]]),
            jnp.stack([small[1, F:], small[3, F:], small[1, :F], small[0, F:]]))


def solution(mesh):
    whole, flat, copied = P("ctx", None, None, None), P("ctx"), P()
    return jax.shard_map(
        on_device, mesh=mesh,
        in_specs=(whole, whole, flat, flat, flat, copied, copied, copied, copied, copied),
        out_specs=(whole, whole, flat, flat, flat, copied, copied, copied, copied),
        check_vma=False,
    )
```

```python
import functools
import math
import jax
import jax.numpy as jnp
from jax import lax
from jax.experimental import pallas as pl
from jax.experimental.pallas import tpu as pltpu
from jax.sharding import PartitionSpec as P

EPS = 1e-05
BF = jnp.bfloat16
F32 = jnp.float32
L = 128
R = 16
SHIFT = 16
WIDE = 256


def params(mb=52):
    return pltpu.CompilerParams(dimension_semantics=("arbitrary",), vmem_limit_bytes=mb * 1024 * 1024)


def cost(flops, nbytes, trans=0):
    return pl.CostEstimate(flops=int(flops), bytes_accessed=int(nbytes), transcendentals=int(trans))


def rows_at(i):
    return pl.ds(pl.multiple_of(i * R, R), R)


def loop(n, body, init, unroll=25):
    return lax.fori_loop(0, n, body, init, unroll=min(n, unroll))


def fold(v):
    return v[:8] + v[8:]


def total8(v):
    return jnp.sum(v, axis=0, keepdims=True)


def nt(a, b):
    return lax.dot_general(a, b, (((1,), (1,)), ((), ())), preferred_element_type=F32)


def nn(a, b):
    return jnp.dot(a, b, preferred_element_type=F32)


def chunks(N, width):
    return [slice(l, min(N, l + width)) for l in range(0, N, width)]


def spread(table, rows, w):
    return jnp.concatenate([table[rows, :]] * (-(-w // L)), axis=1)[:, :w]


def fill_table(table, row):
    table[...] = jnp.broadcast_to(row, (L, row.shape[1])).T


def col_stats(read, chans, N, unroll=25):
    acc = loop(chans // R, lambda i, a: a + fold(read(i)), jnp.zeros((8, N), F32), unroll)
    mean = total8(acc) * (1.0 / chans)

    def second(i, a):
        cen = read(i) - mean
        return a + fold(cen * cen)

    acc = loop(chans // R, second, jnp.zeros((8, N), F32), unroll)
    return mean, lax.rsqrt(total8(acc) * (1.0 / chans) + EPS)


def gate(h):
    t = jnp.tanh(h)
    r = h + h * t
    return r, (1.0 + t) + (r - r * t)


def lane_sum(acc_ref, rows, v):
    N = v.shape[1]
    full = N // L * L
    tot = v[:, :L]
    for j in range(L, full, L):
        tot = tot + v[:, j:j + L]
    if full < N:
        tot = tot + jnp.concatenate([v[:, full:], jnp.zeros((v.shape[0], L - (N - full)), v.dtype)], axis=1)
    acc_ref[rows, :] += tot


def seq_spec(B, rows, N):
    return pl.BlockSpec((B, rows, N), lambda i: (i, 0, 0))


def fixed(shape):
    zero = (0,) * len(shape)
    return pl.BlockSpec(shape, lambda i: zero, pipeline_mode=pl.Buffered(1))


def smem():
    return pl.BlockSpec(memory_space=pltpu.SMEM)


def vmem():
    return pl.BlockSpec(memory_space=pltpu.VMEM)


def lane_total(acc):
    return jnp.sum(acc.T, axis=0, keepdims=True)


def unit_plan(n, M, C):
    size = M * C // n
    whole = math.gcd(size, C)
    q = max(d for d in range(1, WIDE + 1) if whole % d == 0)
    return q, C // q, size // q


def unit_slices(n, M, C):
    q, parts, units = unit_plan(n, M, C)
    out = []
    for p in range(n):
        for h in range(parts):
            lo = -((h - units * p) // parts)
            hi = -((h - units * (p + 1)) // parts)
            if hi > lo:
                out.append((p, h, lo, hi - lo, lo * parts + h - units * p))
    return out


def strided(start, size, step):
    return pl.ds(start, size, stride=step) if step > 1 else pl.ds(start, size)


def planes(q):
    return [(j, j * L, min(q - j * L, L)) for j in range(-(-q // L))]


def put_matrix(n, mat_ref, f32_ref, off):
    M, C = mat_ref.shape
    q, parts, _ = unit_plan(n, M, C)
    for p, h, lo, cnt, u in unit_slices(n, M, C):
        for j, at, w in planes(q):
            mat_ref[lo:lo + cnt, h * q + at:h * q + at + w] = f32_ref[p, j, strided(off + u, cnt, parts), :][:, :w]


def put_pieces(n, out_ref, mat_ref, M, C, off):
    q, parts, _ = unit_plan(n, M, C)
    for p, h, lo, cnt, u in unit_slices(n, M, C):
        for j, at, w in planes(q):
            v = mat_ref[lo:lo + cnt, h * q + at:h * q + at + w]
            if w < L:
                v = jnp.concatenate([v, jnp.zeros((cnt, L - w), v.dtype)], axis=1)
            out_ref[p, j, strided(off + u, cnt, parts), :] = v


def flipped(mat):
    C = mat.shape[1]
    eye = (lax.broadcasted_iota(jnp.int32, (C, C), 0) == lax.broadcasted_iota(jnp.int32, (C, C), 1)).astype(BF)
    return nt(eye, mat).astype(BF)


def ordered(n, slots_ref, a_ref, b_ref, f32_ref):
    odd = slots_ref[n]
    for p in range(n):
        slot = slots_ref[p]
        piece = jnp.where(odd == p % 2, a_ref[slot].astype(F32), b_ref[slot].astype(F32))
        f32_ref[p] = piece


def bias_block(row):
    v = jnp.broadcast_to(row, (L, row.shape[1])).T[:, :R]
    hi = v.astype(BF)
    rest = v - hi.astype(F32)
    mid = rest.astype(BF)
    low = (rest - mid.astype(F32)).astype(BF)
    col = lax.broadcasted_iota(jnp.int32, v.shape, 1)
    zero = jnp.zeros_like(v)
    return jnp.where(col == 0, hi.astype(F32), jnp.where(col == 1, mid.astype(F32), jnp.where(col == 2, low.astype(F32), zero))).astype(BF)


def unpack_in_kernel(n, slots_ref, a_ref, b_ref, bias_ref, token_ref, w1_ref, w1t_ref, f32_ref, mat_ref):
    ordered(n, slots_ref, a_ref, b_ref, f32_ref)
    put_matrix(n, mat_ref, f32_ref, 0)
    D, F = mat_ref.shape
    w1_ref[...] = mat_ref[...].astype(BF)
    w1t_ref[:, :D] = flipped(w1_ref[...])
    w1t_ref[:, D:] = bias_block(bias_ref[0:1, :])


def unpack_in(n, slots, a, b, bias, token, D, F):
    sd = jax.ShapeDtypeStruct
    return pl.pallas_call(
        functools.partial(unpack_in_kernel, n),
        in_specs=[smem()] + [vmem()] * 3 + [pl.BlockSpec(memory_space=pl.ANY)], out_specs=[vmem(), vmem()],
        out_shape=[sd((D, F), BF), sd((F, D + R), BF)],
        scratch_shapes=[pltpu.VMEM((n,) + a.shape[1:], F32), pltpu.VMEM((D, F), F32)],
        compiler_params=pltpu.CompilerParams(vmem_limit_bytes=40 * 1024 * 1024), name="unpack_in",
        cost_estimate=cost(1e9, 6e6),
    )(slots, a, b, bias, token)


def unpack_rest_kernel(n, slots_ref, a_ref, b_ref, bias_ref, wide_ref, wc_ref, wct_ref, w3_ref, w3t_ref, f32_ref, matc_ref, mat3_ref):
    F, D = mat3_ref.shape
    ordered(n, slots_ref, a_ref, b_ref, f32_ref)
    put_matrix(n, matc_ref, f32_ref, 0)
    put_matrix(n, mat3_ref, f32_ref, unit_plan(n, 3 * F, F)[2])
    for k in range(3):
        tap = matc_ref[k * F:(k + 1) * F, :].astype(BF)
        wc_ref[:, k * F:(k + 1) * F] = tap
        wct_ref[:, k * F:(k + 1) * F] = flipped(tap)
    wct_ref[:, 3 * F:] = bias_block(bias_ref[2:3, :])
    w3_ref[...] = mat3_ref[...].astype(BF)
    w3t_ref[:, :F] = flipped(w3_ref[...])
    w3t_ref[:, F:] = bias_block(wide_ref[1:2, :])


def unpack_rest(n, slots, a, b, bias, wide_bias, D, F):
    sd = jax.ShapeDtypeStruct
    return pl.pallas_call(
        functools.partial(unpack_rest_kernel, n),
        in_specs=[smem()] + [vmem()] * 4, out_specs=[vmem()] * 4,
        out_shape=[sd((F, 3 * F), BF), sd((F, 3 * F + R), BF), sd((F, D), BF), sd((D, F + R), BF)],
        scratch_shapes=[pltpu.VMEM((n,) + a.shape[1:], F32), pltpu.VMEM((3 * F, F), F32), pltpu.VMEM((F, D), F32)],
        compiler_params=pltpu.CompilerParams(vmem_limit_bytes=40 * 1024 * 1024), name="unpack_rest",
        cost_estimate=cost(2e9, 14e6),
    )(slots, a, b, bias, wide_bias)


def rim_store(ref, i, steps, cols):
    for s in range(2 * steps):
        @pl.when(i == s)
        def _(s=s):
            w = cols[0].shape[1]
            for q, v in enumerate(cols):
                at = (s % steps * len(cols) + q) * w
                ref[s // steps, :, at:at + w] = v


def rim_load(buf, i, steps, first, second):
    w = buf.shape[1]
    for s in range(2 * steps):
        @pl.when(i == s)
        def _(s=s):
            src = first() if s < steps else second()
            buf[...] = src[:, s % steps * w:(s % steps + 1) * w]


def wide_fwd_kernel(Q, start, x_ref, gain_ref, bias_ref, *refs):
    r1_ref, n0_ref, s0_ref, rstd_ref, token_ref, gtab, btab, rbuf = refs[-8:]
    D, N = x_ref.shape[1:]
    i = pl.program_id(0)

    @pl.when(i == 0)
    def _():
        fill_table(gtab, gain_ref[...].reshape(1, D) * 0.5)
        fill_table(btab, bias_ref[0:1, :] * 0.5)
        token_ref[...] = jnp.zeros_like(token_ref)

    read = lambda j: x_ref[0, rows_at(j), :].astype(F32)
    mean, rstd = col_stats(read, D, N, 10)
    rstd_ref[0] = rstd

    def act(j, _):
        rows = rows_at(j)
        n = (read(j) - mean) * rstd
        r, d = gate(n * spread(gtab, rows, N) + spread(btab, rows, N))
        n0_ref[0, rows, :] = n.astype(BF)
        s0_ref[0, rows, :] = d.astype(BF)
        rbuf[rows, :] = r.astype(BF)
        return 0

    loop(D // R, act, 0, 10)
    for q in range(Q):
        @pl.when(lax.rem(start + i, Q) == q)
        def _(q=q):
            r1_ref[0, :D, q * N:(q + 1) * N] = rbuf[...]
            r1_ref[0, D:, q * N:(q + 1) * N] = jnp.ones((r1_ref.shape[1] - D, N), BF)


def wide_fwd(xT, gain, bias, Q, start=0, steps=None, into=None, token=None):
    S, D, N = xT.shape
    steps = S if steps is None else steps
    sd = jax.ShapeDtypeStruct
    at = lambda i: (start + i, 0, 0)
    into = tuple(into or ())
    token = () if token is None else (token,)
    one = lambda rows: pl.BlockSpec((1, rows, N), at)
    return pl.pallas_call(
        functools.partial(wide_fwd_kernel, Q, start), grid=(steps,),
        in_specs=[one(D), fixed((D,)), fixed((2, D))] + [pl.BlockSpec(memory_space=pl.ANY)] * len(into + token),
        out_specs=[pl.BlockSpec((1, D + R, Q * N), lambda i: ((start + i) // Q, 0, 0)), one(D), one(D), one(1), fixed((8, L))],
        out_shape=[sd((S // Q, D + R, Q * N), BF), sd((S, D, N), BF), sd((S, D, N), BF), sd((S, 1, N), F32), sd((8, L), F32)],
        scratch_shapes=[pltpu.VMEM((D, L), F32)] * 2 + [pltpu.VMEM((D, N), BF)],
        input_output_aliases={3 + j: j for j in range(len(into))},
        compiler_params=params(52), name="wide_fwd", cost_estimate=cost(1e9 * steps, 5.5e6 * steps),
    )(xT, gain, bias, *into, *token)


CH = 384


def front_kernel(Q, steps, r1_ref, w1t_ref, gain_ref, bias_ref, u_ref, n_ref, s_ref, rstd_ref, tail_ref, h_ref, gtab, btab):
    F, N = h_ref.shape
    T = N // Q
    i = pl.program_id(0)

    @pl.when(i == 0)
    def _():
        fill_table(gtab, gain_ref[0:1, :] * 0.5)
        fill_table(btab, bias_ref[1:2, :] * 0.5)

    h_ref[...] = nn(w1t_ref[...], r1_ref[0])
    for ls in chunks(N, CH):
        W = ls.stop - ls.start
        read = lambda j: h_ref[rows_at(j), ls]
        mean, rstd = col_stats(read, F, W)
        rstd_ref[0, :, ls] = rstd

        def act(j, _):
            rows = rows_at(j)
            n = (read(j) - mean) * rstd
            r, d = gate(n * spread(gtab, rows, W) + spread(btab, rows, W))
            u_ref[0, rows, ls] = r.astype(BF)
            n_ref[0, rows, ls] = n.astype(BF)
            s_ref[0, rows, ls] = d.astype(BF)
            return 0

        loop(F // R, act, 0)
    rim_store(tail_ref, i, steps, [u_ref[0, :, (q + 1) * T - 2 * SHIFT:(q + 1) * T] for q in range(Q)])


def front(r1, w1t, gain, bias, Q):
    G, DE, N = r1.shape
    F = w1t.shape[0]
    sd = jax.ShapeDtypeStruct
    rim = (2, F, G // 2 * Q * 2 * SHIFT)
    return pl.pallas_call(
        functools.partial(front_kernel, Q, G // 2), grid=(G,),
        in_specs=[seq_spec(1, DE, N), fixed(w1t.shape), fixed(gain.shape), fixed(bias.shape)],
        out_specs=[seq_spec(1, F, N)] * 3 + [seq_spec(1, 1, N), fixed(rim)],
        out_shape=[sd((G, F, N), BF)] * 3 + [sd((G, 1, N), F32), sd(rim, BF)],
        scratch_shapes=[pltpu.VMEM((F, N), F32)] + [pltpu.VMEM((F, L), F32)] * 2,
        compiler_params=params(52), name="front", cost_estimate=cost(4e9, 19e6),
    )(r1, w1t, gain, bias)


def pull(F, W, ls, d_ref, n_at, s_at, rstd, gtab, gacc, bacc, e_ref, unroll=25):
    def first(j, carry):
        m1, m2 = carry
        rows = rows_at(j)
        ds = d_ref[rows, ls] * s_at(rows).astype(F32)
        dn = ds * n_at(rows).astype(F32)
        gain = spread(gtab, rows, W)
        t = ds * gain
        d_ref[rows, ls] = t
        lane_sum(bacc, rows, ds)
        lane_sum(gacc, rows, dn)
        return m1 + fold(t), m2 + fold(dn * gain)

    zero = jnp.zeros((8, W), F32)
    m1, m2 = loop(F // R, first, (zero, zero), unroll)
    m1, m2 = total8(m1) * (1.0 / F) * rstd, total8(m2) * (1.0 / F) * rstd

    def second(j, _):
        rows = rows_at(j)
        e_ref[0, rows, ls] = ((d_ref[rows, ls] * rstd - m1) - n_at(rows).astype(F32) * m2).astype(BF)
        return 0

    loop(F // R, second, 0, unroll)


def middle_kernel(n, Q, steps, flags_ref, u_ref, below_ref, above_ref, tail_ref, c_ref, x_ref, wct_ref, w3_ref, w3t_ref,
                  gain_ref, bias_ref, e_ref, out_ref, pieces_ref, small_ref, head_ref,
                  ubuf, cbuf, rbuf, h_ref, d_ref, n_ref, s_ref, o_ref, gacc, bacc, gwo_ref, gwc_ref, hbuf, gtab, btab, pieces32):
    F, N = h_ref.shape
    T = N // Q
    D = c_ref.shape[1]
    i = pl.program_id(0)

    @pl.when(i == 0)
    def _():
        fill_table(gtab, gain_ref[1:2, :] * 0.5)
        fill_table(btab, bias_ref[3:4, :] * 0.5)
        ubuf[3 * F:, :] = jnp.ones((R, N), BF)
        rbuf[F:, :] = jnp.ones((R, N), BF)
        gwo_ref[...] = jnp.zeros_like(gwo_ref)
        gwc_ref[...] = jnp.zeros_like(gwc_ref)
        gacc[...] = jnp.zeros_like(gacc)
        bacc[...] = jnp.zeros_like(bacc)

    rim_load(hbuf, i, steps,
             lambda: jnp.where(flags_ref[0] == 1, jnp.zeros_like(below_ref[...]), below_ref[...]),
             lambda: jnp.where(flags_ref[1] == 1, tail_ref[0], above_ref[...]))
    ubuf[:F, :] = u_ref[0]
    for k in (1, 2):
        w = k * SHIFT
        parts = []
        for q in range(Q):
            parts += [hbuf[:, (q + 1) * 2 * SHIFT - w:(q + 1) * 2 * SHIFT], u_ref[0, :, q * T:(q + 1) * T - w]]
        ubuf[k * F:(k + 1) * F, :] = jnp.concatenate(parts, axis=1)
    for q in range(Q):
        cbuf[:, q * T:(q + 1) * T] = c_ref[q]
    h_ref[...] = nn(wct_ref[...], ubuf[...])
    d_ref[...] = nn(w3_ref[...], cbuf[...])
    rstds = []
    for ls in chunks(N, CH):
        W = ls.stop - ls.start
        read = lambda j: h_ref[rows_at(j), ls]
        mean, rstd = col_stats(read, F, W)
        rstds.append(rstd)

        def act(j, _):
            rows = rows_at(j)
            v = (read(j) - mean) * rstd
            r, d = gate(v * spread(gtab, rows, W) + spread(btab, rows, W))
            rbuf[rows, ls] = r.astype(BF)
            n_ref[rows, ls] = v
            s_ref[rows, ls] = d
            return 0

        loop(F // R, act, 0)
    o_ref[...] = nn(w3t_ref[...], rbuf[...])
    gwo_ref[...] += nt(rbuf[...], cbuf[...])
    for ls, rstd in zip(chunks(N, CH), rstds):
        pull(F, ls.stop - ls.start, ls, d_ref, lambda rows: n_ref[rows, ls], lambda rows: s_ref[rows, ls], rstd, gtab, gacc, bacc, e_ref)
    gwc_ref[...] += nt(ubuf[...], e_ref[0])
    for q in range(Q):
        def emit(j, _):
            rows = rows_at(j)
            out_ref[q, rows, :] = (o_ref[rows, q * T:(q + 1) * T] + x_ref[q, rows, :].astype(F32)).astype(BF)
            return 0

        loop(D // R, emit, 0, 50)
    rim_store(head_ref, i, steps, [e_ref[0, :, q * T:q * T + 2 * SHIFT] for q in range(Q)])

    @pl.when(i == pl.num_programs(0) - 1)
    def _():
        small_ref[...] = jnp.zeros_like(small_ref)
        small_ref[0:1, :F] = lane_total(gacc[...]) * 0.5
        small_ref[0:1, F:] = lane_total(bacc[...]) * 0.5
        small_ref[1:2, :F] = gwc_ref[3 * F:3 * F + 1, :]
        small_ref[2:3, :] = gwo_ref[F:F + 1, :]
        put_pieces(n, pieces32, gwc_ref, 3 * F, F, 0)
        put_pieces(n, pieces32, gwo_ref, F, D, unit_plan(n, 3 * F, F)[2])
        pieces_ref[...] = pieces32[...].astype(BF)


def middle(n, Q, flags, uT, below, above, tails, cT, xT, wct, w3, w3t, gain, bias, rows):
    G, F, N = uT.shape
    S, D, T = cT.shape
    sd = jax.ShapeDtypeStruct
    return pl.pallas_call(
        functools.partial(middle_kernel, n, Q, G // 2), grid=(G,),
        in_specs=[smem(), seq_spec(1, F, N), fixed(below.shape), fixed(above.shape), fixed(tails.shape), seq_spec(Q, D, T), seq_spec(Q, D, T),
                  fixed(wct.shape), fixed(w3.shape), fixed(w3t.shape), fixed(gain.shape), fixed(bias.shape)],
        out_specs=[seq_spec(1, F, N), seq_spec(Q, D, T), fixed((n, WIDE // L, rows, L)), fixed((8, D)), fixed(tails.shape)],
        out_shape=[sd((G, F, N), BF), sd((S, D, T), BF), sd((n, WIDE // L, rows, L), BF), sd((8, D), F32), sd(tails.shape, BF)],
        scratch_shapes=[pltpu.VMEM((3 * F + R, N), BF), pltpu.VMEM((D, N), BF), pltpu.VMEM((F + R, N), BF), pltpu.VMEM((F, N), F32),
                        pltpu.VMEM((F, N), F32), pltpu.VMEM((F, N), F32), pltpu.VMEM((F, N), F32), pltpu.VMEM((D, N), F32),
                        pltpu.VMEM((F, L), F32), pltpu.VMEM((F, L), F32), pltpu.VMEM((F + R, D), F32),
                        pltpu.VMEM((3 * F + R, F), F32), pltpu.VMEM((F, Q * 2 * SHIFT), BF), pltpu.VMEM((F, L), F32), pltpu.VMEM((F, L), F32),
                        pltpu.VMEM((n, WIDE // L, rows, L), F32)],
        compiler_params=params(46 if n <= 32 else 60), name="middle", cost_estimate=cost(18e9, 36e6),
    )(flags, uT, below, above, tails, cT, xT, wct, w3, w3t, gain, bias)


def back_kernel(n, Q, steps, flags_ref, e_ref, below_ref, above_ref, head_ref, n_ref, s_ref, rstd_ref, r1_ref, wc_ref, gain_ref,
                small_in, e1_ref, pieces_ref, small_ref, ebuf, d_ref, gacc, bacc, gwi_ref, hbuf, gtab, e1buf, pieces32):
    F, N = d_ref.shape
    T = N // Q
    D = gwi_ref.shape[0] - R
    i = pl.program_id(0)

    @pl.when(i == 0)
    def _():
        fill_table(gtab, gain_ref[0:1, :] * 0.5)
        gwi_ref[...] = jnp.zeros_like(gwi_ref)
        gacc[...] = jnp.zeros_like(gacc)
        bacc[...] = jnp.zeros_like(bacc)

    rim_load(hbuf, i, steps,
             lambda: jnp.where(flags_ref[1] == 1, head_ref[1], above_ref[...]),
             lambda: jnp.where(flags_ref[0] == 1, jnp.zeros_like(below_ref[...]), below_ref[...]))
    ebuf[:F, :] = e_ref[0]
    for k in (1, 2):
        w = k * SHIFT
        parts = []
        for q in range(Q):
            parts += [e_ref[0, :, q * T + w:(q + 1) * T], hbuf[:, q * 2 * SHIFT:q * 2 * SHIFT + w]]
        ebuf[k * F:(k + 1) * F, :] = jnp.concatenate(parts, axis=1)
    d_ref[...] = nn(wc_ref[...], ebuf[...])
    for ls in chunks(N, CH):
        pull(F, ls.stop - ls.start, ls, d_ref, lambda rows: n_ref[0, rows, ls], lambda rows: s_ref[0, rows, ls], rstd_ref[0, :, ls],
             gtab, gacc, bacc, e1buf)
    gwi_ref[...] += nt(r1_ref[0], e1buf[0])
    for q in range(Q):
        e1_ref[q] = e1buf[0, :, q * T:(q + 1) * T]

    @pl.when(i == pl.num_programs(0) - 1)
    def _():
        small_ref[...] = small_in[...]
        small_ref[1:2, F:] = gwi_ref[D:D + 1, :]
        small_ref[3:4, :F] = lane_total(gacc[...]) * 0.5
        small_ref[3:4, F:] = lane_total(bacc[...]) * 0.5
        put_pieces(n, pieces32, gwi_ref, D, F, 0)
        pieces_ref[...] = pieces32[...].astype(BF)


def back(n, Q, flags, eT, below, above, heads, n1, s1, rstd1, r1, wc, gain, small, rows):
    G, F, N = eT.shape
    DE = r1.shape[1]
    sd = jax.ShapeDtypeStruct
    return pl.pallas_call(
        functools.partial(back_kernel, n, Q, G // 2), grid=(G,),
        in_specs=[smem(), seq_spec(1, F, N), fixed(below.shape), fixed(above.shape), fixed(heads.shape), seq_spec(1, F, N), seq_spec(1, F, N),
                  seq_spec(1, 1, N), seq_spec(1, DE, N), fixed(wc.shape), fixed(gain.shape), fixed(small.shape)],
        out_specs=[seq_spec(Q, F, N // Q), fixed((n, WIDE // L, rows, L)), fixed(small.shape)],
        out_shape=[sd((G * Q, F, N // Q), BF), sd((n, WIDE // L, rows, L), BF), sd(small.shape, F32)],
        scratch_shapes=[pltpu.VMEM((3 * F, N), BF), pltpu.VMEM((F, N), F32), pltpu.VMEM((F, L), F32), pltpu.VMEM((F, L), F32),
                        pltpu.VMEM((DE, F), F32), pltpu.VMEM((F, Q * 2 * SHIFT), BF), pltpu.VMEM((F, L), F32),
                        pltpu.VMEM((1, F, N), BF), pltpu.VMEM((n, WIDE // L, rows, L), F32)],
        compiler_params=params(52), name="back", cost_estimate=cost(8e9, 25e6),
    )(flags, eT, below, above, heads, n1, s1, rstd1, r1, wc, gain, small)


def wide_bwd_kernel(Q, e_ref, w1_ref, n_ref, s_ref, rstd_ref, c_ref, gain_ref, small_in, *refs):
    dx_ref, small_ref, gtab, gacc, bacc = refs[-5 - Q:-Q]
    d_refs = refs[-Q:]
    D, N = d_refs[0].shape
    i = pl.program_id(0)

    @pl.when(i == 0)
    def _():
        fill_table(gtab, gain_ref[...].reshape(1, D) * 0.5)
        gacc[...] = jnp.zeros_like(gacc)
        bacc[...] = jnp.zeros_like(bacc)

    def dot(q):
        d_refs[q][...] = nn(w1_ref[...], e_ref[q])

    def pull_wide(q):
        d_ref = d_refs[q]

        def first(j, carry):
            m1, m2 = carry
            rows = rows_at(j)
            ds = d_ref[rows, :] * s_ref[q, rows, :].astype(F32)
            dn = ds * n_ref[q, rows, :].astype(F32)
            gain = spread(gtab, rows, N)
            t = ds * gain
            d_ref[rows, :] = t
            lane_sum(bacc, rows, ds)
            lane_sum(gacc, rows, dn)
            return m1 + fold(t), m2 + fold(dn * gain)

        zero = jnp.zeros((8, N), F32)
        m1, m2 = loop(D // R, first, (zero, zero), 50)
        rstd = rstd_ref[q]
        m1, m2 = total8(m1) * (1.0 / D) * rstd, total8(m2) * (1.0 / D) * rstd

        def second(j, _):
            rows = rows_at(j)
            g = (d_ref[rows, :] * rstd - m1) - n_ref[q, rows, :].astype(F32) * m2
            dx_ref[q, rows, :] = (g + c_ref[q, rows, :].astype(F32)).astype(BF)
            return 0

        loop(D // R, second, 0, 50)

    dot(0)
    for q in range(Q):
        if q + 1 < Q:
            dot(q + 1)
        pull_wide(q)

    @pl.when(i == pl.num_programs(0) - 1)
    def _():
        small_ref[...] = small_in[...]
        small_ref[4:5, :] = small_in[4:5, :] + lane_total(gacc[...]) * 0.5
        small_ref[5:6, :] = small_in[5:6, :] + lane_total(bacc[...]) * 0.5


def wide_bwd(Q, e1, w1, n0, s0, rstd0, cT, gain, small, start=0, steps=None, into=None):
    S, D, N = cT.shape
    F = e1.shape[1]
    steps = S // Q if steps is None else steps
    sd = jax.ShapeDtypeStruct
    at = lambda i: (start + i, 0, 0)
    into = () if into is None else (into,)
    part = lambda rows: pl.BlockSpec((Q, rows, N), at)
    return pl.pallas_call(
        functools.partial(wide_bwd_kernel, Q), grid=(steps,),
        in_specs=[part(F), fixed(w1.shape), part(D), part(D), part(1), part(D),
                  fixed(gain.shape), fixed(small.shape)] + [pl.BlockSpec(memory_space=pl.ANY)] * len(into),
        out_specs=[part(D), fixed(small.shape)],
        out_shape=[sd((S, D, N), BF), sd(small.shape, F32)],
        scratch_shapes=[pltpu.VMEM((D, L), F32)] * 3 + [pltpu.VMEM((D, N), F32)] * Q,
        input_output_aliases={8: 0} if into else {},
        compiler_params=params(52), name="wide_bwd", cost_estimate=cost(2e9 * steps, 8.4e6 * steps),
    )(e1, w1, n0, s0, rstd0, cT, gain, small, *into)


def swap(v, bit, n):
    return lax.ppermute(v, "ctx", [(i, i ^ bit) for i in range(n)])


def bits_of(n):
    out, b = [], 1
    while b < n:
        out.append(b)
        b *= 2
    return out


def together(*values):
    return lax.optimization_barrier(values)


def slot_table(n, me):
    diff = jnp.arange(n, dtype=jnp.int32) ^ me
    slots = sum((jnp.where((diff & bit) != 0, n // 2 // bit, 0) for bit in bits_of(n)[1:]), jnp.zeros_like(diff))
    return jnp.concatenate([slots, (me & 1)[None].astype(jnp.int32)])


def split_for(full, bit, me):
    pairs = full.reshape((-1, 2) + full.shape[1:])
    mine = jnp.where((me & bit) == 0, 0, 1)
    keep = lax.dynamic_index_in_dim(pairs, mine, 1, keepdims=False)
    return keep, lax.dynamic_index_in_dim(pairs, 1 - mine, 1, keepdims=False).astype(BF)


def sum_all(v, n):
    for bit in bits_of(n):
        v = v + swap(v, bit, n)
    return v


def to_units(flat, n, M, C, rows=None):
    q, parts, units = unit_plan(n, M, C)
    return jnp.pad(flat.reshape(units, q), ((0, 0), (0, WIDE - q))).reshape(units, WIDE // L, L).transpose(1, 0, 2)


def round_up(v, m=8):
    return -(-v // m) * m


def on_device(block_input, cotangent, w_in, w_conv, w_out, wide_gain, wide_bias, narrow_gain, narrow_bias, dealing):
    slots, seqs, T, D = block_input.shape
    F = narrow_gain.shape[1]
    n = lax.axis_size("ctx")
    half = dealing.shape[0] // 2
    me = lax.axis_index("ctx")
    pair = jnp.sum(jnp.where(dealing[:half] == me, jnp.arange(half, dtype=jnp.int32), 0))
    flags = jnp.stack([pair == 0, pair == half - 1]).astype(jnp.int32)
    up = [(i, (i + 1) % n) for i in range(n)]
    down = [((i + 1) % n, i) for i in range(n)]
    table = slot_table(n, me)
    units_in, units_conv, units_out = (unit_plan(n, m, c)[2] for m, c in ((D, F), (3 * F, F), (F, D)))
    rows_in, rows_rest = round_up(units_in), round_up(units_conv + units_out)

    xT = block_input.transpose(0, 1, 3, 2).reshape(slots * seqs, D, T)
    cT = cotangent.transpose(0, 1, 3, 2).reshape(slots * seqs, D, T)

    piece_in = jnp.pad(to_units(w_in, n, D, F), ((0, 0), (0, rows_in - units_in), (0, 0)))
    piece_rest = jnp.concatenate([to_units(w_conv, n, 3 * F, F), to_units(w_out, n, F, D)], axis=1)
    piece_rest = jnp.pad(piece_rest, ((0, 0), (0, rows_rest - piece_rest.shape[1]), (0, 0)))
    gain0 = wide_gain
    bits = bits_of(n)
    Q = 2
    steps = slots * seqs // Q

    buf_in, buf_rest = piece_in[None], piece_rest[None]
    acts, gain, done, token = (), gain0, 0, None
    far = list(reversed(bits))
    for s, bit in enumerate(far):
        got_in = swap(buf_in, bit, n)
        if s < len(far) - 2:
            got_rest = swap(buf_rest, bit, n)
        count = (steps * (s + 1)) // (len(far) - 1) * Q - done if s < len(far) - 1 else 0
        if count:
            *acts, token = wide_fwd(xT, gain, wide_bias, Q, done, count, acts, token)
            done += count
        if s < len(far) - 1:
            buf_in = jnp.concatenate([buf_in, got_in], axis=0)
        if s < len(far) - 2:
            buf_rest = jnp.concatenate([buf_rest, got_rest], axis=0)
        buf_in, buf_rest, token, gain = together(buf_in, buf_rest, token, gain)
    r1, n0, s0, rstd0 = acts
    got_rest = swap(buf_rest, far[-2], n)
    w1, w1t = unpack_in(n, table, buf_in, got_in, narrow_bias, token, D, F)
    uT, n1, s1, rstd1, tails = front(r1, w1t, narrow_gain, narrow_bias, Q)
    buf_rest, tails = together(jnp.concatenate([buf_rest, got_rest], axis=0), tails)
    below = lax.ppermute(tails[0], "ctx", up)
    above = lax.ppermute(tails[1], "ctx", down)
    got_rest = swap(buf_rest, far[-1], n)
    wc, wct, w3, w3t = unpack_rest(n, table, buf_rest, got_rest, narrow_bias, wide_bias, D, F)
    eT, outT, rest, small, heads = middle(n, Q, flags, uT, below, above, tails, cT, xT, wct, w3, w3t,
                                          narrow_gain, narrow_bias, rows_rest)

    keep, send = split_for(rest, bits[0], me)
    got = swap(send, bits[0], n)
    above = lax.ppermute(heads[0], "ctx", down)
    below = lax.ppermute(heads[1], "ctx", up)
    rest = keep + got.astype(F32)
    keep, send = split_for(rest, bits[1], me)
    send, gain1 = together(send, narrow_gain)
    got = swap(send, bits[1], n)
    e1, into, small = back(n, Q, flags, eT, below, above, heads, n1, s1, rstd1, r1, wc, gain1, small, rows_in)
    rest, small = together(keep + got.astype(F32), small)

    dxT, gain, halves = None, gain0, 2
    for s in range(halves):
        keep_i, send_i = split_for(into, bits[s], me)
        keep_r, send_r = split_for(rest, bits[s + 2], me)
        send_r, send_i, gain = together(send_r, send_i, gain)
        got_r, got_i = swap(send_r, bits[s + 2], n), swap(send_i, bits[s], n)
        dxT, small = wide_bwd(Q, e1, w1, n0, s0, rstd0, cT, gain, small, s * steps // halves, steps // halves, dxT)
        rest, into, small = together(keep_r + got_r.astype(F32), keep_i + got_i.astype(F32), small)
    def owned(own, at, M, C):
        q, parts, units = unit_plan(n, M, C)
        return own[:, at:at + units].transpose(1, 0, 2).reshape(units, WIDE)[:, :q].reshape(-1)


    rest_bits, in_bits = bits[2 + halves:], bits[halves:]
    flat = {}
    order = in_bits + bits[:halves][::-1]
    for j in range(len(bits)):
        if j == len(in_bits) + 1:
            small, flat["in"], flat["conv"] = together(small, owned(into[0], 0, D, F), owned(rest[0], 0, 3 * F, F))
        got = swap(small, order[j], n)
        if order[j] in rest_bits:
            keep_r, send_r = split_for(rest, order[j], me)
            rest = keep_r + swap(send_r, order[j], n).astype(F32)
        if j < len(in_bits):
            keep_i, send_i = split_for(into, in_bits[j], me)
            into = keep_i + swap(send_i, in_bits[j], n).astype(F32)
        small = small + got
        if j < len(in_bits):
            small, rest, into = together(small, rest, into)

    back4 = lambda v: v.reshape(slots, seqs, D, T).transpose(0, 1, 3, 2)
    return (back4(outT), back4(dxT), flat["in"], flat["conv"], owned(rest[0], units_conv, F, D),
            small[4], jnp.stack([small[5], small[2]]), jnp.stack([small[3, :F], small[0, :F]]),
            jnp.stack([small[1, F:], small[3, F:], small[1, :F], small[0, F:]]))


def solution(mesh):
    whole, flat, copied = P("ctx", None, None, None), P("ctx"), P()
    return jax.shard_map(
        on_device, mesh=mesh,
        in_specs=(whole, whole, flat, flat, flat, copied, copied, copied, copied, copied),
        out_specs=(whole, whole, flat, flat, flat, copied, copied, copied, copied),
        check_vma=False,
    )
```
